256 devices in a mesh: req: 64 (over z, x, core), ffn: 4 (over y).
Axes of the slice: x: 4, y: 4, z: 8, core: 2. Of those that a mesh axis runs over, the one named last changes fastest.
Arguments:
- residual: bfloat16 [16384, 2048], P('req')
- queries: bfloat16 [16384, 4096], P('req', 'ffn')
- rotated_key_rows: bfloat16 [16384, 2048], P('req', 'ffn')
- values: bfloat16 [16384, 2048], P('req', 'ffn'), may hold values from -6 to 6
- req_start: int32 [16384], P('req'), may hold values from 0 to 16383, as said below
- head_sink_logit: float32 [32], P('ffn'), may hold values from 6 to 11
- out_proj: bfloat16 [4096, 2048], P('ffn', 'req'), may hold values from -0.25 to 0.25
- mid_gain: float32 [2048], replicated, may hold values from 0.1 to 1.9
- router_logits: float32 [16384, 8], P('req')
- routes: int32 [16384, 2], P('req'), may hold values from 0 to 63, as said below
- placement: int32 [64], replicated, may hold values from 0 to 7, as said below
- w_gate: bfloat16 [64, 2048, 3072], P('req', None, 'ffn'), as said below
- w_up: bfloat16 [64, 2048, 3072], P('req', None, 'ffn'), as said below
- w_down: bfloat16 [64, 2048, 3072], P('req', None, 'ffn'), as said below
Outputs:
- layer_out: bfloat16 [16384, 2048], P('req', 'ffn')
The draws below stay inside these ranges and needn't reach their ends.
Inputs may be any that keep to these rules, and one draw needn't show every extreme that they name: req_start[p] is the first position of the request that holds position p; requests are runs of consecutive positions, each at most 8192 long, one is exactly 8192 long, and the last position is a request of one token. `routes`: the two entries of a token name indices that host different experts. Among the 512 entries of the tokens of one index of req, an index appears at most 10 times, and every index that hosts one certain expert appears exactly 10 times, in every such block. `placement`: every expert is hosted at one index or more. `w_gate`: rows k and m are equal where placement[k] == placement[m]. `w_up`: rows k and m are equal where placement[k] == placement[m]. `w_down`: rows k and m are equal where placement[k] == placement[m].
All inputs are finite; a program needn't handle non-finite values.
Results may differ from the reference program's by a relative error of at most 0.0075.
Values may be sent and summed in bfloat16 or wider, within the bound.
A program may use at most 128 MiB of HBM per device.

```python
import math
import jax
import jax.numpy as jnp
from jax import lax

D = 2048
QUERY_HEADS = 32
KEY_VALUE_HEADS = 16
HEAD_SIZE = 128
EXPERTS = 8
FF = 3072
TOKENS_PER_SHARD = 256
TOTAL_TOKENS = 16384
WINDOW_TOKENS = 4096
MAXLEN = 8192
CAP = 10
N_REQ = 64
N_FFN = 4


def folded_random_key(key, number):
    return jax.random.fold_in(key, number)


def base_keys(key):
    return jnp.clip(jax.random.normal(folded_random_key(key, 22), (TOTAL_TOKENS, KEY_VALUE_HEADS * HEAD_SIZE), jnp.float32), -5.0, 5.0) * 1.6


def draw_residual(key, part):
    log_low = math.log(0.3)
    log_high = math.log(3.0)
    col_scale = jnp.exp(jax.random.uniform(folded_random_key(key, 41), (1, D), jnp.float32, log_low, log_high))
    row_scale = jnp.exp(jax.random.uniform(folded_random_key(key, 42), (TOTAL_TOKENS, 1), jnp.float32, log_low, log_high))
    base_draw = jnp.clip(jax.random.normal(folded_random_key(key, 43), (TOTAL_TOKENS, D), jnp.float32), -4.0, 4.0)
    return (base_draw * row_scale * col_scale).astype(jnp.bfloat16)


def draw_rotated_key_rows(key, part):
    starting_keys = base_keys(key)
    return starting_keys.astype(jnp.bfloat16)


def draw_queries(key, part):
    query_draw = jnp.clip(jax.random.normal(folded_random_key(key, 23), (TOTAL_TOKENS, QUERY_HEADS * HEAD_SIZE), jnp.float32), -5.0, 5.0) * 1.6
    return query_draw.astype(jnp.bfloat16)


def draw_router_logits(key, part):
    logits = jnp.clip(jax.random.normal(folded_random_key(key, 31), (TOTAL_TOKENS, EXPERTS), jnp.float32), -6.0, 6.0) * 2.0
    return logits


def host_table(key):
    profile = jnp.array([4, 3, 2, 2, 2, 1, 1, 1], jnp.int32)
    extra_slots = N_REQ - EXPERTS
    extra_quota = extra_slots * profile // 16
    leftover = extra_slots - jnp.sum(extra_quota)
    host_counts = 1 + extra_quota + (jnp.arange(EXPERTS) < leftover).astype(jnp.int32)
    hot_order = jax.random.permutation(folded_random_key(key, 51), EXPERTS)
    by_expert = jnp.zeros((EXPERTS,), jnp.int32).at[hot_order].set(host_counts)
    host_ends = jnp.cumsum(by_expert)
    slot_ids = jnp.arange(N_REQ)
    unsorted = jnp.sum((slot_ids[:, None] >= host_ends[None, :]).astype(jnp.int32), axis=1)
    shuffle = jax.random.permutation(folded_random_key(key, 52), N_REQ)
    return unsorted[shuffle].astype(jnp.int32)


def draw_placement(key, part):
    return host_table(key)


def placed_weights(key, number, fan_in):
    base_draw = jnp.clip(jax.random.normal(folded_random_key(key, number), (EXPERTS, D, FF), jnp.float32), -6.0, 6.0) * fan_in ** (-0.5)
    return jnp.take(base_draw, host_table(key), axis=0).astype(jnp.bfloat16)


def draw_w_gate(key, part):
    return placed_weights(key, 71, D)


def draw_w_up(key, part):
    return placed_weights(key, 72, D)


def draw_w_down(key, part):
    return placed_weights(key, 73, FF)


def draw_routes(key, part):
    hosts = host_table(key)
    tickets = N_REQ * CAP
    ticket_ids = jnp.arange(tickets, dtype=jnp.int32)
    ticket_dest = ticket_ids // CAP
    ticket_expert = hosts[ticket_dest]
    heavy_expert = jax.random.randint(folded_random_key(key, 53), (), 0, EXPERTS)

    def one_block(block_key):
        noise_draw = jax.random.randint(block_key, (tickets,), 0, 1 << 16)
        ticket_score = noise_draw * tickets + ticket_ids
        ticket_score = jnp.where(ticket_expert == heavy_expert, ticket_score - (1 << 16) * tickets, ticket_score)
        picked = jnp.argsort(ticket_score)[:2 * TOKENS_PER_SHARD]
        picked_expert = ticket_expert[picked]
        ranking = jnp.argsort(picked_expert * tickets + picked)
        ranked = ticket_dest[picked[ranking]]
        first = ranked[:TOKENS_PER_SHARD]
        second = ranked[TOKENS_PER_SHARD:]
        flip_pair = jax.random.randint(folded_random_key(block_key, 1), (TOKENS_PER_SHARD,), 0, 2) == 1
        paired = jnp.stack([jnp.where(flip_pair, second, first), jnp.where(flip_pair, first, second)], axis=1)
        shuffle = jax.random.permutation(folded_random_key(block_key, 2), TOKENS_PER_SHARD)
        return paired[shuffle]
    keys_in_block = jax.vmap(lambda index_value: jax.random.fold_in(folded_random_key(key, 54), index_value))(jnp.arange(N_REQ))
    return jax.vmap(one_block)(keys_in_block).reshape(TOTAL_TOKENS, 2).astype(jnp.int32)


def draw_req_start(key, part):
    positions = jnp.arange(TOTAL_TOKENS, dtype=jnp.int32)
    offset = jax.random.randint(folded_random_key(key, 61), (), 0, MAXLEN)
    full_count = (TOTAL_TOKENS - 1 - offset) // MAXLEN
    chosen = jax.random.randint(folded_random_key(key, 62), (), 0, full_count)
    low_edge = offset + chosen * MAXLEN
    extra_cuts = jax.random.randint(folded_random_key(key, 63), (TOTAL_TOKENS,), 0, 512) == 0
    guarded = (positions > low_edge) & (positions < low_edge + MAXLEN)
    is_start = (positions == 0) | (positions == TOTAL_TOKENS - 1) | ((positions - offset) % MAXLEN == 0) | extra_cuts & jnp.logical_not(guarded)
    marked = jnp.where(is_start, positions, 0)
    return lax.cummax(marked, axis=0).astype(jnp.int32)


def shard_levels(key, extent, split, least, high):
    level = 1.0
    for dim, blocks in split:
        heights = jax.random.uniform(jax.random.fold_in(jax.random.fold_in(key, 6), dim), (blocks,), jnp.float32, least / len(split), high / len(split))
        level = level * jnp.repeat(jnp.exp(heights), extent[dim] // blocks).reshape((-1,) + (1,) * (len(extent) - 1 - dim))
    return level


def centred(own_key, shape, width, most, pieces=(), kind=jnp.bfloat16):
    entries = width * jax.random.normal(own_key, shape, jnp.float32)
    if pieces:
        entries = entries * shard_levels(own_key, shape, pieces, -0.22, 0.18)
    return jnp.clip(entries, -most, most).astype(kind)


def setup_inputs(seed: int = 0) -> dict:
    key_of = jax.random.split(jax.random.key(seed), 15)
    return {
        "residual": draw_residual(jax.random.fold_in(key_of[14], 71), 0),
        "queries": draw_queries(jax.random.fold_in(key_of[14], 71), 0),
        "rotated_key_rows": draw_rotated_key_rows(jax.random.fold_in(key_of[14], 71), 0),
        "values": centred(key_of[3], (TOTAL_TOKENS, KEY_VALUE_HEADS * HEAD_SIZE), 1.0, 6.0, ((0, 64), (1, 4))),
        "req_start": draw_req_start(jax.random.fold_in(key_of[14], 71), 0),
        "head_sink_logit": jnp.clip(6.0 + 5.0 * jax.random.uniform(key_of[5], (QUERY_HEADS,), jnp.float32) ** shard_levels(key_of[5], (QUERY_HEADS,), ((0, 4),), -0.2, 0.2), 6.0, 11.0),
        "out_proj": centred(key_of[6], (QUERY_HEADS * HEAD_SIZE, D), (QUERY_HEADS * HEAD_SIZE // 8) ** -0.5, 0.25, ((0, 4), (1, 64))),
        "mid_gain": jnp.clip(1.0 + 0.18 * jax.random.normal(key_of[7], (D,), jnp.float32), 0.1, 1.9),
        "router_logits": draw_router_logits(jax.random.fold_in(key_of[14], 71), 0),
        "routes": draw_routes(jax.random.fold_in(key_of[14], 71), 0),
        "placement": draw_placement(jax.random.fold_in(key_of[14], 71), 0),
        "w_gate": draw_w_gate(jax.random.fold_in(key_of[14], 71), 0),
        "w_up": draw_w_up(jax.random.fold_in(key_of[14], 71), 0),
        "w_down": draw_w_down(jax.random.fold_in(key_of[14], 71), 0),
    }


EPS = 1e-06
block_rows = 128

def attention(queries, rotated_key_rows, values, req_start, head_sink_logit):
    query_group_width = QUERY_HEADS // KEY_VALUE_HEADS
    logit_scale_factor = HEAD_SIZE ** (-0.5)
    leading_zero_rows = jnp.zeros((WINDOW_TOKENS, KEY_VALUE_HEADS * HEAD_SIZE), rotated_key_rows.dtype)
    gathered_keys = jnp.concatenate([leading_zero_rows, rotated_key_rows], axis=0)
    gathered_values = jnp.concatenate([leading_zero_rows, values], axis=0)
    key_range_length = WINDOW_TOKENS + TOKENS_PER_SHARD
    initial_sink_logit = head_sink_logit.reshape(KEY_VALUE_HEADS, query_group_width, 1)

    def one_block(block_index):
        leading_row = block_index * TOKENS_PER_SHARD
        queries_in_block = lax.dynamic_slice_in_dim(queries, leading_row, TOKENS_PER_SHARD, 0).astype(jnp.float32).reshape(TOKENS_PER_SHARD, KEY_VALUE_HEADS, query_group_width, HEAD_SIZE)
        keys_in_block = lax.dynamic_slice_in_dim(gathered_keys, leading_row, key_range_length, 0).astype(jnp.float32).reshape(key_range_length, KEY_VALUE_HEADS, HEAD_SIZE)
        values_in_block = lax.dynamic_slice_in_dim(gathered_values, leading_row, key_range_length, 0).astype(jnp.float32).reshape(key_range_length, KEY_VALUE_HEADS, HEAD_SIZE)
        starts = lax.dynamic_slice_in_dim(req_start, leading_row, TOKENS_PER_SHARD, 0)
        query_pos = leading_row + jnp.arange(TOKENS_PER_SHARD, dtype=jnp.int32)
        key_pos = leading_row - WINDOW_TOKENS + jnp.arange(key_range_length, dtype=jnp.int32)
        visible = (key_pos[None, :] >= starts[:, None]) & (key_pos[None, :] <= query_pos[:, None]) & (query_pos[:, None] - key_pos[None, :] < WINDOW_TOKENS)
        attention_logits = jnp.einsum('veck,uek->ecvu', queries_in_block, keys_in_block) * logit_scale_factor
        attention_logits = jnp.where(visible[None, None], attention_logits, -jnp.inf)
        row_peak = jnp.maximum(lax.optimization_barrier(jnp.max(attention_logits, axis=-1)), initial_sink_logit)
        probs = jnp.exp(attention_logits - row_peak[..., None])
        row_total = lax.optimization_barrier(jnp.sum(probs, axis=-1)) + jnp.exp(initial_sink_logit - row_peak)
        reduced_probabilities = lax.optimization_barrier(probs.astype(jnp.bfloat16)).astype(jnp.float32)
        weighted_value_sum = jnp.einsum('plyw,wpj->plyj', reduced_probabilities, values_in_block)
        result = weighted_value_sum / row_total[..., None]
        return jnp.transpose(result, (2, 0, 1, 3)).reshape(TOKENS_PER_SHARD, QUERY_HEADS * HEAD_SIZE).astype(jnp.bfloat16)
    blocks = lax.map(one_block, jnp.arange(TOTAL_TOKENS // TOKENS_PER_SHARD, dtype=jnp.int32))
    return blocks.reshape(TOTAL_TOKENS, QUERY_HEADS * HEAD_SIZE)

def expert_outputs(normed, hosts_flat, w_gate, w_up, w_down):
    row_count = hosts_flat.shape[0]
    group_count = N_REQ
    by_host = jnp.argsort(hosts_flat, stable=True).astype(jnp.int32)
    host_hot = (hosts_flat[:, None] == jnp.arange(group_count, dtype=jnp.int32)[None, :]).astype(jnp.int32)
    counts = lax.optimization_barrier(jnp.sum(host_hot, axis=0))
    padded = (counts + block_rows - 1) // block_rows * block_rows
    pad_start = jnp.cumsum(padded) - padded
    plain_start = jnp.cumsum(counts) - counts
    sorted_ids = hosts_flat[by_host]
    slot_of = pad_start[sorted_ids] + jnp.arange(row_count, dtype=jnp.int32) - plain_start[sorted_ids]
    capacity = (row_count + block_rows - 1) // block_rows * block_rows + group_count * block_rows
    buffer = jnp.zeros((capacity, D), normed.dtype).at[slot_of].set(normed[by_host // 2])
    block_count = capacity // block_rows
    block_first = jnp.arange(block_count, dtype=jnp.int32) * block_rows
    block_host = jnp.minimum(lax.optimization_barrier(jnp.sum((block_first[:, None] >= (pad_start + padded)[None, :]).astype(jnp.int32), axis=1)), group_count - 1)
    quarter = FF // N_FFN

    def one_block(operands):
        block_in, host = operands
        inputs = block_in.astype(jnp.float32)
        gate_val = jnp.dot(inputs, w_gate[host].astype(jnp.float32), preferred_element_type=jnp.float32)
        up_val = jnp.dot(inputs, w_up[host].astype(jnp.float32), preferred_element_type=jnp.float32)
        activated = (jax.nn.silu(gate_val) * up_val).astype(jnp.bfloat16).astype(jnp.float32)
        down_mat = w_down[host].astype(jnp.float32)
        summed = jnp.zeros((block_rows, D), jnp.float32)
        for piece_idx in range(N_FFN):
            low_cols = piece_idx * quarter
            piece = jnp.dot(activated[:, low_cols:low_cols + quarter], down_mat[:, low_cols:low_cols + quarter].T, preferred_element_type=jnp.float32)
            piece = lax.optimization_barrier(piece.astype(jnp.bfloat16))
            summed = summed + piece.astype(jnp.float32)
        return summed
    results = lax.map(one_block, (buffer.reshape(block_count, block_rows, D), block_host))
    gathered = results.reshape(capacity, D)[slot_of]
    return jnp.zeros((row_count, D), jnp.float32).at[by_host].set(gathered)

def reference(residual, queries, rotated_key_rows, values, req_start, head_sink_logit, out_proj, mid_gain, router_logits, routes, placement, w_gate, w_up, w_down):
    attended = attention(queries, rotated_key_rows, values, req_start, head_sink_logit)
    proj = jnp.dot(attended.astype(jnp.float32), out_proj.astype(jnp.float32), preferred_element_type=jnp.float32)
    hidden = residual.astype(jnp.float32) + proj
    mean_sq = lax.optimization_barrier(jnp.mean(hidden * hidden, axis=1, keepdims=True))
    normed = (hidden * lax.rsqrt(mean_sq + EPS) * mid_gain).astype(jnp.bfloat16)
    expert_of = placement[routes]
    expert_hot = (expert_of[:, :, None] == jnp.arange(EXPERTS, dtype=jnp.int32)[None, None, :]).astype(jnp.float32)
    chosen = lax.optimization_barrier(jnp.sum(router_logits[:, None, :] * expert_hot, axis=2))
    logit_peak = lax.optimization_barrier(jnp.max(chosen, axis=1, keepdims=True))
    exp_logits = jnp.exp(chosen - logit_peak)
    gate_weights = exp_logits / lax.optimization_barrier(jnp.sum(exp_logits, axis=1, keepdims=True))
    outputs = expert_outputs(normed, routes.reshape(-1).astype(jnp.int32), w_gate, w_up, w_down).reshape(TOTAL_TOKENS, 2, D)
    mixture = lax.optimization_barrier(jnp.sum(outputs * gate_weights[:, :, None], axis=1))
    return (hidden + mixture).astype(jnp.bfloat16)
```

```python
import jax
import jax.numpy as jnp
from jax import lax
from jax.experimental import pallas as pl
from jax.experimental.pallas import tpu as pltpu
from jax.sharding import PartitionSpec as P

QUERY_HEADS = 32
KEY_VALUE_HEADS = 16
HEAD_SIZE = 128
EXPERTS = 8
EPS = 1e-06
MESH = pl.DeviceIdType.MESH
BF = jnp.bfloat16
F32 = jnp.float32

NREQ = 64
NFFN = 4
NZ = 8
TOK = 256
D = 2048
Q = D // NFFN
HID = 768
WIDE = Q + 128
Z_ORDER = (0, 1, 7, 2, 6, 3, 5, 4)


def dot(a, b):
    return jnp.dot(a, b, preferred_element_type=F32)


def dot_nt(a, b):
    return lax.dot_general(a, b, (((1,), (1,)), ((), ())), preferred_element_type=F32)


def iota(shape, dim):
    return lax.broadcasted_iota(jnp.int32, shape, dim)


def remote(src, dst, send_sem, recv_sem, req, ffn):
    return pltpu.make_async_remote_copy(
        src_ref=src, dst_ref=dst, send_sem=send_sem, recv_sem=recv_sem,
        device_id=(req, ffn), device_id_type=MESH,
    )


def layer_kernel(
    att_ref, wo_hbm, res_hbm, gain_hbm, logits_ref, routes_ref, placement_ref, wg_hbm, wu_hbm, wd_hbm,
    out_ref,
    wo, res, gain, wg, wu, wd,
    proj_send, proj_recv, hid, stat_send, stat_recv,
    e_main, e_rem, g_main, g_rem,
    disp, rows, xbuf, act, part, hop_l, hop_r, from_l, from_r, fin, ret,
    in_sem, proj_ssem, proj_rsem, stat_ssem, stat_rsem,
    a2a_ssem, a2a_rsem, ag_ssem, ag_rsem, rs_ssem, rs_rsem, ret_ssem, ret_rsem, own_sem,
):
    r = lax.axis_index("req")
    y = lax.axis_index("ffn")
    z = r // 8
    yp, ym, y2 = lax.rem(y + 1, 4), lax.rem(y + 3, 4), lax.rem(y + 2, 4)
    peers = (yp, y2, ym)

    bar = pltpu.get_barrier_semaphore()

    def greet(o, c):
        pl.semaphore_signal(bar, inc=1, device_id=(lax.rem(r + o, NREQ), y), device_id_type=MESH)
        return c

    lax.fori_loop(1, NREQ, greet, 0)
    for p in peers:
        pl.semaphore_signal(bar, inc=1, device_id=(r, p), device_id_type=MESH)

    y_cols = pl.ds(pl.multiple_of(y * Q, Q), Q)
    loads = [
        pltpu.make_async_copy(wo_hbm, wo, in_sem.at[0]),
        pltpu.make_async_copy(res_hbm.at[:, y_cols], res, in_sem.at[1]),
        pltpu.make_async_copy(gain_hbm.at[:, y_cols], gain, in_sem.at[2]),
        pltpu.make_async_copy(wg_hbm, wg, in_sem.at[3]),
        pltpu.make_async_copy(wu_hbm, wu, in_sem.at[4]),
        pltpu.make_async_copy(wd_hbm, wd, in_sem.at[5]),
    ]
    for load in loads:
        load.start()

    route0, route1 = routes_ref[0:1, :], routes_ref[1:2, :]
    dest = iota((NREQ, TOK), 0)
    hot0 = jnp.where(dest == route0, 1.0, 0.0)
    hot1 = jnp.where(dest == route1, 1.0, 0.0)
    before = jnp.where(iota((TOK, TOK), 0) < iota((TOK, TOK), 1), 1.0, 0.0).astype(BF)
    earlier = dot((hot0 + hot1).astype(BF), before)
    slot0 = route0.astype(F32) * 16.0 + jnp.sum(hot0 * earlier, axis=0, keepdims=True)
    slot1 = route1.astype(F32) * 16.0 + jnp.sum(hot1 * (earlier + hot0), axis=0, keepdims=True)
    line = iota((512, TOK), 0)
    main_id = ((line >> 3) * 16 + (line & 7)).astype(F32)
    rem_id = ((line >> 3) * 16 + 8 + (line & 1)).astype(F32)
    e_main[...] = jnp.where((main_id == slot0) | (main_id == slot1), 1.0, 0.0).astype(BF)
    e_rem[...] = jnp.where((rem_id == slot0) | (rem_id == slot1), 1.0, 0.0).astype(BF)
    hosts = jnp.where(iota((EXPERTS, NREQ), 0) == placement_ref[...], 1.0, 0.0).astype(BF)
    logits = logits_ref[...]
    pick0 = jnp.sum(logits * dot(hosts, hot0.astype(BF)), axis=0, keepdims=True)
    pick1 = jnp.sum(logits * dot(hosts, hot1.astype(BF)), axis=0, keepdims=True)
    top = jnp.maximum(pick0, pick1)
    exp0, exp1 = jnp.exp(pick0 - top), jnp.exp(pick1 - top)
    total = exp0 + exp1
    sub = iota((128, TOK), 0)
    packed = jnp.where(sub == 0, slot0, jnp.where(sub == 1, slot1, jnp.where(sub == 2, exp0 / total, exp1 / total)))
    turned = packed.T
    s0, s1, w0, w1 = turned[:, 0:1], turned[:, 1:2], turned[:, 2:3], turned[:, 3:4]
    col = iota((TOK, 512), 1)
    for ids, ref in (((col >> 3) * 16 + (col & 7), g_main), ((col >> 3) * 16 + 8 + (col & 1), g_rem)):
        ids = ids.astype(F32)
        gate = jnp.where(ids == s0, w0, 0.0) + jnp.where(ids == s1, w1, 0.0)
        high = gate.astype(BF)
        ref[0] = high
        ref[1] = (gate - high.astype(F32)).astype(BF)

    pl.semaphore_wait(bar, NREQ - 1 + 3)

    loads[0].wait()

    def project(which):
        return dot_nt(att_ref[...], wo[pl.ds(pl.multiple_of(which * Q, Q), Q), :])

    proj_copies = []
    for i in (1, 0, 2):
        proj_send[i] = project(peers[i]).astype(BF)
        copy = remote(proj_send.at[i], proj_recv.at[2 - i], proj_ssem.at[i], proj_rsem.at[2 - i], r, peers[i])
        copy.start()
        proj_copies.append(copy)
    loads[1].wait()
    own = res[...].astype(F32) + project(y)
    for i in range(3):
        pltpu.make_async_copy(proj_recv.at[i], proj_recv.at[i], proj_rsem.at[i]).wait()
    hidden = own + proj_recv[0].astype(F32) + proj_recv[1].astype(F32) + proj_recv[2].astype(F32)
    hid[...] = hidden

    square = jnp.sum(hidden * hidden, axis=1, keepdims=True)
    stat_send[...] = jnp.broadcast_to(square, (TOK, 128)).T[0:8, :]
    stat_copies = []
    for i in range(3):
        copy = remote(stat_send, stat_recv.at[2 - i], stat_ssem.at[i], stat_rsem.at[2 - i], r, peers[i])
        copy.start()
        stat_copies.append(copy)
    loads[2].wait()
    for i in range(3):
        pltpu.make_async_copy(stat_recv.at[i], stat_recv.at[i], stat_rsem.at[i]).wait()
    squares = stat_send[...] + stat_recv[0] + stat_recv[1] + stat_recv[2]
    factor = lax.rsqrt(squares[0:1, :] * (1.0 / D) + EPS)
    factor = jnp.broadcast_to(factor, (128, TOK)).T[:, 0:1]
    normed = (hidden * factor * gain[...]).astype(BF)

    disp2 = disp.reshape(512, WIDE)
    disp2[:, 0:Q] = dot(e_main[...], normed).astype(BF)
    spread = dot(e_rem[...], normed)
    piece = (iota((512, 128), 0) & 7) >> 1

    def by_piece(parts):
        return jnp.where(piece == 0, parts[0], jnp.where(piece == 1, parts[1], jnp.where(piece == 2, parts[2], parts[3])))

    disp2[:, Q:WIDE] = by_piece([spread[:, 128 * k:128 * k + 128] for k in range(4)]).astype(BF)

    def exchange(source, target, send_sem, recv_sems):
        for dz in Z_ORDER:
            def push(k, c):
                d = lax.rem(z + dz, NZ) * 8 + lax.rem(r + k, 8)
                remote(source.at[d], target.at[r], send_sem, recv_sems.at[z], d, y).start()
                return c
            lax.fori_loop(1 if dz == 0 else 0, 8, push, 0)
        copy = pltpu.make_async_copy(source.at[r], target.at[r], own_sem)
        copy.start()
        copy.wait()

    def arrived(target, recv_sems, dz):
        g = lax.rem(z + dz, NZ)
        count = 7 if dz == 0 else 8
        view = target.at[pl.ds(g * 8, count)]
        pltpu.make_async_copy(view, view, recv_sems.at[g]).wait()

    mine = rows.at[y]
    exchange(disp, mine, a2a_ssem, a2a_rsem)

    ag_copies = []

    def forward(i):
        g = pl.ds(lax.rem(z + Z_ORDER[i], NZ) * 8, 8)
        here, there, side = (ym, yp, 0) if i % 2 == 0 else (yp, ym, 1)
        view = rows.at[here, g]
        pltpu.make_async_copy(view, view, ag_rsem.at[side, i]).wait()
        copy = remote(view, view, ag_ssem.at[2, i], ag_rsem.at[2, i], r, there)
        copy.start()
        ag_copies.append(copy)

    for i, dz in enumerate(Z_ORDER):
        arrived(mine, a2a_rsem, dz)
        g = pl.ds(lax.rem(z + dz, NZ) * 8, 8)
        view = rows.at[y, g]
        for side, there in ((0, yp), (1, ym)):
            copy = remote(view, view, ag_ssem.at[side, i], ag_rsem.at[side, i], r, there)
            copy.start()
            ag_copies.append(copy)
        if i > 0:
            forward(i - 1)
    forward(7)
    for i in range(8):
        g = pl.ds(lax.rem(z + Z_ORDER[i], NZ) * 8, 8)
        here, side = (yp, 1) if i % 2 == 0 else (ym, 0)
        view = rows.at[here, g]
        pltpu.make_async_copy(view, view, ag_rsem.at[side, i]).wait()
        view = rows.at[y2, g]
        pltpu.make_async_copy(view, view, ag_rsem.at[2, i]).wait()

    rows2 = rows.reshape(4, 512, WIDE)
    row_id = iota((128, 512), 0)
    line_id = iota((128, 512), 1)
    for q in range(4):
        xbuf[0:512, Q * q:Q * q + Q] = rows2[q, :, 0:Q]
    for k in range(4):
        select = jnp.where(line_id == (row_id >> 1) * 8 + 2 * k + (row_id & 1), 1.0, 0.0).astype(BF)
        for q in range(4):
            xbuf[512:640, Q * q + 128 * k:Q * q + 128 * k + 128] = dot(select, rows2[q, :, Q:WIDE]).astype(BF)
    loads[3].wait()
    loads[4].wait()

    def inner(n, c):
        cols = pl.ds(pl.multiple_of(n * 256, 256), 256)
        gate = dot(xbuf[...], wg[:, cols])
        up = dot(xbuf[...], wu[:, cols])
        act[:, cols] = (gate / (1.0 + jnp.exp(-gate)) * up).astype(BF)
        return c

    lax.fori_loop(0, HID // 256, inner, 0)
    loads[5].wait()

    line_of = iota((512, 512), 0)
    row_of = iota((512, 512), 1)
    scatter = jnp.where(
        line_of == ((row_of & 127) >> 1) * 8 + 2 * (row_of >> 7) + (row_of & 1), 1.0, 0.0
    ).astype(BF)
    part2 = part.reshape(4, 512, WIDE)
    for j, which in enumerate((y2, yp, ym, y)):
        piece_out = dot_nt(act[...], wd[pl.ds(pl.multiple_of(which * Q, Q), Q), :])
        part2[j, :, 0:Q] = piece_out[0:512].astype(BF)
        tail = piece_out[512:640].astype(BF)
        stacked = jnp.concatenate([tail[:, 128 * k:128 * k + 128] for k in range(4)], axis=0)
        part2[j, :, Q:WIDE] = dot(scatter, stacked).astype(BF)
        if j == 0:
            rs = [
                remote(part.at[0, pl.ds(0, 32)], hop_l, rs_ssem.at[0], rs_rsem.at[0], r, yp),
                remote(part.at[0, pl.ds(32, 32)], hop_r, rs_ssem.at[1], rs_rsem.at[1], r, ym),
            ]
            rs[0].start()
            rs[1].start()
        if j == 1:
            rs.append(remote(part.at[1, pl.ds(32, 32)], from_l.at[pl.ds(32, 32)], rs_ssem.at[2], rs_rsem.at[2], r, yp))
            rs[2].start()
        if j == 2:
            rs.append(remote(part.at[2, pl.ds(0, 32)], from_r.at[pl.ds(0, 32)], rs_ssem.at[3], rs_rsem.at[3], r, ym))
            rs[3].start()
    hop_l2, hop_r2 = hop_l.reshape(256, WIDE), hop_r.reshape(256, WIDE)
    pltpu.make_async_copy(hop_l, hop_l, rs_rsem.at[0]).wait()
    part2[1, 0:256, :] = (part2[1, 0:256, :].astype(F32) + hop_l2[...].astype(F32)).astype(BF)
    rs.append(remote(part.at[1, pl.ds(0, 32)], from_l.at[pl.ds(0, 32)], rs_ssem.at[4], rs_rsem.at[4], r, yp))
    rs[4].start()
    pltpu.make_async_copy(hop_r, hop_r, rs_rsem.at[1]).wait()
    part2[2, 256:512, :] = (part2[2, 256:512, :].astype(F32) + hop_r2[...].astype(F32)).astype(BF)
    rs.append(remote(part.at[2, pl.ds(32, 32)], from_r.at[pl.ds(32, 32)], rs_ssem.at[5], rs_rsem.at[5], r, ym))
    rs[5].start()
    low, high = pl.ds(0, 32), pl.ds(32, 32)
    for ref, half, k in ((from_l, high, 2), (from_r, low, 3), (from_l, low, 4), (from_r, high, 5)):
        view = ref.at[half]
        pltpu.make_async_copy(view, view, rs_rsem.at[k]).wait()
    fin2 = fin.reshape(512, WIDE)
    from_l2, from_r2 = from_l.reshape(512, WIDE), from_r.reshape(512, WIDE)
    fin2[...] = (part2[3].astype(F32) + from_l2[...].astype(F32) + from_r2[...].astype(F32)).astype(BF)

    exchange(fin, ret, ret_ssem, ret_rsem)
    for dz in Z_ORDER:
        arrived(ret, ret_rsem, dz)
    ret2 = ret.reshape(512, WIDE)
    back = ret2[:, 0:Q]
    lines = ret2[:, Q:WIDE]
    masked = jnp.concatenate([jnp.where(piece == k, lines.astype(F32), 0.0).astype(BF) for k in range(4)], axis=1)
    mixture = dot(g_main[0], back) + dot(g_main[1], back) + dot(g_rem[0], masked) + dot(g_rem[1], masked)
    out_ref[...] = (hid[...] + mixture).astype(BF)

    for copy in proj_copies + stat_copies + ag_copies + rs:
        copy.wait_send()
    for sem, ref in ((a2a_ssem, disp), (ret_ssem, fin)):
        view = ref.at[pl.ds(0, NREQ - 1)]
        pltpu.make_async_copy(view, view, sem).wait()


def layer_call(att, wo, residual, gain, logits, routes, placement, wg, wu, wd):
    vmem = pl.BlockSpec(memory_space=pltpu.VMEM)
    hbm = pl.BlockSpec(memory_space=pl.ANY)
    dma = pltpu.SemaphoreType.DMA
    chunk = (NREQ, 8, WIDE)
    return pl.pallas_call(
        layer_kernel,
        out_shape=jax.ShapeDtypeStruct((TOK, Q), BF),
        in_specs=[vmem, hbm, hbm, hbm, vmem, vmem, vmem, hbm, hbm, hbm],
        out_specs=vmem,
        scratch_shapes=[
            pltpu.VMEM((D, D // 2), BF), pltpu.VMEM((TOK, Q), BF), pltpu.VMEM((1, Q), F32),
            pltpu.VMEM((D, HID), BF), pltpu.VMEM((D, HID), BF), pltpu.VMEM((D, HID), BF),
            pltpu.VMEM((3, TOK, Q), BF), pltpu.VMEM((3, TOK, Q), BF), pltpu.VMEM((TOK, Q), F32),
            pltpu.VMEM((8, TOK), F32), pltpu.VMEM((3, 8, TOK), F32),
            pltpu.VMEM((512, TOK), BF), pltpu.VMEM((512, TOK), BF),
            pltpu.VMEM((2, TOK, 512), BF), pltpu.VMEM((2, TOK, 512), BF),
            pltpu.VMEM(chunk, BF), pltpu.VMEM((4,) + chunk, BF), pltpu.VMEM((640, D), BF), pltpu.VMEM((640, HID), BF),
            pltpu.VMEM((4,) + chunk, BF), pltpu.VMEM((32, 8, WIDE), BF), pltpu.VMEM((32, 8, WIDE), BF),
            pltpu.VMEM(chunk, BF), pltpu.VMEM(chunk, BF), pltpu.VMEM(chunk, BF), pltpu.VMEM(chunk, BF),
            dma((6,)), dma((3,)), dma((3,)), dma((3,)), dma((3,)),
            dma, dma((8,)), dma((3, 8)), dma((3, 8)), dma((6,)), dma((6,)), dma, dma((8,)), dma,
        ],
        compiler_params=pltpu.CompilerParams(
            collective_id=1, has_side_effects=True, vmem_limit_bytes=56 << 20
        ),
        name="layer",
    )(att, wo, residual, gain, logits, routes, placement, wg, wu, wd)


def shifted(value, axis, steps):
    count = lax.axis_size(axis)
    initial, last = (max(0, -steps), min(count, count - steps))
    return lax.ppermute(value, axis, [(source, source + steps) for source in range(initial, last)])


def step_back(keys_in_block, values_in_block):
    return shifted((keys_in_block, values_in_block), "req", 1)


def per_device(
    residual, queries, rotated_key_rows, values, req_start, head_sink_logit, out_proj, mid_gain,
    router_logits, routes, placement, w_gate, w_up, w_down,
):
    tok_count = residual.shape[0]
    req_size = lax.axis_size("req")
    own_req = lax.axis_index("req")
    query_group_width = QUERY_HEADS // KEY_VALUE_HEADS
    kv_heads = rotated_key_rows.shape[1] // HEAD_SIZE
    shard_queries = queries.reshape(tok_count, kv_heads, query_group_width, HEAD_SIZE)
    local_keys = rotated_key_rows.reshape(tok_count, kv_heads, HEAD_SIZE)
    local_values = values.reshape(tok_count, kv_heads, HEAD_SIZE)
    win_span = min(16, req_size // 2)
    window = win_span * tok_count
    query_pos = own_req * tok_count + jnp.arange(tok_count, dtype=jnp.int32)
    logit_scale_factor = HEAD_SIZE ** (-0.5)

    def attend(carry_state, keys_in_block, values_in_block, key_first):
        running_max, row_total, weighted_value_sum = carry_state
        attention_logits = (
            jnp.einsum(
                "veck,uek->ecvu", shard_queries, keys_in_block, preferred_element_type=jnp.float32
            )
            * logit_scale_factor
        )
        key_pos = key_first + jnp.arange(keys_in_block.shape[0], dtype=jnp.int32)
        visible = (
            (key_pos[None, :] >= req_start[:, None])
            & (key_pos[None, :] <= query_pos[:, None])
            & (query_pos[:, None] - key_pos[None, :] < window)
        )
        attention_logits = jnp.where(visible[None, None], attention_logits, -jnp.inf)
        new_max = jnp.maximum(running_max, jnp.max(attention_logits, axis=-1))
        probs = jnp.exp(attention_logits - new_max[..., None])
        factor = jnp.exp(running_max - new_max)
        row_total = row_total * factor + jnp.sum(probs, axis=-1)
        weighted_value_sum = weighted_value_sum * factor[..., None] + jnp.einsum(
            "plyw,wpj->plyj",
            probs.astype(jnp.bfloat16),
            values_in_block,
            preferred_element_type=jnp.float32,
        )
        return (new_max, row_total, weighted_value_sum)

    initial_sink_logit = jnp.broadcast_to(
        head_sink_logit.reshape(kv_heads, query_group_width, 1),
        (kv_heads, query_group_width, tok_count),
    )
    carry_state = (
        initial_sink_logit,
        jnp.ones((kv_heads, query_group_width, tok_count), jnp.float32),
        jnp.zeros((kv_heads, query_group_width, tok_count, HEAD_SIZE), jnp.float32),
    )
    carry_state = attend(carry_state, local_keys, local_values, own_req * tok_count)

    def pair_step(step_idx, loop_carry):
        folded, near_keys, near_values = loop_carry
        mid_keys, mid_values = step_back(near_keys, near_values)
        far_keys, far_values = step_back(mid_keys, mid_values)
        key_first = (own_req - 2 * step_idx - 2) * tok_count
        folded = attend(
            folded,
            jnp.concatenate([far_keys, mid_keys], 0),
            jnp.concatenate([far_values, mid_values], 0),
            key_first,
        )
        return (folded, far_keys, far_values)

    carry_state, unused_keys, unused_values = lax.fori_loop(
        0, win_span // 2, pair_step, (carry_state, local_keys, local_values)
    )
    running_max, row_total, weighted_value_sum = carry_state
    attended = (weighted_value_sum / row_total[..., None]).astype(jnp.bfloat16)
    flat_attended = jnp.transpose(attended, (2, 0, 1, 3)).reshape(tok_count, -1)
    wo = lax.all_gather(out_proj.T, "req", axis=0, tiled=True)
    return layer_call(
        flat_attended, wo, residual, mid_gain.reshape(1, D), router_logits.T, routes.T,
        placement.reshape(1, NREQ), w_gate[0], w_up[0], w_down[0],
    )


def solution(mesh):
    in_specs = (
        P("req", None),
        P("req", "ffn"),
        P("req", "ffn"),
        P("req", "ffn"),
        P("req"),
        P("ffn"),
        P("ffn", "req"),
        P(),
        P("req", None),
        P("req", None),
        P(),
        P("req", None, "ffn"),
        P("req", None, "ffn"),
        P("req", None, "ffn"),
    )
    out_specs = P("req", "ffn")
    return jax.shard_map(
        per_device, mesh=mesh, in_specs=in_specs, out_specs=out_specs, check_vma=False
    )
```

```python
import jax
import jax.numpy as jnp
from jax import lax
from jax.experimental import pallas as pl
from jax.experimental.pallas import tpu as pltpu
from jax.sharding import PartitionSpec as P

QUERY_HEADS = 32
KEY_VALUE_HEADS = 16
HEAD_SIZE = 128
EXPERTS = 8
EPS = 1e-06
MESH = pl.DeviceIdType.MESH
BF = jnp.bfloat16
F32 = jnp.float32

NREQ = 64
NFFN = 4
NZ = 8
TOK = 256
D = 2048
Q = D // NFFN
HID = 768
WIDE = Q + 128
Z_ORDER = (0, 1, 7, 2, 6, 3, 5, 4)


def dot(a, b):
    return jnp.dot(a, b, preferred_element_type=F32)


def dot_nt(a, b):
    return lax.dot_general(a, b, (((1,), (1,)), ((), ())), preferred_element_type=F32)


def iota(shape, dim):
    return lax.broadcasted_iota(jnp.int32, shape, dim)


def remote(src, dst, send_sem, recv_sem, req, ffn):
    return pltpu.make_async_remote_copy(
        src_ref=src, dst_ref=dst, send_sem=send_sem, recv_sem=recv_sem,
        device_id=(req, ffn), device_id_type=MESH,
    )


SCALE2 = HEAD_SIZE ** (-0.5) * 1.4426950408889634
MASKED = -1e30


def layer_kernel(
    q_hbm, k_hbm, v_hbm, start_hbm, sink_ref, wo_hbm, res_hbm, gain_hbm, logits_ref, routes_ref, placement_ref,
    wg_hbm, wu_hbm, wd_hbm,
    out_ref,
    kv, qb, qt, vt, starts, peak, mass, acc, att_out, att_in,
    wo, res, gain, wg, wu, wd,
    proj_send, proj_recv, hid, stat_send, stat_recv,
    e_main, e_rem, g_main, g_rem,
    disp, rows, xbuf, act, part, hop_l, hop_r, from_l, from_r, fin, ret,
    kv_ssem, kv_rsem, half_ssem, half_rsem, loc_sem, wo_ssem, wo_rsem, ring_ssem, ring_rsem, pair_ssem, pair_rsem,
    att_ssem, att_rsem,
    in_sem, proj_ssem, proj_rsem, stat_ssem, stat_rsem,
    a2a_ssem, a2a_rsem, ag_ssem, ag_rsem, rs_ssem, rs_rsem, ret_ssem, ret_rsem, own_sem,
):
    r = lax.axis_index("req")
    y = lax.axis_index("ffn")
    z = r // 8
    x = lax.rem(r // 2, 4)
    c = lax.rem(r, 2)
    chip = r // 2
    mate = r + 1 - 2 * c
    yp, ym, y2 = lax.rem(y + 1, 4), lax.rem(y + 3, 4), lax.rem(y + 2, 4)
    peers = (yp, y2, ym)

    bar = pltpu.get_barrier_semaphore()

    def greet(o, c):
        pl.semaphore_signal(bar, inc=1, device_id=(lax.rem(r + o, NREQ), y), device_id_type=MESH)
        return c

    lax.fori_loop(1, NREQ, greet, 0)
    for p in peers:
        pl.semaphore_signal(bar, inc=1, device_id=(r, p), device_id_type=MESH)

    y_cols = pl.ds(pl.multiple_of(y * Q, Q), Q)
    loads = [
        pltpu.make_async_copy(res_hbm.at[:, y_cols], res, in_sem.at[0]),
        pltpu.make_async_copy(gain_hbm.at[:, y_cols], gain, in_sem.at[1]),
        pltpu.make_async_copy(wg_hbm, wg, in_sem.at[2]),
        pltpu.make_async_copy(wu_hbm, wu, in_sem.at[3]),
        pltpu.make_async_copy(wd_hbm, wd, in_sem.at[4]),
    ]
    for load in loads:
        load.start()

    def head(n):
        return pl.ds(pl.multiple_of(n * HEAD_SIZE, HEAD_SIZE), HEAD_SIZE)

    own_tok = pl.ds(pl.multiple_of(c * TOK, TOK), TOK)
    mate_tok = pl.ds(pl.multiple_of((1 - c) * TOK, TOK), TOK)
    for k in range(2):
        for i, ref in ((0, k_hbm), (1, v_hbm)):
            pltpu.make_async_copy(ref.at[:, head(2 * c + k)], kv.at[0, k, i, own_tok], loc_sem.at[k]).start()
    for k in range(2):
        for h in range(2):
            pltpu.make_async_copy(q_hbm.at[:, head(4 * c + 2 * k + h)], qb.at[k, h, own_tok], loc_sem.at[2]).start()
    pltpu.make_async_copy(start_hbm, starts.at[c], loc_sem.at[3]).start()
    pltpu.make_async_copy(wo_hbm.at[:, pl.ds(pl.multiple_of(c * 512, 512), 512)], wo.at[c, r], loc_sem.at[4]).start()

    pl.semaphore_wait(bar, NREQ - 1 + 3)

    mate_copies = []

    def to_mate(src, dst, n, sem):
        copy = remote(src, dst, half_ssem.at[n], sem, mate, y)
        copy.start()
        mate_copies.append(copy)

    for k in range(2):
        for i, ref in ((0, k_hbm), (1, v_hbm)):
            to_mate(ref.at[:, head(2 * (1 - c) + k)], kv.at[0, k, i, own_tok], 2 * k + i, half_rsem.at[k])
    for k in range(2):
        for h in range(2):
            to_mate(q_hbm.at[:, head(4 * (1 - c) + 2 * k + h)], qb.at[k, h, own_tok], 4 + 2 * k + h, half_rsem.at[2])
    to_mate(start_hbm, starts.at[c], 8, half_rsem.at[3])

    def chip_at(dz, dx):
        return lax.rem(z + dz, NZ) * 8 + lax.rem(x + dx, 4) * 2 + c

    def send(src, dst, k, dz, dx):
        remote(kv.at[src, k], kv.at[dst, k], kv_ssem.at[dst, k], kv_rsem.at[dst, k], chip_at(dz, dx), y).start()

    def took(slot, k):
        view = kv.at[slot, k]
        pltpu.make_async_copy(view, view, kv_rsem.at[slot, k]).wait()

    wraps = {1: (x + 1) // 4, 3: (x + 3) // 4}
    odd = lax.rem(x, 2)

    for k in range(2):
        view = kv.at[0, k, :, own_tok]
        pltpu.make_async_copy(view, view, loc_sem.at[k]).wait()
        view = kv.at[0, k, :, mate_tok]
        pltpu.make_async_copy(view, view, half_rsem.at[k]).wait()
        send(0, 4, k, 1, 0)
        for d in (1, 3):
            @pl.when(wraps[d] == 0)
            def _():
                send(0, d, k, 0, d)

    def took4(k):
        took(4, k)
        send(4, 8, k, 1, 0)
        for d in (1, 3):
            send(4, d + 4 * (1 - wraps[d]), k, 0, d)

    def took8(k):
        took(8, k)
        for d in (1, 3):
            @pl.when(wraps[d] == 1)
            def _():
                send(8, d + 4, k, 0, d)

    def took13(k):
        took(1, k)
        took(3, k)
        send(1 + 2 * odd, 2, k, 0, 1 + 2 * odd)

    def took2(k):
        took(2, k)
        send(2, 6, k, 1, 0)

    wo_copies = []
    for h in range(2):
        half = pl.ds(h * 512, 512)
        for dx in range(4):
            target = z * 8 + lax.rem(x + dx, 4) * 2 + h

            def give(target=target, half=half, h=h):
                remote(wo_hbm.at[:, half], wo.at[h, r], wo_ssem.at[0], wo_rsem.at[0], target, y).start()

            if dx == 0:
                pl.when(c != h)(give)
            else:
                give()

    def ring(t):
        g = pl.ds(lax.rem(z + t, NZ) * 8, 8)
        view = wo.at[c, g]
        if t == 0:
            few = wo.at[c, pl.ds(z * 8, 7)]
            pltpu.make_async_copy(few, few, wo_rsem.at[0]).wait()
            one = wo.at[c, r]
            pltpu.make_async_copy(one, one, loc_sem.at[4]).wait()
        else:
            pltpu.make_async_copy(view, view, ring_rsem.at[t - 1]).wait()
        if t < NZ - 1:
            copy = remote(view, view, ring_ssem.at[t], ring_rsem.at[t], chip_at(NZ - 1, 0), y)
            copy.start()
            wo_copies.append(copy)
        remote(view, view, pair_ssem, pair_rsem, mate, y).start()

    view = qb.at[:, :, own_tok]
    pltpu.make_async_copy(view, view, loc_sem.at[2]).wait()
    view = qb.at[:, :, mate_tok]
    pltpu.make_async_copy(view, view, half_rsem.at[2]).wait()
    for k in range(2):
        qt[k] = jnp.concatenate([qb[k, 0].T, qb[k, 1].T], axis=1)
        for h in range(2):
            peak[k, :, 512 * h:512 * h + 512] = jnp.full((1, 512), sink_ref[4 * c + 2 * k + h] * HEAD_SIZE ** 0.5, F32)
    mass[...] = jnp.ones_like(mass)
    acc[...] = jnp.zeros_like(acc)
    pltpu.make_async_copy(starts.at[c], starts.at[c], loc_sem.at[3]).wait()
    pltpu.make_async_copy(starts.at[1 - c], starts.at[1 - c], half_rsem.at[3]).wait()
    ring(0)

    def attend(s, k):
        vt[...] = kv[s, k, 1].T
        first = (chip - s) * 512

        def tiles(h, carry):
            for half in range(2):
                cols = pl.ds(pl.multiple_of(h * 512 + half * 256, 256), 256)
                scores = dot(kv[s, k, 0], qt[k, :, cols])
                at = iota((1, 256), 1) + 256 * half
                low = jnp.maximum(starts[half] - first, at + (512 * s - 4095))
                key = iota((512, 256), 0)
                seen = key >= low
                if s == 0:
                    seen = seen & (key <= at)
                scores = jnp.where(seen, scores, MASKED)
                old = peak[k, :, cols]
                new = jnp.maximum(old, jnp.max(scores, axis=0, keepdims=True))
                probs = jnp.exp2((scores - new) * SCALE2)
                alpha = jnp.exp2((old - new) * SCALE2)
                peak[k, :, cols] = new
                mass[k, :, cols] = mass[k, :, cols] * alpha + jnp.sum(probs, axis=0, keepdims=True)
                acc[k, :, cols] = acc[k, :, cols] * alpha + dot(vt[...], probs.astype(BF))
            return carry

        lax.fori_loop(0, 2, tiles, 0)

    attend(0, 0)
    took4(0)
    attend(0, 1)
    took13(0)
    ring(1)
    attend(4, 0)
    took4(1)
    attend(1, 0)
    took13(1)
    attend(3, 0)
    ring(2)
    attend(4, 1)
    attend(1, 1)
    took8(0)
    attend(3, 1)
    took2(0)
    ring(3)
    attend(8, 0)
    took8(1)
    attend(2, 0)
    took2(1)
    attend(8, 1)
    ring(4)
    attend(2, 1)
    took(5, 0)
    attend(5, 0)
    route0, route1 = routes_ref[0:1, :], routes_ref[1:2, :]
    dest = iota((NREQ, TOK), 0)
    hot0 = jnp.where(dest == route0, 1.0, 0.0)
    hot1 = jnp.where(dest == route1, 1.0, 0.0)
    before = jnp.where(iota((TOK, TOK), 0) < iota((TOK, TOK), 1), 1.0, 0.0).astype(BF)
    earlier = dot((hot0 + hot1).astype(BF), before)
    slot0 = route0.astype(F32) * 16.0 + jnp.sum(hot0 * earlier, axis=0, keepdims=True)
    slot1 = route1.astype(F32) * 16.0 + jnp.sum(hot1 * (earlier + hot0), axis=0, keepdims=True)
    line = iota((512, TOK), 0)
    main_id = ((line >> 3) * 16 + (line & 7)).astype(F32)
    rem_id = ((line >> 3) * 16 + 8 + (line & 1)).astype(F32)
    e_main[...] = jnp.where((main_id == slot0) | (main_id == slot1), 1.0, 0.0).astype(BF)
    e_rem[...] = jnp.where((rem_id == slot0) | (rem_id == slot1), 1.0, 0.0).astype(BF)
    hosts = jnp.where(iota((EXPERTS, NREQ), 0) == placement_ref[...], 1.0, 0.0).astype(BF)
    logits = logits_ref[...]
    pick0 = jnp.sum(logits * dot(hosts, hot0.astype(BF)), axis=0, keepdims=True)
    pick1 = jnp.sum(logits * dot(hosts, hot1.astype(BF)), axis=0, keepdims=True)
    top = jnp.maximum(pick0, pick1)
    exp0, exp1 = jnp.exp(pick0 - top), jnp.exp(pick1 - top)
    total = exp0 + exp1
    sub = iota((128, TOK), 0)
    packed = jnp.where(sub == 0, slot0, jnp.where(sub == 1, slot1, jnp.where(sub == 2, exp0 / total, exp1 / total)))
    turned = packed.T
    s0, s1, w0, w1 = turned[:, 0:1], turned[:, 1:2], turned[:, 2:3], turned[:, 3:4]
    col = iota((TOK, 512), 1)
    for ids, ref in (((col >> 3) * 16 + (col & 7), g_main), ((col >> 3) * 16 + 8 + (col & 1), g_rem)):
        ids = ids.astype(F32)
        gate = jnp.where(ids == s0, w0, 0.0) + jnp.where(ids == s1, w1, 0.0)
        high = gate.astype(BF)
        ref[0] = high
        ref[1] = (gate - high.astype(F32)).astype(BF)


    took(7, 0)
    attend(7, 0)
    ring(5)
    took(5, 1)
    attend(5, 1)
    took(7, 1)
    attend(7, 1)
    ring(6)
    for k in range(2):
        took(6, k)
        attend(6, k)
    ring(7)

    for k in range(2):
        out = acc[k] / mass[k]
        for h in range(2):
            block = out[:, 512 * h:512 * h + 512].astype(BF).T
            part_cols = slice(128 * (2 * k + h), 128 * (2 * k + h) + 128)
            att_out[0, :, part_cols] = block[0:TOK]
            att_out[1, :, part_cols] = block[TOK:2 * TOK]
    copy = remote(att_out.at[1 - c], att_in, att_ssem, att_rsem, mate, y)
    copy.start()
    mate_copies.append(copy)
    wo2 = wo.reshape(2, D, 512)
    pltpu.make_async_copy(wo.at[1 - c], wo.at[1 - c], pair_rsem).wait()
    pltpu.make_async_copy(att_in, att_in, att_rsem).wait()


    def project(which):
        f = pl.ds(pl.multiple_of(which * Q, Q), Q)
        return dot_nt(att_out[c], wo2[c, f, :]) + dot_nt(att_in[...], wo2[1 - c, f, :])

    proj_copies = []
    for i in (1, 0, 2):
        proj_send[i] = project(peers[i]).astype(BF)
        copy = remote(proj_send.at[i], proj_recv.at[2 - i], proj_ssem.at[i], proj_rsem.at[2 - i], r, peers[i])
        copy.start()
        proj_copies.append(copy)
    loads[0].wait()
    own = res[...].astype(F32) + project(y)
    for i in range(3):
        pltpu.make_async_copy(proj_recv.at[i], proj_recv.at[i], proj_rsem.at[i]).wait()
    hidden = own + proj_recv[0].astype(F32) + proj_recv[1].astype(F32) + proj_recv[2].astype(F32)
    hid[...] = hidden

    square = jnp.sum(hidden * hidden, axis=1, keepdims=True)
    stat_send[...] = jnp.broadcast_to(square, (TOK, 128)).T[0:8, :]
    stat_copies = []
    for i in range(3):
        copy = remote(stat_send, stat_recv.at[2 - i], stat_ssem.at[i], stat_rsem.at[2 - i], r, peers[i])
        copy.start()
        stat_copies.append(copy)
    loads[1].wait()
    for i in range(3):
        pltpu.make_async_copy(stat_recv.at[i], stat_recv.at[i], stat_rsem.at[i]).wait()
    squares = stat_send[...] + stat_recv[0] + stat_recv[1] + stat_recv[2]
    factor = lax.rsqrt(squares[0:1, :] * (1.0 / D) + EPS)
    factor = jnp.broadcast_to(factor, (128, TOK)).T[:, 0:1]
    normed = (hidden * factor * gain[...]).astype(BF)

    disp2 = disp.reshape(512, WIDE)
    disp2[:, 0:Q] = dot(e_main[...], normed).astype(BF)
    spread = dot(e_rem[...], normed)
    piece = (iota((512, 128), 0) & 7) >> 1

    def by_piece(parts):
        return jnp.where(piece == 0, parts[0], jnp.where(piece == 1, parts[1], jnp.where(piece == 2, parts[2], parts[3])))

    disp2[:, Q:WIDE] = by_piece([spread[:, 128 * k:128 * k + 128] for k in range(4)]).astype(BF)

    def exchange(source, target, send_sem, recv_sems):
        for dz in Z_ORDER:
            def push(k, c):
                d = lax.rem(z + dz, NZ) * 8 + lax.rem(r + k, 8)
                remote(source.at[d], target.at[r], send_sem, recv_sems.at[z], d, y).start()
                return c
            lax.fori_loop(1 if dz == 0 else 0, 8, push, 0)
        copy = pltpu.make_async_copy(source.at[r], target.at[r], own_sem)
        copy.start()
        copy.wait()

    def arrived(target, recv_sems, dz):
        g = lax.rem(z + dz, NZ)
        count = 7 if dz == 0 else 8
        view = target.at[pl.ds(g * 8, count)]
        pltpu.make_async_copy(view, view, recv_sems.at[g]).wait()

    mine = rows.at[y]
    exchange(disp, mine, a2a_ssem, a2a_rsem)

    ag_copies = []

    def forward(i):
        g = pl.ds(lax.rem(z + Z_ORDER[i], NZ) * 8, 8)
        here, there, side = (ym, yp, 0) if i % 2 == 0 else (yp, ym, 1)
        view = rows.at[here, g]
        pltpu.make_async_copy(view, view, ag_rsem.at[side, i]).wait()
        copy = remote(view, view, ag_ssem.at[2, i], ag_rsem.at[2, i], r, there)
        copy.start()
        ag_copies.append(copy)

    for i, dz in enumerate(Z_ORDER):
        arrived(mine, a2a_rsem, dz)
        g = pl.ds(lax.rem(z + dz, NZ) * 8, 8)
        view = rows.at[y, g]
        for side, there in ((0, yp), (1, ym)):
            copy = remote(view, view, ag_ssem.at[side, i], ag_rsem.at[side, i], r, there)
            copy.start()
            ag_copies.append(copy)
        if i > 0:
            forward(i - 1)
    forward(7)
    for i in range(8):
        g = pl.ds(lax.rem(z + Z_ORDER[i], NZ) * 8, 8)
        here, side = (yp, 1) if i % 2 == 0 else (ym, 0)
        view = rows.at[here, g]
        pltpu.make_async_copy(view, view, ag_rsem.at[side, i]).wait()
        view = rows.at[y2, g]
        pltpu.make_async_copy(view, view, ag_rsem.at[2, i]).wait()

    rows2 = rows.reshape(4, 512, WIDE)
    row_id = iota((128, 512), 0)
    line_id = iota((128, 512), 1)
    for q in range(4):
        xbuf[0:512, Q * q:Q * q + Q] = rows2[q, :, 0:Q]
    for k in range(4):
        select = jnp.where(line_id == (row_id >> 1) * 8 + 2 * k + (row_id & 1), 1.0, 0.0).astype(BF)
        for q in range(4):
            xbuf[512:640, Q * q + 128 * k:Q * q + 128 * k + 128] = dot(select, rows2[q, :, Q:WIDE]).astype(BF)
    loads[2].wait()
    loads[3].wait()

    def inner(n, c):
        cols = pl.ds(pl.multiple_of(n * 256, 256), 256)
        gate = dot(xbuf[...], wg[:, cols])
        up = dot(xbuf[...], wu[:, cols])
        act[:, cols] = (gate / (1.0 + jnp.exp(-gate)) * up).astype(BF)
        return c

    lax.fori_loop(0, HID // 256, inner, 0)
    loads[4].wait()

    line_of = iota((512, 512), 0)
    row_of = iota((512, 512), 1)
    scatter = jnp.where(
        line_of == ((row_of & 127) >> 1) * 8 + 2 * (row_of >> 7) + (row_of & 1), 1.0, 0.0
    ).astype(BF)
    part2 = part.reshape(4, 512, WIDE)
    for j, which in enumerate((y2, yp, ym, y)):
        piece_out = dot_nt(act[...], wd[pl.ds(pl.multiple_of(which * Q, Q), Q), :])
        part2[j, :, 0:Q] = piece_out[0:512].astype(BF)
        tail = piece_out[512:640].astype(BF)
        stacked = jnp.concatenate([tail[:, 128 * k:128 * k + 128] for k in range(4)], axis=0)
        part2[j, :, Q:WIDE] = dot(scatter, stacked).astype(BF)
        if j == 0:
            rs = [
                remote(part.at[0, pl.ds(0, 32)], hop_l, rs_ssem.at[0], rs_rsem.at[0], r, yp),
                remote(part.at[0, pl.ds(32, 32)], hop_r, rs_ssem.at[1], rs_rsem.at[1], r, ym),
            ]
            rs[0].start()
            rs[1].start()
        if j == 1:
            rs.append(remote(part.at[1, pl.ds(32, 32)], from_l.at[pl.ds(32, 32)], rs_ssem.at[2], rs_rsem.at[2], r, yp))
            rs[2].start()
        if j == 2:
            rs.append(remote(part.at[2, pl.ds(0, 32)], from_r.at[pl.ds(0, 32)], rs_ssem.at[3], rs_rsem.at[3], r, ym))
            rs[3].start()
    hop_l2, hop_r2 = hop_l.reshape(256, WIDE), hop_r.reshape(256, WIDE)
    pltpu.make_async_copy(hop_l, hop_l, rs_rsem.at[0]).wait()
    part2[1, 0:256, :] = (part2[1, 0:256, :].astype(F32) + hop_l2[...].astype(F32)).astype(BF)
    rs.append(remote(part.at[1, pl.ds(0, 32)], from_l.at[pl.ds(0, 32)], rs_ssem.at[4], rs_rsem.at[4], r, yp))
    rs[4].start()
    pltpu.make_async_copy(hop_r, hop_r, rs_rsem.at[1]).wait()
    part2[2, 256:512, :] = (part2[2, 256:512, :].astype(F32) + hop_r2[...].astype(F32)).astype(BF)
    rs.append(remote(part.at[2, pl.ds(32, 32)], from_r.at[pl.ds(32, 32)], rs_ssem.at[5], rs_rsem.at[5], r, ym))
    rs[5].start()
    low, high = pl.ds(0, 32), pl.ds(32, 32)
    for ref, half, k in ((from_l, high, 2), (from_r, low, 3), (from_l, low, 4), (from_r, high, 5)):
        view = ref.at[half]
        pltpu.make_async_copy(view, view, rs_rsem.at[k]).wait()
    fin2 = fin.reshape(512, WIDE)
    from_l2, from_r2 = from_l.reshape(512, WIDE), from_r.reshape(512, WIDE)
    fin2[...] = (part2[3].astype(F32) + from_l2[...].astype(F32) + from_r2[...].astype(F32)).astype(BF)

    exchange(fin, ret, ret_ssem, ret_rsem)
    for dz in Z_ORDER:
        arrived(ret, ret_rsem, dz)
    ret2 = ret.reshape(512, WIDE)
    back = ret2[:, 0:Q]
    lines = ret2[:, Q:WIDE]
    masked = jnp.concatenate([jnp.where(piece == k, lines.astype(F32), 0.0).astype(BF) for k in range(4)], axis=1)
    mixture = dot(g_main[0], back) + dot(g_main[1], back) + dot(g_rem[0], masked) + dot(g_rem[1], masked)
    out_ref[...] = (hid[...] + mixture).astype(BF)

    for copy in mate_copies + wo_copies + proj_copies + stat_copies + ag_copies + rs:
        copy.wait_send()
    few = wo.at[0, pl.ds(0, 7)]
    pltpu.make_async_copy(few, few, wo_ssem.at[0]).wait()
    pltpu.make_async_copy(wo.at[c], wo.at[c], pair_ssem).wait()
    for sem, ref in ((a2a_ssem, disp), (ret_ssem, fin)):
        view = ref.at[pl.ds(0, NREQ - 1)]
        pltpu.make_async_copy(view, view, sem).wait()
    for s in range(1, 9):
        for k in range(2):
            view = kv.at[s, k]
            pltpu.make_async_copy(view, view, kv_ssem.at[s, k]).wait()


def layer_call(*args):
    vmem = pl.BlockSpec(memory_space=pltpu.VMEM)
    smem = pl.BlockSpec(memory_space=pltpu.SMEM)
    hbm = pl.BlockSpec(memory_space=pl.ANY)
    dma = pltpu.SemaphoreType.DMA
    chunk = (NREQ, 8, WIDE)
    return pl.pallas_call(
        layer_kernel,
        out_shape=jax.ShapeDtypeStruct((TOK, Q), BF),
        in_specs=[hbm, hbm, hbm, hbm, smem, hbm, hbm, hbm, vmem, vmem, vmem, hbm, hbm, hbm],
        out_specs=vmem,
        scratch_shapes=[
            pltpu.VMEM((9, 2, 2, 512, HEAD_SIZE), BF), pltpu.VMEM((2, 2, 512, HEAD_SIZE), BF),
            pltpu.VMEM((2, HEAD_SIZE, 1024), BF), pltpu.VMEM((HEAD_SIZE, 512), BF), pltpu.VMEM((2, 1, TOK), jnp.int32),
            pltpu.VMEM((2, 1, 1024), F32), pltpu.VMEM((2, 1, 1024), F32), pltpu.VMEM((2, HEAD_SIZE, 1024), F32),
            pltpu.VMEM((2, TOK, 512), BF), pltpu.VMEM((TOK, 512), BF),
            pltpu.VMEM((2, NREQ, 32, 512), BF), pltpu.VMEM((TOK, Q), BF), pltpu.VMEM((1, Q), F32),
            pltpu.VMEM((D, HID), BF), pltpu.VMEM((D, HID), BF), pltpu.VMEM((D, HID), BF),
            pltpu.VMEM((3, TOK, Q), BF), pltpu.VMEM((3, TOK, Q), BF), pltpu.VMEM((TOK, Q), F32),
            pltpu.VMEM((8, TOK), F32), pltpu.VMEM((3, 8, TOK), F32),
            pltpu.VMEM((512, TOK), BF), pltpu.VMEM((512, TOK), BF),
            pltpu.VMEM((2, TOK, 512), BF), pltpu.VMEM((2, TOK, 512), BF),
            pltpu.VMEM(chunk, BF), pltpu.VMEM((4,) + chunk, BF), pltpu.VMEM((640, D), BF), pltpu.VMEM((640, HID), BF),
            pltpu.VMEM((4,) + chunk, BF), pltpu.VMEM((32, 8, WIDE), BF), pltpu.VMEM((32, 8, WIDE), BF),
            pltpu.VMEM(chunk, BF), pltpu.VMEM(chunk, BF), pltpu.VMEM(chunk, BF), pltpu.VMEM(chunk, BF),
            dma((9, 2)), dma((9, 2)), dma((9,)), dma((4,)), dma((5,)), dma((1,)), dma((1,)), dma((7,)), dma((7,)),
            dma, dma, dma, dma,
            dma((5,)), dma((3,)), dma((3,)), dma((3,)), dma((3,)),
            dma, dma((8,)), dma((3, 8)), dma((3, 8)), dma((6,)), dma((6,)), dma, dma((8,)), dma,
        ],
        compiler_params=pltpu.CompilerParams(
            collective_id=1, has_side_effects=True, vmem_limit_bytes=60 << 20
        ),
        name="layer",
    )(*args)


def per_device(
    residual, queries, rotated_key_rows, values, req_start, head_sink_logit, out_proj, mid_gain,
    router_logits, routes, placement, w_gate, w_up, w_down,
):
    return layer_call(
        queries, rotated_key_rows, values, req_start.reshape(1, TOK), head_sink_logit, out_proj.T, residual,
        mid_gain.reshape(1, D), router_logits.T, routes.T, placement.reshape(1, NREQ), w_gate[0], w_up[0], w_down[0],
    )


def solution(mesh):
    in_specs = (
        P("req", None),
        P("req", "ffn"),
        P("req", "ffn"),
        P("req", "ffn"),
        P("req"),
        P("ffn"),
        P("ffn", "req"),
        P(),
        P("req", None),
        P("req", None),
        P(),
        P("req", None, "ffn"),
        P("req", None, "ffn"),
        P("req", None, "ffn"),
    )
    out_specs = P("req", "ffn")
    return jax.shard_map(
        per_device, mesh=mesh, in_specs=in_specs, out_specs=out_specs, check_vma=False
    )
```

```python
import jax
import jax.numpy as jnp
from jax import lax
from jax.experimental import pallas as pl
from jax.experimental.pallas import tpu as pltpu
from jax.sharding import PartitionSpec as P

QUERY_HEADS = 32
KEY_VALUE_HEADS = 16
HEAD_SIZE = 128
EXPERTS = 8
EPS = 1e-06
MESH = pl.DeviceIdType.MESH
BF = jnp.bfloat16
F32 = jnp.float32

NREQ = 64
NFFN = 4
NZ = 8
TOK = 256
D = 2048
Q = D // NFFN
HID = 768
WIDE = Q + 128
Z_ORDER = (0, 1, 7, 2, 6, 3, 5, 4)


def dot(a, b):
    return jnp.dot(a, b, preferred_element_type=F32)


def dot_nt(a, b):
    return lax.dot_general(a, b, (((1,), (1,)), ((), ())), preferred_element_type=F32)


def dot_tn(a, b):
    return lax.dot_general(a, b, (((0,), (0,)), ((), ())), preferred_element_type=F32)


def iota(shape, dim):
    return lax.broadcasted_iota(jnp.int32, shape, dim)


def remote(src, dst, send_sem, recv_sem, req, ffn):
    return pltpu.make_async_remote_copy(
        src_ref=src, dst_ref=dst, send_sem=send_sem, recv_sem=recv_sem,
        device_id=(req, ffn), device_id_type=MESH,
    )


SCALE = HEAD_SIZE ** (-0.5)
MASKED = -1e30


def layer_kernel(
    q_hbm, k_hbm, v_hbm, start_hbm, sink_ref, wo_hbm, res_hbm, gain_hbm, logits_ref, routes_ref, placement_ref,
    wg_hbm, wu_hbm, wd_hbm,
    out_ref,
    kv, qb, qt, starts, peak, mass, acc, att_out, att_in,
    wo, res, gain, wg, wu, wd,
    proj_send, proj_recv, hid, stat_send, stat_recv,
    e_main, e_rem, g_main, g_rem,
    disp, rows, xbuf, act, part, hop_l, hop_r, from_l, from_r, fin, ret,
    kv_ssem, kv_rsem, half_ssem, half_rsem, loc_sem, wo_ssem, wo_rsem, ring_ssem, ring_rsem, pair_ssem, pair_rsem,
    att_ssem, att_rsem,
    in_sem, proj_ssem, proj_rsem, stat_ssem, stat_rsem,
    a2a_ssem, a2a_rsem, ag_ssem, ag_rsem, rs_ssem, rs_rsem, ret_ssem, ret_rsem, own_sem,
):
    r = lax.axis_index("req")
    y = lax.axis_index("ffn")
    z = r // 8
    x = lax.rem(r // 2, 4)
    c = lax.rem(r, 2)
    chip = r // 2
    mate = r + 1 - 2 * c
    yp, ym, y2 = lax.rem(y + 1, 4), lax.rem(y + 3, 4), lax.rem(y + 2, 4)
    peers = (yp, y2, ym)

    bar = pltpu.get_barrier_semaphore()

    near = [(lax.rem(r + 8, NREQ), y), (lax.rem(r + NREQ - 8, NREQ), y)]
    near += [(z * 8 + lax.rem(r + k, 8), y) for k in range(1, 8)]
    near += [(r, p) for p in peers]
    for device in near:
        pl.semaphore_signal(bar, inc=1, device_id=device, device_id_type=MESH)

    y_cols = pl.ds(pl.multiple_of(y * Q, Q), Q)
    loads = [
        pltpu.make_async_copy(res_hbm.at[:, y_cols], res, in_sem.at[0]),
        pltpu.make_async_copy(gain_hbm.at[:, y_cols], gain, in_sem.at[1]),
        pltpu.make_async_copy(wg_hbm, wg, in_sem.at[2]),
        pltpu.make_async_copy(wu_hbm, wu, in_sem.at[3]),
        pltpu.make_async_copy(wd_hbm, wd, in_sem.at[4]),
    ]
    for load in loads:
        load.start()

    def head(n):
        return pl.ds(pl.multiple_of(n * HEAD_SIZE, HEAD_SIZE), HEAD_SIZE)

    own_tok = pl.ds(pl.multiple_of(c * TOK, TOK), TOK)
    mate_tok = pl.ds(pl.multiple_of((1 - c) * TOK, TOK), TOK)
    for k in range(2):
        for i, ref in ((0, k_hbm), (1, v_hbm)):
            pltpu.make_async_copy(ref.at[:, head(2 * c + k)], kv.at[0, k, i, own_tok], loc_sem.at[k]).start()
    for k in range(2):
        for h in range(2):
            pltpu.make_async_copy(q_hbm.at[:, head(4 * c + 2 * k + h)], qb.at[k, h, own_tok], loc_sem.at[2]).start()
    pltpu.make_async_copy(start_hbm, starts.at[c], loc_sem.at[3]).start()
    pltpu.make_async_copy(wo_hbm.at[:, pl.ds(pl.multiple_of(c * 512, 512), 512)], wo.at[c, r], loc_sem.at[4]).start()

    pl.semaphore_wait(bar, len(near))

    mate_copies = []

    def to_mate(src, dst, n, sem):
        copy = remote(src, dst, half_ssem.at[n], sem, mate, y)
        copy.start()
        mate_copies.append(copy)

    for k in range(2):
        for i, ref in ((0, k_hbm), (1, v_hbm)):
            to_mate(ref.at[:, head(2 * (1 - c) + k)], kv.at[0, k, i, own_tok], 2 * k + i, half_rsem.at[k])
    for k in range(2):
        for h in range(2):
            to_mate(q_hbm.at[:, head(4 * (1 - c) + 2 * k + h)], qb.at[k, h, own_tok], 4 + 2 * k + h, half_rsem.at[2])
    to_mate(start_hbm, starts.at[c], 8, half_rsem.at[3])

    def chip_at(dz, dx):
        return lax.rem(z + dz, NZ) * 8 + lax.rem(x + dx, 4) * 2 + c

    def send(src, dst, k, dz, dx):
        remote(kv.at[src, k], kv.at[dst, k], kv_ssem.at[dst, k], kv_rsem.at[dst, k], chip_at(dz, dx), y).start()

    def took(slot, k):
        view = kv.at[slot, k]
        pltpu.make_async_copy(view, view, kv_rsem.at[slot, k]).wait()

    wraps = {1: (x + 1) // 4, 3: (x + 3) // 4}
    odd = lax.rem(x, 2)

    for k in range(2):
        view = kv.at[0, k, :, own_tok]
        pltpu.make_async_copy(view, view, loc_sem.at[k]).wait()
        view = kv.at[0, k, :, mate_tok]
        pltpu.make_async_copy(view, view, half_rsem.at[k]).wait()
        send(0, 4, k, 1, 0)
        for d in (1, 3):
            @pl.when(wraps[d] == 0)
            def _():
                send(0, d, k, 0, d)

    def took4(k):
        took(4, k)
        send(4, 8, k, 1, 0)
        for d in (1, 3):
            @pl.when(wraps[d] == 1)
            def _():
                send(4, d, k, 0, d)

    def took8(k):
        took(8, k)
        for d in (1, 3):
            @pl.when(wraps[d] == 1)
            def _():
                send(8, d + 4, k, 0, d)

    def took13(k):
        took(1, k)
        took(3, k)
        send(1 + 2 * odd, 2, k, 0, 1 + 2 * odd)
        if k == 1:
            for d in (1, 3):
                @pl.when(wraps[d] == 0)
                def _():
                    send(4, d + 4, 0, 0, d)
                    send(4, d + 4, 1, 0, d)

    def took2(k):
        took(2, k)
        send(2, 6, k, 1, 0)

    wo_copies = []
    for h in range(2):
        half = pl.ds(h * 512, 512)
        for dx in range(4):
            target = z * 8 + lax.rem(x + dx, 4) * 2 + h

            def give(target=target, half=half, h=h):
                remote(wo_hbm.at[:, half], wo.at[h, r], wo_ssem.at[0], wo_rsem.at[0], target, y).start()

            if dx == 0:
                pl.when(c != h)(give)
            else:
                give()

    def ring(t, half):
        view = wo.at[c, pl.ds(lax.rem(z + t, NZ) * 8 + 4 * half, 4)]
        if t > 0:
            pltpu.make_async_copy(view, view, ring_rsem.at[t - 1, half]).wait()
        elif half == 0:
            few = wo.at[c, pl.ds(z * 8, 7)]
            pltpu.make_async_copy(few, few, wo_rsem.at[0]).wait()
            one = wo.at[c, r]
            pltpu.make_async_copy(one, one, loc_sem.at[4]).wait()
        if t < NZ - 1:
            copy = remote(view, view, ring_ssem.at[t, half], ring_rsem.at[t, half], chip_at(NZ - 1, 0), y)
            copy.start()
            wo_copies.append(copy)
        remote(view, view, pair_ssem, pair_rsem, mate, y).start()

    ring(0, 0)
    ring(0, 1)
    view = qb.at[:, :, own_tok]
    pltpu.make_async_copy(view, view, loc_sem.at[2]).wait()
    view = qb.at[:, :, mate_tok]
    pltpu.make_async_copy(view, view, half_rsem.at[2]).wait()
    for k in range(2):
        qt[k] = jnp.concatenate([qb[k, 0].T, qb[k, 1].T], axis=1)
        for h in range(2):
            peak[k, :, 512 * h:512 * h + 512] = jnp.full((1, 512), sink_ref[4 * c + 2 * k + h] * HEAD_SIZE ** 0.5, F32)
    mass[...] = jnp.ones_like(mass)
    acc[...] = jnp.zeros_like(acc)
    pltpu.make_async_copy(starts.at[c], starts.at[c], loc_sem.at[3]).wait()
    pltpu.make_async_copy(starts.at[1 - c], starts.at[1 - c], half_rsem.at[3]).wait()

    def attend(s, k):
        first = (chip - s) * 512
        scores = dot(kv[s, k, 0], qt[k])
        token = iota((1, 1024), 1) & 511
        both = jnp.concatenate([starts[0], starts[1]], axis=1)
        low = jnp.maximum(jnp.concatenate([both, both], axis=1) - first, token + (512 * s - 4095))
        key = iota((512, 1024), 0)
        seen = key >= low
        if s == 0:
            seen = seen & (key <= token)
        scores = jnp.where(seen, scores, MASKED)
        old = peak[k]
        new = jnp.maximum(old, jnp.max(scores, axis=0, keepdims=True))
        probs = jnp.exp((scores - new) * SCALE)
        alpha = jnp.exp((old - new) * SCALE)
        peak[k] = new
        mass[k] = mass[k] * alpha + jnp.sum(probs, axis=0, keepdims=True)
        acc[k] = acc[k] * alpha + dot_tn(kv[s, k, 1], probs.astype(BF))

    attend(0, 0)
    attend(0, 1)
    took4(0)
    ring(1, 0)
    attend(4, 0)
    ring(1, 1)
    route0, route1 = routes_ref[0:1, :], routes_ref[1:2, :]
    dest = iota((NREQ, TOK), 0)
    hot0 = jnp.where(dest == route0, 1.0, 0.0)
    hot1 = jnp.where(dest == route1, 1.0, 0.0)
    before = jnp.where(iota((TOK, TOK), 0) < iota((TOK, TOK), 1), 1.0, 0.0).astype(BF)
    earlier = dot((hot0 + hot1).astype(BF), before)
    slot0 = route0.astype(F32) * 16.0 + jnp.sum(hot0 * earlier, axis=0, keepdims=True)
    slot1 = route1.astype(F32) * 16.0 + jnp.sum(hot1 * (earlier + hot0), axis=0, keepdims=True)
    line = iota((512, TOK), 0)
    main_id = ((line >> 3) * 16 + (line & 7)).astype(F32)
    rem_id = ((line >> 3) * 16 + 8 + (line & 1)).astype(F32)
    e_main[...] = jnp.where((main_id == slot0) | (main_id == slot1), 1.0, 0.0).astype(BF)
    e_rem[...] = jnp.where((rem_id == slot0) | (rem_id == slot1), 1.0, 0.0).astype(BF)
    hosts = jnp.where(iota((EXPERTS, NREQ), 0) == placement_ref[...], 1.0, 0.0).astype(BF)
    logits = logits_ref[...]
    pick0 = jnp.sum(logits * dot(hosts, hot0.astype(BF)), axis=0, keepdims=True)
    pick1 = jnp.sum(logits * dot(hosts, hot1.astype(BF)), axis=0, keepdims=True)
    top = jnp.maximum(pick0, pick1)
    exp0, exp1 = jnp.exp(pick0 - top), jnp.exp(pick1 - top)
    total = exp0 + exp1
    sub = iota((128, TOK), 0)
    packed = jnp.where(sub == 0, slot0, jnp.where(sub == 1, slot1, jnp.where(sub == 2, exp0 / total, exp1 / total)))
    turned = packed.T
    s0, s1, w0, w1 = turned[:, 0:1], turned[:, 1:2], turned[:, 2:3], turned[:, 3:4]
    col = iota((TOK, 512), 1)
    for ids, ref in (((col >> 3) * 16 + (col & 7), g_main), ((col >> 3) * 16 + 8 + (col & 1), g_rem)):
        ids = ids.astype(F32)
        gate = jnp.where(ids == s0, w0, 0.0) + jnp.where(ids == s1, w1, 0.0)
        high = gate.astype(BF)
        ref[0] = high
        ref[1] = (gate - high.astype(F32)).astype(BF)


    took13(0)
    took4(1)
    ring(2, 0)
    attend(1, 0)
    attend(3, 0)
    ring(2, 1)
    attend(4, 1)
    took13(1)
    took8(0)
    ring(3, 0)
    attend(1, 1)
    attend(3, 1)
    ring(3, 1)
    took2(0)
    attend(8, 0)
    ring(4, 0)
    took8(1)
    attend(2, 0)
    ring(4, 1)
    took2(1)
    attend(8, 1)
    ring(5, 0)
    attend(2, 1)
    ring(5, 1)
    took(5, 0)
    attend(5, 0)
    ring(6, 0)
    took(7, 0)
    attend(7, 0)
    ring(6, 1)
    took(5, 1)
    attend(5, 1)
    ring(7, 0)
    took(7, 1)
    attend(7, 1)
    ring(7, 1)
    for k in range(2):
        took(6, k)
        attend(6, k)

    for k in range(2):
        out = acc[k] / mass[k]
        for h in range(2):
            block = out[:, 512 * h:512 * h + 512].astype(BF).T
            part_cols = slice(128 * (2 * k + h), 128 * (2 * k + h) + 128)
            att_out[0, :, part_cols] = block[0:TOK]
            att_out[1, :, part_cols] = block[TOK:2 * TOK]
    copy = remote(att_out.at[1 - c], att_in, att_ssem, att_rsem, mate, y)
    copy.start()
    mate_copies.append(copy)
    wo2 = wo.reshape(2, D, 512)
    pltpu.make_async_copy(wo.at[1 - c], wo.at[1 - c], pair_rsem).wait()
    pltpu.make_async_copy(att_in, att_in, att_rsem).wait()


    def project(which):
        f = pl.ds(pl.multiple_of(which * Q, Q), Q)
        return dot_nt(att_out[c], wo2[c, f, :]) + dot_nt(att_in[...], wo2[1 - c, f, :])

    proj_copies = []
    for i in (1, 0, 2):
        proj_send[i] = project(peers[i]).astype(BF)
        copy = remote(proj_send.at[i], proj_recv.at[2 - i], proj_ssem.at[i], proj_rsem.at[2 - i], r, peers[i])
        copy.start()
        proj_copies.append(copy)
    loads[0].wait()
    own = res[...].astype(F32) + project(y)
    for i in range(3):
        pltpu.make_async_copy(proj_recv.at[i], proj_recv.at[i], proj_rsem.at[i]).wait()
    hidden = own + proj_recv[0].astype(F32) + proj_recv[1].astype(F32) + proj_recv[2].astype(F32)
    hid[...] = hidden

    square = jnp.sum(hidden * hidden, axis=1, keepdims=True)
    stat_send[...] = jnp.broadcast_to(square, (TOK, 128)).T[0:8, :]
    stat_copies = []
    for i in range(3):
        copy = remote(stat_send, stat_recv.at[2 - i], stat_ssem.at[i], stat_rsem.at[2 - i], r, peers[i])
        copy.start()
        stat_copies.append(copy)
    loads[1].wait()
    for i in range(3):
        pltpu.make_async_copy(stat_recv.at[i], stat_recv.at[i], stat_rsem.at[i]).wait()
    squares = stat_send[...] + stat_recv[0] + stat_recv[1] + stat_recv[2]
    factor = lax.rsqrt(squares[0:1, :] * (1.0 / D) + EPS)
    factor = jnp.broadcast_to(factor, (128, TOK)).T[:, 0:1]
    normed = (hidden * factor * gain[...]).astype(BF)

    disp2 = disp.reshape(512, WIDE)
    disp2[:, 0:Q] = dot(e_main[...], normed).astype(BF)
    spread = dot(e_rem[...], normed)
    piece = (iota((512, 128), 0) & 7) >> 1

    def by_piece(parts):
        return jnp.where(piece == 0, parts[0], jnp.where(piece == 1, parts[1], jnp.where(piece == 2, parts[2], parts[3])))

    disp2[:, Q:WIDE] = by_piece([spread[:, 128 * k:128 * k + 128] for k in range(4)]).astype(BF)

    def exchange(source, target, send_sem, recv_sems):
        for dz in Z_ORDER:
            def push(k, c):
                d = lax.rem(z + dz, NZ) * 8 + lax.rem(r + k, 8)
                remote(source.at[d], target.at[r], send_sem, recv_sems.at[z], d, y).start()
                return c
            lax.fori_loop(1 if dz == 0 else 0, 8, push, 0)
        copy = pltpu.make_async_copy(source.at[r], target.at[r], own_sem)
        copy.start()
        copy.wait()

    def arrived(target, recv_sems, dz):
        g = lax.rem(z + dz, NZ)
        count = 7 if dz == 0 else 8
        view = target.at[pl.ds(g * 8, count)]
        pltpu.make_async_copy(view, view, recv_sems.at[g]).wait()

    mine = rows.at[y]
    exchange(disp, mine, a2a_ssem, a2a_rsem)

    ag_copies = []

    def forward(i):
        g = pl.ds(lax.rem(z + Z_ORDER[i], NZ) * 8, 8)
        here, there, side = (ym, yp, 0) if i % 2 == 0 else (yp, ym, 1)
        view = rows.at[here, g]
        pltpu.make_async_copy(view, view, ag_rsem.at[side, i]).wait()
        copy = remote(view, view, ag_ssem.at[2, i], ag_rsem.at[2, i], r, there)
        copy.start()
        ag_copies.append(copy)

    for i, dz in enumerate(Z_ORDER):
        arrived(mine, a2a_rsem, dz)
        g = pl.ds(lax.rem(z + dz, NZ) * 8, 8)
        view = rows.at[y, g]
        for side, there in ((0, yp), (1, ym)):
            copy = remote(view, view, ag_ssem.at[side, i], ag_rsem.at[side, i], r, there)
            copy.start()
            ag_copies.append(copy)
        if i > 0:
            forward(i - 1)
    forward(7)
    for i in range(8):
        g = pl.ds(lax.rem(z + Z_ORDER[i], NZ) * 8, 8)
        here, side = (yp, 1) if i % 2 == 0 else (ym, 0)
        view = rows.at[here, g]
        pltpu.make_async_copy(view, view, ag_rsem.at[side, i]).wait()
        view = rows.at[y2, g]
        pltpu.make_async_copy(view, view, ag_rsem.at[2, i]).wait()

    rows2 = rows.reshape(4, 512, WIDE)
    row_id = iota((128, 512), 0)
    line_id = iota((128, 512), 1)
    for q in range(4):
        xbuf[0:512, Q * q:Q * q + Q] = rows2[q, :, 0:Q]
    for k in range(4):
        select = jnp.where(line_id == (row_id >> 1) * 8 + 2 * k + (row_id & 1), 1.0, 0.0).astype(BF)
        for q in range(4):
            xbuf[512:640, Q * q + 128 * k:Q * q + 128 * k + 128] = dot(select, rows2[q, :, Q:WIDE]).astype(BF)
    loads[2].wait()
    loads[3].wait()

    def inner(n, c):
        cols = pl.ds(pl.multiple_of(n * 256, 256), 256)
        gate = dot(xbuf[...], wg[:, cols])
        up = dot(xbuf[...], wu[:, cols])
        act[:, cols] = (gate / (1.0 + jnp.exp(-gate)) * up).astype(BF)
        return c

    lax.fori_loop(0, HID // 256, inner, 0)
    loads[4].wait()

    line_of = iota((512, 512), 0)
    row_of = iota((512, 512), 1)
    scatter = jnp.where(
        line_of == ((row_of & 127) >> 1) * 8 + 2 * (row_of >> 7) + (row_of & 1), 1.0, 0.0
    ).astype(BF)
    part2 = part.reshape(4, 512, WIDE)
    for j, which in enumerate((y2, yp, ym, y)):
        piece_out = dot_nt(act[...], wd[pl.ds(pl.multiple_of(which * Q, Q), Q), :])
        part2[j, :, 0:Q] = piece_out[0:512].astype(BF)
        tail = piece_out[512:640].astype(BF)
        stacked = jnp.concatenate([tail[:, 128 * k:128 * k + 128] for k in range(4)], axis=0)
        part2[j, :, Q:WIDE] = dot(scatter, stacked).astype(BF)
        if j == 0:
            rs = [
                remote(part.at[0, pl.ds(0, 32)], hop_l, rs_ssem.at[0], rs_rsem.at[0], r, yp),
                remote(part.at[0, pl.ds(32, 32)], hop_r, rs_ssem.at[1], rs_rsem.at[1], r, ym),
            ]
            rs[0].start()
            rs[1].start()
        if j == 1:
            rs.append(remote(part.at[1, pl.ds(32, 32)], from_l.at[pl.ds(32, 32)], rs_ssem.at[2], rs_rsem.at[2], r, yp))
            rs[2].start()
        if j == 2:
            rs.append(remote(part.at[2, pl.ds(0, 32)], from_r.at[pl.ds(0, 32)], rs_ssem.at[3], rs_rsem.at[3], r, ym))
            rs[3].start()
    hop_l2, hop_r2 = hop_l.reshape(256, WIDE), hop_r.reshape(256, WIDE)
    pltpu.make_async_copy(hop_l, hop_l, rs_rsem.at[0]).wait()
    part2[1, 0:256, :] = (part2[1, 0:256, :].astype(F32) + hop_l2[...].astype(F32)).astype(BF)
    rs.append(remote(part.at[1, pl.ds(0, 32)], from_l.at[pl.ds(0, 32)], rs_ssem.at[4], rs_rsem.at[4], r, yp))
    rs[4].start()
    pltpu.make_async_copy(hop_r, hop_r, rs_rsem.at[1]).wait()
    part2[2, 256:512, :] = (part2[2, 256:512, :].astype(F32) + hop_r2[...].astype(F32)).astype(BF)
    rs.append(remote(part.at[2, pl.ds(32, 32)], from_r.at[pl.ds(32, 32)], rs_ssem.at[5], rs_rsem.at[5], r, ym))
    rs[5].start()
    low, high = pl.ds(0, 32), pl.ds(32, 32)
    for ref, half, k in ((from_l, high, 2), (from_r, low, 3), (from_l, low, 4), (from_r, high, 5)):
        view = ref.at[half]
        pltpu.make_async_copy(view, view, rs_rsem.at[k]).wait()
    fin2 = fin.reshape(512, WIDE)
    from_l2, from_r2 = from_l.reshape(512, WIDE), from_r.reshape(512, WIDE)
    fin2[...] = (part2[3].astype(F32) + from_l2[...].astype(F32) + from_r2[...].astype(F32)).astype(BF)

    exchange(fin, ret, ret_ssem, ret_rsem)
    for dz in Z_ORDER:
        arrived(ret, ret_rsem, dz)
    ret2 = ret.reshape(512, WIDE)
    back = ret2[:, 0:Q]
    lines = ret2[:, Q:WIDE]
    masked = jnp.concatenate([jnp.where(piece == k, lines.astype(F32), 0.0).astype(BF) for k in range(4)], axis=1)
    mixture = dot(g_main[0], back) + dot(g_main[1], back) + dot(g_rem[0], masked) + dot(g_rem[1], masked)
    out_ref[...] = (hid[...] + mixture).astype(BF)

    for copy in mate_copies + wo_copies + proj_copies + stat_copies + ag_copies + rs:
        copy.wait_send()
    few = wo.at[0, pl.ds(0, 7)]
    pltpu.make_async_copy(few, few, wo_ssem.at[0]).wait()
    pltpu.make_async_copy(wo.at[c], wo.at[c], pair_ssem).wait()
    for sem, ref in ((a2a_ssem, disp), (ret_ssem, fin)):
        view = ref.at[pl.ds(0, NREQ - 1)]
        pltpu.make_async_copy(view, view, sem).wait()
    for s in range(1, 9):
        for k in range(2):
            view = kv.at[s, k]
            pltpu.make_async_copy(view, view, kv_ssem.at[s, k]).wait()


def layer_call(*args):
    vmem = pl.BlockSpec(memory_space=pltpu.VMEM)
    smem = pl.BlockSpec(memory_space=pltpu.SMEM)
    hbm = pl.BlockSpec(memory_space=pl.ANY)
    dma = pltpu.SemaphoreType.DMA
    chunk = (NREQ, 8, WIDE)
    return pl.pallas_call(
        layer_kernel,
        out_shape=jax.ShapeDtypeStruct((TOK, Q), BF),
        in_specs=[hbm, hbm, hbm, hbm, smem, hbm, hbm, hbm, vmem, vmem, vmem, hbm, hbm, hbm],
        out_specs=vmem,
        scratch_shapes=[
            pltpu.VMEM((9, 2, 2, 512, HEAD_SIZE), BF), pltpu.VMEM((2, 2, 512, HEAD_SIZE), BF),
            pltpu.VMEM((2, HEAD_SIZE, 1024), BF), pltpu.VMEM((2, 1, TOK), jnp.int32),
            pltpu.VMEM((2, 1, 1024), F32), pltpu.VMEM((2, 1, 1024), F32), pltpu.VMEM((2, HEAD_SIZE, 1024), F32),
            pltpu.VMEM((2, TOK, 512), BF), pltpu.VMEM((TOK, 512), BF),
            pltpu.VMEM((2, NREQ, 32, 512), BF), pltpu.VMEM((TOK, Q), BF), pltpu.VMEM((1, Q), F32),
            pltpu.VMEM((D, HID), BF), pltpu.VMEM((D, HID), BF), pltpu.VMEM((D, HID), BF),
            pltpu.VMEM((3, TOK, Q), BF), pltpu.VMEM((3, TOK, Q), BF), pltpu.VMEM((TOK, Q), F32),
            pltpu.VMEM((8, TOK), F32), pltpu.VMEM((3, 8, TOK), F32),
            pltpu.VMEM((512, TOK), BF), pltpu.VMEM((512, TOK), BF),
            pltpu.VMEM((2, TOK, 512), BF), pltpu.VMEM((2, TOK, 512), BF),
            pltpu.VMEM(chunk, BF), pltpu.VMEM((4,) + chunk, BF), pltpu.VMEM((640, D), BF), pltpu.VMEM((640, HID), BF),
            pltpu.VMEM((4,) + chunk, BF), pltpu.VMEM((32, 8, WIDE), BF), pltpu.VMEM((32, 8, WIDE), BF),
            pltpu.VMEM(chunk, BF), pltpu.VMEM(chunk, BF), pltpu.VMEM(chunk, BF), pltpu.VMEM(chunk, BF),
            dma((9, 2)), dma((9, 2)), dma((9,)), dma((4,)), dma((5,)), dma((1,)), dma((1,)), dma((7, 2)), dma((7, 2)),
            dma, dma, dma, dma,
            dma((5,)), dma((3,)), dma((3,)), dma((3,)), dma((3,)),
            dma, dma((8,)), dma((3, 8)), dma((3, 8)), dma((6,)), dma((6,)), dma, dma((8,)), dma,
        ],
        compiler_params=pltpu.CompilerParams(
            collective_id=1, has_side_effects=True, vmem_limit_bytes=60 << 20
        ),
        name="layer",
    )(*args)


def per_device(
    residual, queries, rotated_key_rows, values, req_start, head_sink_logit, out_proj, mid_gain,
    router_logits, routes, placement, w_gate, w_up, w_down,
):
    return layer_call(
        queries, rotated_key_rows, values, req_start.reshape(1, TOK), head_sink_logit, out_proj.T, residual,
        mid_gain.reshape(1, D), router_logits.T, routes.T, placement.reshape(1, NREQ), w_gate[0], w_up[0], w_down[0],
    )


def solution(mesh):
    in_specs = (
        P("req", None),
        P("req", "ffn"),
        P("req", "ffn"),
        P("req", "ffn"),
        P("req"),
        P("ffn"),
        P("ffn", "req"),
        P(),
        P("req", None),
        P("req", None),
        P(),
        P("req", None, "ffn"),
        P("req", None, "ffn"),
        P("req", None, "ffn"),
    )
    out_specs = P("req", "ffn")
    return jax.shard_map(
        per_device, mesh=mesh, in_specs=in_specs, out_specs=out_specs, check_vma=False
    )
```

```python
import jax
import jax.numpy as jnp
from jax import lax
from jax.experimental import pallas as pl
from jax.experimental.pallas import tpu as pltpu
from jax.sharding import PartitionSpec as P

QUERY_HEADS = 32
KEY_VALUE_HEADS = 16
HEAD_SIZE = 128
EXPERTS = 8
EPS = 1e-06
MESH = pl.DeviceIdType.MESH
BF = jnp.bfloat16
F32 = jnp.float32

NREQ = 64
NFFN = 4
NZ = 8
TOK = 256
D = 2048
Q = D // NFFN
HID = 768
WIDE = Q + 128
Z_ORDER = (0, 1, 7, 2, 6, 3, 5, 4)


def dot(a, b):
    return jnp.dot(a, b, preferred_element_type=F32)


def dot_nt(a, b):
    return lax.dot_general(a, b, (((1,), (1,)), ((), ())), preferred_element_type=F32)


def dot_tn(a, b):
    return lax.dot_general(a, b, (((0,), (0,)), ((), ())), preferred_element_type=F32)


def iota(shape, dim):
    return lax.broadcasted_iota(jnp.int32, shape, dim)


def remote(src, dst, send_sem, recv_sem, req, ffn):
    return pltpu.make_async_remote_copy(
        src_ref=src, dst_ref=dst, send_sem=send_sem, recv_sem=recv_sem,
        device_id=(req, ffn), device_id_type=MESH,
    )


SCALE = HEAD_SIZE ** (-0.5)
MASKED = -1e30


def layer_kernel(
    q_hbm, k_hbm, v_hbm, start_hbm, sink_ref, wo_hbm, res_hbm, gain_hbm, logits_ref, routes_ref, placement_ref,
    wg_hbm, wu_hbm, wd_hbm,
    out_ref,
    kv, qb, qt, starts, peak, mass, acc, att_out, att_in,
    wo, res, gain, wg, wu, wd,
    proj_send, proj_recv, hid, stat_send, stat_recv,
    e_main, e_rem, g_main, g_rem,
    disp, rows, xbuf, act, part, hop_l, hop_r, from_l, from_r, fin, ret,
    kv_ssem, kv_rsem, half_ssem, half_rsem, loc_sem, wo_ssem, wo_rsem, ring_ssem, ring_rsem, pair_ssem, pair_rsem,
    att_ssem, att_rsem,
    in_sem, proj_ssem, proj_rsem, stat_ssem, stat_rsem,
    a2a_ssem, a2a_rsem, ag_ssem, ag_rsem, rs_ssem, rs_rsem, ret_ssem, ret_rsem, own_sem,
):
    r = lax.axis_index("req")
    y = lax.axis_index("ffn")
    z = r // 8
    x = lax.rem(r // 2, 4)
    c = lax.rem(r, 2)
    chip = r // 2
    mate = r + 1 - 2 * c
    yp, ym, y2 = lax.rem(y + 1, 4), lax.rem(y + 3, 4), lax.rem(y + 2, 4)
    peers = (yp, y2, ym)

    bar = pltpu.get_barrier_semaphore()

    near = [(lax.rem(r + 8, NREQ), y), (lax.rem(r + NREQ - 8, NREQ), y)]
    near += [(z * 8 + lax.rem(r + k, 8), y) for k in range(1, 8)]
    near += [(r, p) for p in peers]
    for device in near:
        pl.semaphore_signal(bar, inc=1, device_id=device, device_id_type=MESH)

    y_cols = pl.ds(pl.multiple_of(y * Q, Q), Q)
    loads = [
        pltpu.make_async_copy(res_hbm.at[:, y_cols], res, in_sem.at[0]),
        pltpu.make_async_copy(gain_hbm.at[:, y_cols], gain, in_sem.at[1]),
        pltpu.make_async_copy(wg_hbm, wg, in_sem.at[2]),
        pltpu.make_async_copy(wu_hbm, wu, in_sem.at[3]),
        pltpu.make_async_copy(wd_hbm, wd, in_sem.at[4]),
    ]
    for load in loads:
        load.start()

    def head(n):
        return pl.ds(pl.multiple_of(n * HEAD_SIZE, HEAD_SIZE), HEAD_SIZE)

    own_tok = pl.ds(pl.multiple_of(c * TOK, TOK), TOK)
    mate_tok = pl.ds(pl.multiple_of((1 - c) * TOK, TOK), TOK)
    for k in range(2):
        for i, ref in ((0, k_hbm), (1, v_hbm)):
            pltpu.make_async_copy(ref.at[:, head(2 * c + k)], kv.at[0, k, i, own_tok], loc_sem.at[k]).start()
    for k in range(2):
        for h in range(2):
            pltpu.make_async_copy(q_hbm.at[:, head(4 * c + 2 * k + h)], qb.at[k, h, own_tok], loc_sem.at[2]).start()
    pltpu.make_async_copy(start_hbm, starts.at[c], loc_sem.at[3]).start()
    pltpu.make_async_copy(wo_hbm.at[:, pl.ds(pl.multiple_of(c * 512, 512), 512)], wo.at[c, r], loc_sem.at[4]).start()

    pl.semaphore_wait(bar, len(near))

    mate_copies = []

    def to_mate(src, dst, n, sem):
        copy = remote(src, dst, half_ssem.at[n], sem, mate, y)
        copy.start()
        mate_copies.append(copy)

    for k in range(2):
        for i, ref in ((0, k_hbm), (1, v_hbm)):
            to_mate(ref.at[:, head(2 * (1 - c) + k)], kv.at[0, k, i, own_tok], 2 * k + i, half_rsem.at[k])
    for k in range(2):
        for h in range(2):
            to_mate(q_hbm.at[:, head(4 * (1 - c) + 2 * k + h)], qb.at[k, h, own_tok], 4 + 2 * k + h, half_rsem.at[2])
    to_mate(start_hbm, starts.at[c], 8, half_rsem.at[3])

    def chip_at(dz, dx):
        return lax.rem(z + dz, NZ) * 8 + lax.rem(x + dx, 4) * 2 + c

    def send(src, dst, k, dz, dx):
        remote(kv.at[src, k], kv.at[dst, k], kv_ssem.at[dst, k], kv_rsem.at[dst, k], chip_at(dz, dx), y).start()

    def took(slot, k):
        view = kv.at[slot, k]
        pltpu.make_async_copy(view, view, kv_rsem.at[slot, k]).wait()

    wraps = {1: (x + 1) // 4, 3: (x + 3) // 4}
    odd = lax.rem(x, 2)

    for k in range(2):
        view = kv.at[0, k, :, own_tok]
        pltpu.make_async_copy(view, view, loc_sem.at[k]).wait()
        view = kv.at[0, k, :, mate_tok]
        pltpu.make_async_copy(view, view, half_rsem.at[k]).wait()
        send(0, 4, k, 1, 0)
        for d in (1, 3):
            @pl.when(wraps[d] == 0)
            def _():
                send(0, d, k, 0, d)

    def took4(k):
        took(4, k)
        send(4, 8, k, 1, 0)
        for d in (1, 3):
            @pl.when(wraps[d] == 1)
            def _():
                send(4, d, k, 0, d)

    def took8(k):
        took(8, k)
        for d in (1, 3):
            @pl.when(wraps[d] == 1)
            def _():
                send(8, d + 4, k, 0, d)

    def took13(k):
        took(1, k)
        took(3, k)
        send(1 + 2 * odd, 2, k, 0, 1 + 2 * odd)
        if k == 1:
            for d in (1, 3):
                @pl.when(wraps[d] == 0)
                def _():
                    send(4, d + 4, 0, 0, d)
                    send(4, d + 4, 1, 0, d)

    def took2(k):
        took(2, k)
        send(2, 6, k, 1, 0)

    wo_copies = []
    for h in range(2):
        half = pl.ds(h * 512, 512)
        for dx in range(4):
            target = z * 8 + lax.rem(x + dx, 4) * 2 + h

            def give(target=target, half=half, h=h):
                remote(wo_hbm.at[:, half], wo.at[h, r], wo_ssem.at[0], wo_rsem.at[0], target, y).start()

            if dx == 0:
                pl.when(c != h)(give)
            else:
                give()

    def ring(t, half):
        view = wo.at[c, pl.ds(lax.rem(z + t, NZ) * 8 + 4 * half, 4)]
        if t > 0:
            pltpu.make_async_copy(view, view, ring_rsem.at[t - 1, half]).wait()
        elif half == 0:
            few = wo.at[c, pl.ds(z * 8, 7)]
            pltpu.make_async_copy(few, few, wo_rsem.at[0]).wait()
            one = wo.at[c, r]
            pltpu.make_async_copy(one, one, loc_sem.at[4]).wait()
        if t < NZ - 1:
            copy = remote(view, view, ring_ssem.at[t, half], ring_rsem.at[t, half], chip_at(NZ - 1, 0), y)
            copy.start()
            wo_copies.append(copy)
        remote(view, view, pair_ssem, pair_rsem, mate, y).start()

    ring(0, 0)
    ring(0, 1)
    view = qb.at[:, :, own_tok]
    pltpu.make_async_copy(view, view, loc_sem.at[2]).wait()
    view = qb.at[:, :, mate_tok]
    pltpu.make_async_copy(view, view, half_rsem.at[2]).wait()
    for k in range(2):
        qt[k] = jnp.concatenate([qb[k, 0].T, qb[k, 1].T], axis=1)
        for h in range(2):
            peak[k, :, 512 * h:512 * h + 512] = jnp.full((1, 512), sink_ref[4 * c + 2 * k + h] * HEAD_SIZE ** 0.5, F32)
    mass[...] = jnp.ones_like(mass)
    acc[...] = jnp.zeros_like(acc)
    pltpu.make_async_copy(starts.at[c], starts.at[c], loc_sem.at[3]).wait()
    pltpu.make_async_copy(starts.at[1 - c], starts.at[1 - c], half_rsem.at[3]).wait()

    def attend(s, k):
        first = (chip - s) * 512
        scores = dot(kv[s, k, 0], qt[k])
        token = iota((1, 1024), 1) & 511
        both = jnp.concatenate([starts[0], starts[1]], axis=1)
        low = jnp.maximum(jnp.concatenate([both, both], axis=1) - first, token + (512 * s - 4095))
        key = iota((512, 1024), 0)
        seen = key >= low
        if s == 0:
            seen = seen & (key <= token)
        scores = jnp.where(seen, scores, MASKED)
        old = peak[k]
        new = jnp.maximum(old, jnp.max(scores, axis=0, keepdims=True))
        probs = jnp.exp((scores - new) * SCALE)
        alpha = jnp.exp((old - new) * SCALE)
        peak[k] = new
        mass[k] = mass[k] * alpha + jnp.sum(probs, axis=0, keepdims=True)
        acc[k] = acc[k] * alpha + dot_tn(kv[s, k, 1], probs.astype(BF))

    attend(0, 0)
    attend(0, 1)
    took4(0)
    ring(1, 0)
    attend(4, 0)
    ring(1, 1)
    route0, route1 = routes_ref[0:1, :], routes_ref[1:2, :]
    dest = iota((NREQ, TOK), 0)
    hot0 = jnp.where(dest == route0, 1.0, 0.0)
    hot1 = jnp.where(dest == route1, 1.0, 0.0)
    before = jnp.where(iota((TOK, TOK), 0) < iota((TOK, TOK), 1), 1.0, 0.0).astype(BF)
    earlier = dot((hot0 + hot1).astype(BF), before)
    slot0 = route0.astype(F32) * 16.0 + jnp.sum(hot0 * earlier, axis=0, keepdims=True)
    slot1 = route1.astype(F32) * 16.0 + jnp.sum(hot1 * (earlier + hot0), axis=0, keepdims=True)
    line = iota((512, TOK), 0)
    main_id = ((line >> 3) * 16 + (line & 7)).astype(F32)
    rem_id = ((line >> 3) * 16 + 8 + (line & 1)).astype(F32)
    e_main[...] = jnp.where((main_id == slot0) | (main_id == slot1), 1.0, 0.0).astype(BF)
    e_rem[...] = jnp.where((rem_id == slot0) | (rem_id == slot1), 1.0, 0.0).astype(BF)
    hosts = jnp.where(iota((EXPERTS, NREQ), 0) == placement_ref[...], 1.0, 0.0).astype(BF)
    logits = logits_ref[...]
    pick0 = jnp.sum(logits * dot(hosts, hot0.astype(BF)), axis=0, keepdims=True)
    pick1 = jnp.sum(logits * dot(hosts, hot1.astype(BF)), axis=0, keepdims=True)
    top = jnp.maximum(pick0, pick1)
    exp0, exp1 = jnp.exp(pick0 - top), jnp.exp(pick1 - top)
    total = exp0 + exp1
    sub = iota((128, TOK), 0)
    packed = jnp.where(sub == 0, slot0, jnp.where(sub == 1, slot1, jnp.where(sub == 2, exp0 / total, exp1 / total)))
    turned = packed.T
    s0, s1, w0, w1 = turned[:, 0:1], turned[:, 1:2], turned[:, 2:3], turned[:, 3:4]
    col = iota((TOK, 512), 1)
    for ids, ref in (((col >> 3) * 16 + (col & 7), g_main), ((col >> 3) * 16 + 8 + (col & 1), g_rem)):
        ids = ids.astype(F32)
        gate = jnp.where(ids == s0, w0, 0.0) + jnp.where(ids == s1, w1, 0.0)
        high = gate.astype(BF)
        ref[0] = high
        ref[1] = (gate - high.astype(F32)).astype(BF)


    took13(0)
    took4(1)
    ring(2, 0)
    attend(1, 0)
    attend(3, 0)
    ring(2, 1)
    attend(4, 1)
    took13(1)
    took8(0)
    ring(3, 0)
    attend(1, 1)
    attend(3, 1)
    ring(3, 1)
    took2(0)
    attend(8, 0)
    ring(4, 0)
    took8(1)
    attend(2, 0)
    ring(4, 1)
    took2(1)
    attend(8, 1)
    ring(5, 0)
    attend(2, 1)
    ring(5, 1)
    took(5, 0)
    attend(5, 0)
    ring(6, 0)
    took(7, 0)
    attend(7, 0)
    ring(6, 1)
    took(5, 1)
    attend(5, 1)
    ring(7, 0)
    took(7, 1)
    attend(7, 1)
    ring(7, 1)
    for k in range(2):
        took(6, k)
        attend(6, k)

    for k in range(2):
        out = acc[k] / mass[k]
        for h in range(2):
            block = out[:, 512 * h:512 * h + 512].astype(BF).T
            part_cols = slice(128 * (2 * k + h), 128 * (2 * k + h) + 128)
            att_out[0, :, part_cols] = block[0:TOK]
            att_out[1, :, part_cols] = block[TOK:2 * TOK]
    copy = remote(att_out.at[1 - c], att_in, att_ssem, att_rsem, mate, y)
    copy.start()
    mate_copies.append(copy)
    wo2 = wo.reshape(2, D, 512)
    pltpu.make_async_copy(wo.at[1 - c], wo.at[1 - c], pair_rsem).wait()
    pltpu.make_async_copy(att_in, att_in, att_rsem).wait()


    def project(which):
        f = pl.ds(pl.multiple_of(which * Q, Q), Q)
        return dot_nt(att_out[c], wo2[c, f, :]) + dot_nt(att_in[...], wo2[1 - c, f, :])

    proj_copies = []
    for i in (1, 0, 2):
        proj_send[i] = project(peers[i]).astype(BF)
        copy = remote(proj_send.at[i], proj_recv.at[2 - i], proj_ssem.at[i], proj_rsem.at[2 - i], r, peers[i])
        copy.start()
        proj_copies.append(copy)
    loads[0].wait()
    own = res[...].astype(F32) + project(y)
    for i in range(3):
        pltpu.make_async_copy(proj_recv.at[i], proj_recv.at[i], proj_rsem.at[i]).wait()
    hidden = own + proj_recv[0].astype(F32) + proj_recv[1].astype(F32) + proj_recv[2].astype(F32)
    hid[...] = hidden

    square = jnp.sum(hidden * hidden, axis=1, keepdims=True)
    stat_send[...] = jnp.broadcast_to(square, (TOK, 128)).T[0:8, :]
    stat_copies = []
    for i in range(3):
        copy = remote(stat_send, stat_recv.at[2 - i], stat_ssem.at[i], stat_rsem.at[2 - i], r, peers[i])
        copy.start()
        stat_copies.append(copy)
    loads[1].wait()
    for i in range(3):
        pltpu.make_async_copy(stat_recv.at[i], stat_recv.at[i], stat_rsem.at[i]).wait()
    squares = stat_send[...] + stat_recv[0] + stat_recv[1] + stat_recv[2]
    factor = lax.rsqrt(squares[0:1, :] * (1.0 / D) + EPS)
    factor = jnp.broadcast_to(factor, (128, TOK)).T[:, 0:1]
    normed = (hidden * factor * gain[...]).astype(BF)

    disp2 = disp.reshape(512, WIDE)
    disp2[:, 0:Q] = dot(e_main[...], normed).astype(BF)
    spread = dot(e_rem[...], normed)
    piece = (iota((512, 128), 0) & 7) >> 1

    def by_piece(parts):
        return jnp.where(piece == 0, parts[0], jnp.where(piece == 1, parts[1], jnp.where(piece == 2, parts[2], parts[3])))

    disp2[:, Q:WIDE] = by_piece([spread[:, 128 * k:128 * k + 128] for k in range(4)]).astype(BF)

    def exchange(source, target, send_sem, recv_sems, picks, ordered):
        for i in picks:
            g = lax.rem(z + Z_ORDER[i], NZ)
            base = i * 8 if ordered else g * 8

            def push(k, carry):
                m = lax.rem(r + k, 8)
                remote(source.at[base + m], target.at[r], send_sem, recv_sems.at[z], g * 8 + m, y).start()
                return carry

            lax.fori_loop(1 if i == 0 else 0, 8, push, 0)
            if i == 0:
                copy = pltpu.make_async_copy(source.at[base + lax.rem(r, 8)], target.at[r], own_sem)
                copy.start()
                copy.wait()

    def arrived(target, recv_sems, dz):
        g = lax.rem(z + dz, NZ)
        count = 7 if dz == 0 else 8
        view = target.at[pl.ds(g * 8, count)]
        pltpu.make_async_copy(view, view, recv_sems.at[g]).wait()

    mine = rows.at[y]
    exchange(disp, mine, a2a_ssem, a2a_rsem, range(8), False)

    ag_copies = []

    def forward(i):
        g = pl.ds(lax.rem(z + Z_ORDER[i], NZ) * 8, 8)
        here, there, side = (ym, yp, 0) if i % 2 == 0 else (yp, ym, 1)
        view = rows.at[here, g]
        pltpu.make_async_copy(view, view, ag_rsem.at[side, i]).wait()
        copy = remote(view, view, ag_ssem.at[2, i], ag_rsem.at[2, i], r, there)
        copy.start()
        ag_copies.append(copy)

    for i, dz in enumerate(Z_ORDER):
        arrived(mine, a2a_rsem, dz)
        g = pl.ds(lax.rem(z + dz, NZ) * 8, 8)
        view = rows.at[y, g]
        for side, there in ((0, yp), (1, ym)):
            copy = remote(view, view, ag_ssem.at[side, i], ag_rsem.at[side, i], r, there)
            copy.start()
            ag_copies.append(copy)
        if i > 0:
            forward(i - 1)

    def gathered(i):
        g = pl.ds(lax.rem(z + Z_ORDER[i], NZ) * 8, 8)
        here, side = (yp, 1) if i % 2 == 0 else (ym, 0)
        view = rows.at[here, g]
        pltpu.make_async_copy(view, view, ag_rsem.at[side, i]).wait()
        view = rows.at[y2, g]
        pltpu.make_async_copy(view, view, ag_rsem.at[2, i]).wait()

    rows2 = rows.reshape(4, 512, WIDE)
    part2 = part.reshape(4, 512, WIDE)
    fin2 = fin.reshape(512, WIDE)
    from_l2, from_r2 = from_l.reshape(512, WIDE), from_r.reshape(512, WIDE)
    hop_l2, hop_r2 = hop_l.reshape(2, 128, WIDE), hop_r.reshape(2, 128, WIDE)
    row_id, line_id = iota((64, 256), 0), iota((64, 256), 1)
    line_of, row_of = iota((256, 256), 0), iota((256, 256), 1)
    scatter = jnp.where(
        line_of == ((row_of & 63) >> 1) * 8 + 2 * (row_of >> 6) + (row_of & 1), 1.0, 0.0
    ).astype(BF)
    rs = []

    def hidden_units(p):
        starts_at = [pl.multiple_of(lax.rem(z + Z_ORDER[4 * p + j], NZ) * 64, 64) for j in range(4)]
        for q in range(4):
            for j in range(4):
                xbuf[64 * j:64 * j + 64, Q * q:Q * q + Q] = rows2[q, pl.ds(starts_at[j], 64), 0:Q]
            tails = jnp.concatenate([rows2[q, pl.ds(at, 64), Q:WIDE] for at in starts_at], axis=0)
            for k in range(4):
                select = jnp.where(line_id == (row_id >> 1) * 8 + 2 * k + (row_id & 1), 1.0, 0.0).astype(BF)
                xbuf[256:320, Q * q + 128 * k:Q * q + 128 * k + 128] = dot(select, tails).astype(BF)

        def inner(n, carry):
            cols = pl.ds(pl.multiple_of(n * 256, 256), 256)
            gate = dot(xbuf[...], wg[:, cols])
            up = dot(xbuf[...], wu[:, cols])
            act[:, cols] = (gate / (1.0 + jnp.exp(-gate)) * up).astype(BF)
            return carry

        lax.fori_loop(0, HID // 256, inner, 0)

    def reduce_send(p, n, src, dst, device):
        copy = remote(src, dst, rs_ssem.at[p, n], rs_rsem.at[p, n], r, device)
        copy.start()
        rs.append(copy)

    def outputs(p):
        low, high = pl.ds(32 * p, 16), pl.ds(32 * p + 16, 16)
        for j, which in enumerate((y2, yp, ym, y)):
            piece_out = dot_nt(act[...], wd[pl.ds(pl.multiple_of(which * Q, Q), Q), :])
            part2[j, 256 * p:256 * p + 256, 0:Q] = piece_out[0:256].astype(BF)
            tail = piece_out[256:320].astype(BF)
            stacked = jnp.concatenate([tail[:, 128 * k:128 * k + 128] for k in range(4)], axis=0)
            part2[j, 256 * p:256 * p + 256, Q:WIDE] = dot(scatter, stacked).astype(BF)
            if j == 0:
                reduce_send(p, 0, part.at[0, low], hop_l.at[p], yp)
                reduce_send(p, 1, part.at[0, high], hop_r.at[p], ym)
            if j == 1:
                reduce_send(p, 2, part.at[1, high], from_l.at[high], yp)
            if j == 2:
                reduce_send(p, 3, part.at[2, low], from_r.at[low], ym)

    def hop(p):
        low, high = pl.ds(32 * p, 16), pl.ds(32 * p + 16, 16)
        low2, high2 = slice(256 * p, 256 * p + 128), slice(256 * p + 128, 256 * p + 256)
        pltpu.make_async_copy(hop_l.at[p], hop_l.at[p], rs_rsem.at[p, 0]).wait()
        part2[1, low2, :] = (part2[1, low2, :].astype(F32) + hop_l2[p].astype(F32)).astype(BF)
        reduce_send(p, 4, part.at[1, low], from_l.at[low], yp)
        pltpu.make_async_copy(hop_r.at[p], hop_r.at[p], rs_rsem.at[p, 1]).wait()
        part2[2, high2, :] = (part2[2, high2, :].astype(F32) + hop_r2[p].astype(F32)).astype(BF)
        reduce_send(p, 5, part.at[2, high], from_r.at[high], ym)

    def give_back(p):
        low, high = pl.ds(32 * p, 16), pl.ds(32 * p + 16, 16)
        for ref, half, k in ((from_l, high, 2), (from_r, low, 3), (from_l, low, 4), (from_r, high, 5)):
            view = ref.at[half]
            pltpu.make_async_copy(view, view, rs_rsem.at[p, k]).wait()
        at = slice(256 * p, 256 * p + 256)
        total_out = part2[3, at, :].astype(F32) + from_l2[at, :].astype(F32) + from_r2[at, :].astype(F32)
        fin2[at, :] = total_out.astype(BF)
        exchange(fin, ret, ret_ssem, ret_rsem, range(4 * p, 4 * p + 4), True)

    for i in range(4):
        gathered(i)
    loads[2].wait()
    loads[3].wait()
    hidden_units(0)
    forward(7)
    loads[4].wait()
    outputs(0)
    for i in range(4, 8):
        gathered(i)
    hidden_units(1)
    hop(0)
    outputs(1)
    give_back(0)
    hop(1)
    give_back(1)
    for dz in Z_ORDER:
        arrived(ret, ret_rsem, dz)
    ret2 = ret.reshape(512, WIDE)
    back = ret2[:, 0:Q]
    lines = ret2[:, Q:WIDE]
    masked = jnp.concatenate([jnp.where(piece == k, lines.astype(F32), 0.0).astype(BF) for k in range(4)], axis=1)
    mixture = dot(g_main[0], back) + dot(g_main[1], back) + dot(g_rem[0], masked) + dot(g_rem[1], masked)
    out_ref[...] = (hid[...] + mixture).astype(BF)

    for copy in mate_copies + wo_copies + proj_copies + stat_copies + ag_copies + rs:
        copy.wait_send()
    few = wo.at[0, pl.ds(0, 7)]
    pltpu.make_async_copy(few, few, wo_ssem.at[0]).wait()
    pltpu.make_async_copy(wo.at[c], wo.at[c], pair_ssem).wait()
    for sem, ref in ((a2a_ssem, disp), (ret_ssem, fin)):
        view = ref.at[pl.ds(0, NREQ - 1)]
        pltpu.make_async_copy(view, view, sem).wait()
    for s in range(1, 9):
        for k in range(2):
            view = kv.at[s, k]
            pltpu.make_async_copy(view, view, kv_ssem.at[s, k]).wait()


def layer_call(*args):
    vmem = pl.BlockSpec(memory_space=pltpu.VMEM)
    smem = pl.BlockSpec(memory_space=pltpu.SMEM)
    hbm = pl.BlockSpec(memory_space=pl.ANY)
    dma = pltpu.SemaphoreType.DMA
    chunk = (NREQ, 8, WIDE)
    return pl.pallas_call(
        layer_kernel,
        out_shape=jax.ShapeDtypeStruct((TOK, Q), BF),
        in_specs=[hbm, hbm, hbm, hbm, smem, hbm, hbm, hbm, vmem, vmem, vmem, hbm, hbm, hbm],
        out_specs=vmem,
        scratch_shapes=[
            pltpu.VMEM((9, 2, 2, 512, HEAD_SIZE), BF), pltpu.VMEM((2, 2, 512, HEAD_SIZE), BF),
            pltpu.VMEM((2, HEAD_SIZE, 1024), BF), pltpu.VMEM((2, 1, TOK), jnp.int32),
            pltpu.VMEM((2, 1, 1024), F32), pltpu.VMEM((2, 1, 1024), F32), pltpu.VMEM((2, HEAD_SIZE, 1024), F32),
            pltpu.VMEM((2, TOK, 512), BF), pltpu.VMEM((TOK, 512), BF),
            pltpu.VMEM((2, NREQ, 32, 512), BF), pltpu.VMEM((TOK, Q), BF), pltpu.VMEM((1, Q), F32),
            pltpu.VMEM((D, HID), BF), pltpu.VMEM((D, HID), BF), pltpu.VMEM((D, HID), BF),
            pltpu.VMEM((3, TOK, Q), BF), pltpu.VMEM((3, TOK, Q), BF), pltpu.VMEM((TOK, Q), F32),
            pltpu.VMEM((8, TOK), F32), pltpu.VMEM((3, 8, TOK), F32),
            pltpu.VMEM((512, TOK), BF), pltpu.VMEM((512, TOK), BF),
            pltpu.VMEM((2, TOK, 512), BF), pltpu.VMEM((2, TOK, 512), BF),
            pltpu.VMEM(chunk, BF), pltpu.VMEM((4,) + chunk, BF), pltpu.VMEM((320, D), BF), pltpu.VMEM((320, HID), BF),
            pltpu.VMEM((4,) + chunk, BF), pltpu.VMEM((2, 16, 8, WIDE), BF), pltpu.VMEM((2, 16, 8, WIDE), BF),
            pltpu.VMEM(chunk, BF), pltpu.VMEM(chunk, BF), pltpu.VMEM(chunk, BF), pltpu.VMEM(chunk, BF),
            dma((9, 2)), dma((9, 2)), dma((9,)), dma((4,)), dma((5,)), dma((1,)), dma((1,)), dma((7, 2)), dma((7, 2)),
            dma, dma, dma, dma,
            dma((5,)), dma((3,)), dma((3,)), dma((3,)), dma((3,)),
            dma, dma((8,)), dma((3, 8)), dma((3, 8)), dma((2, 6)), dma((2, 6)), dma, dma((8,)), dma,
        ],
        compiler_params=pltpu.CompilerParams(
            collective_id=1, has_side_effects=True, vmem_limit_bytes=60 << 20
        ),
        name="layer",
    )(*args)


def per_device(
    residual, queries, rotated_key_rows, values, req_start, head_sink_logit, out_proj, mid_gain,
    router_logits, routes, placement, w_gate, w_up, w_down,
):
    return layer_call(
        queries, rotated_key_rows, values, req_start.reshape(1, TOK), head_sink_logit, out_proj.T, residual,
        mid_gain.reshape(1, D), router_logits.T, routes.T, placement.reshape(1, NREQ), w_gate[0], w_up[0], w_down[0],
    )


def solution(mesh):
    in_specs = (
        P("req", None),
        P("req", "ffn"),
        P("req", "ffn"),
        P("req", "ffn"),
        P("req"),
        P("ffn"),
        P("ffn", "req"),
        P(),
        P("req", None),
        P("req", None),
        P(),
        P("req", None, "ffn"),
        P("req", None, "ffn"),
        P("req", None, "ffn"),
    )
    out_specs = P("req", "ffn")
    return jax.shard_map(
        per_device, mesh=mesh, in_specs=in_specs, out_specs=out_specs, check_vma=False
    )
```

```python
import jax
import jax.numpy as jnp
from jax import lax
from jax.experimental import pallas as pl
from jax.experimental.pallas import tpu as pltpu
from jax.sharding import PartitionSpec as P

QUERY_HEADS = 32
KEY_VALUE_HEADS = 16
HEAD_SIZE = 128
EXPERTS = 8
EPS = 1e-06
MESH = pl.DeviceIdType.MESH
BF = jnp.bfloat16
F32 = jnp.float32

NREQ = 64
NFFN = 4
NZ = 8
TOK = 256
D = 2048
Q = D // NFFN
HID = 768
WIDE = Q + 128
Z_ORDER = (0, 1, 7, 2, 6, 3, 5, 4)
PLAN = (
    ("w0a", 1, 0), ("R", 0, 0), ("w0a", 3, 0), ("w0a", 3, 1), ("z4", 0), ("R", 1, 0), ("heads",), ("R", 0, 1),
    ("z4", 1), ("w0a", 1, 1), ("w1a", 3, 0), ("w1a", 1, 0), ("w0b", 1, 0), ("R", 2, 0), ("R", 1, 1),
    ("w1a", 3, 1), ("f", 0), ("w1a", 1, 1), ("z8", 0), ("A", 1, 0), ("w0b", 3, 0), ("R", 2, 1), ("tables",),
    ("A", 4, 1), ("z8", 1), ("R", 3, 0), ("R", 3, 1), ("A", 0, 1), ("f", 1), ("w1b", 1, 0), ("A", 8, 0),
    ("A", 1, 1), ("R", 4, 0), ("R", 4, 1), ("A", 3, 0), ("w0b", 1, 1), ("z6", 0), ("A", 3, 1), ("w1b", 1, 1),
    ("w1b", 3, 1), ("A", 0, 0), ("R", 5, 0), ("A", 2, 0), ("w1b", 3, 0), ("w0b", 3, 1), ("A", 2, 1),
    ("R", 5, 1), ("z6", 1), ("A", 4, 0), ("A", 5, 0), ("R", 6, 0), ("A", 5, 1), ("A", 6, 0), ("R", 6, 1),
    ("A", 8, 1), ("A", 6, 1), ("A", 7, 1), ("A", 7, 0), ("R", 7, 0), ("R", 7, 1),
)
ALL = (0, 1, 2, 3)
WRAPS = {1: (3,), 3: (1, 2, 3)}


def dot(a, b):
    return jnp.dot(a, b, preferred_element_type=F32)


def dot_nt(a, b):
    return lax.dot_general(a, b, (((1,), (1,)), ((), ())), preferred_element_type=F32)


def dot_tn(a, b):
    return lax.dot_general(a, b, (((0,), (0,)), ((), ())), preferred_element_type=F32)


def iota(shape, dim):
    return lax.broadcasted_iota(jnp.int32, shape, dim)


def remote(src, dst, send_sem, recv_sem, req, ffn):
    return pltpu.make_async_remote_copy(
        src_ref=src, dst_ref=dst, send_sem=send_sem, recv_sem=recv_sem,
        device_id=(req, ffn), device_id_type=MESH,
    )


SCALE = HEAD_SIZE ** (-0.5)
MASKED = -1e30


def layer_kernel(
    q_hbm, k_hbm, v_hbm, start_hbm, sink_ref, wo_hbm, res_hbm, gain_hbm, logits_ref, routes_ref, placement_ref,
    wg_hbm, wu_hbm, wd_hbm,
    out_ref,
    kv, qb, qt, starts, peak, mass, acc, att_out, att_in,
    wo, res, gain, wg, wu, wd,
    proj_send, proj_recv, hid, stat_send, stat_recv,
    e_main, e_rem, g_main, g_rem,
    disp, rows, xbuf, act, part, hop_l, hop_r, from_l, from_r, fin, ret,
    kv_ssem, kv_rsem, half_ssem, half_rsem, loc_sem, wo_ssem, wo_rsem, ring_ssem, ring_rsem, pair_ssem, pair_rsem,
    att_ssem, att_rsem,
    in_sem, proj_ssem, proj_rsem, stat_ssem, stat_rsem,
    a2a_ssem, a2a_rsem, ag_ssem, ag_rsem, rs_ssem, rs_rsem, ret_ssem, ret_rsem, own_sem,
):
    r = lax.axis_index("req")
    y = lax.axis_index("ffn")
    z = r // 8
    x = lax.rem(r // 2, 4)
    c = lax.rem(r, 2)
    chip = r // 2
    mate = r + 1 - 2 * c
    yp, ym, y2 = lax.rem(y + 1, 4), lax.rem(y + 3, 4), lax.rem(y + 2, 4)
    peers = (yp, y2, ym)

    bar = pltpu.get_barrier_semaphore()

    near = [(lax.rem(r + 8, NREQ), y), (lax.rem(r + NREQ - 8, NREQ), y)]
    near += [(z * 8 + lax.rem(r + k, 8), y) for k in range(1, 8)]
    near += [(r, p) for p in peers]
    for device in near:
        pl.semaphore_signal(bar, inc=1, device_id=device, device_id_type=MESH)

    y_cols = pl.ds(pl.multiple_of(y * Q, Q), Q)
    loads = [
        pltpu.make_async_copy(res_hbm.at[:, y_cols], res, in_sem.at[0]),
        pltpu.make_async_copy(gain_hbm.at[:, y_cols], gain, in_sem.at[1]),
        pltpu.make_async_copy(wg_hbm, wg, in_sem.at[2]),
        pltpu.make_async_copy(wu_hbm, wu, in_sem.at[3]),
        pltpu.make_async_copy(wd_hbm, wd, in_sem.at[4]),
    ]
    for load in loads:
        load.start()

    def head(n):
        return pl.ds(pl.multiple_of(n * HEAD_SIZE, HEAD_SIZE), HEAD_SIZE)

    own_tok = pl.ds(pl.multiple_of(c * TOK, TOK), TOK)
    mate_tok = pl.ds(pl.multiple_of((1 - c) * TOK, TOK), TOK)
    for k in range(2):
        for i, ref in ((0, k_hbm), (1, v_hbm)):
            pltpu.make_async_copy(ref.at[:, head(2 * c + k)], kv.at[0, k, i, own_tok], loc_sem.at[k]).start()
    for k in range(2):
        for h in range(2):
            pltpu.make_async_copy(q_hbm.at[:, head(4 * c + 2 * k + h)], qb.at[k, h, own_tok], loc_sem.at[2]).start()
    pltpu.make_async_copy(start_hbm, starts.at[c], loc_sem.at[3]).start()
    pltpu.make_async_copy(wo_hbm.at[:, pl.ds(pl.multiple_of(c * 512, 512), 512)], wo.at[c, r], loc_sem.at[4]).start()

    pl.semaphore_wait(bar, len(near))

    mate_copies = []

    def to_mate(src, dst, n, sem):
        copy = remote(src, dst, half_ssem.at[n], sem, mate, y)
        copy.start()
        mate_copies.append(copy)

    for k in range(2):
        for i, ref in ((0, k_hbm), (1, v_hbm)):
            to_mate(ref.at[:, head(2 * (1 - c) + k)], kv.at[0, k, i, own_tok], 2 * k + i, half_rsem.at[k])
    for k in range(2):
        for h in range(2):
            to_mate(q_hbm.at[:, head(4 * (1 - c) + 2 * k + h)], qb.at[k, h, own_tok], 4 + 2 * k + h, half_rsem.at[2])
    to_mate(start_hbm, starts.at[c], 8, half_rsem.at[3])

    def chip_at(dz, dx):
        return lax.rem(z + dz, NZ) * 8 + lax.rem(x + dx, 4) * 2 + c

    def send(src, dst, k, dz, dx):
        remote(kv.at[src, k], kv.at[dst, k], kv_ssem.at[dst, k], kv_rsem.at[dst, k], chip_at(dz, dx), y).start()

    def took(slot, k):
        view = kv.at[slot, k]
        pltpu.make_async_copy(view, view, kv_rsem.at[slot, k]).wait()

    for k in range(2):
        view = kv.at[0, k, :, own_tok]
        pltpu.make_async_copy(view, view, loc_sem.at[k]).wait()
        view = kv.at[0, k, :, mate_tok]
        pltpu.make_async_copy(view, view, half_rsem.at[k]).wait()

    def only(columns, action):
        if len(columns) == 4:
            action()
        elif columns:
            hit = x == columns[0]
            for v in columns[1:]:
                hit = hit | (x == v)
            pl.when(hit)(action)

    waited = {(0, 0): set(ALL), (0, 1): set(ALL)}

    def need(slot, k, columns=ALL):
        done = waited.setdefault((slot, k), set())
        left = tuple(v for v in columns if v not in done)
        done.update(left)
        only(left, lambda: took(slot, k))

    def along_x(slot, dst, k, d, columns):
        need(slot, k, columns)
        only(columns, lambda: send(slot, dst, k, 0, d))

    wo_copies = []
    for h in range(2):
        half = pl.ds(h * 512, 512)
        for dx in range(4):
            target = z * 8 + lax.rem(x + dx, 4) * 2 + h

            def give(target=target, half=half, h=h):
                remote(wo_hbm.at[:, half], wo.at[h, r], wo_ssem.at[0], wo_rsem.at[0], target, y).start()

            if dx == 0:
                pl.when(c != h)(give)
            else:
                give()

    def ring(t, half):
        view = wo.at[c, pl.ds(lax.rem(z + t, NZ) * 8 + 4 * half, 4)]
        if t > 0:
            pltpu.make_async_copy(view, view, ring_rsem.at[t - 1, half]).wait()
        elif half == 0:
            few = wo.at[c, pl.ds(z * 8, 7)]
            pltpu.make_async_copy(few, few, wo_rsem.at[0]).wait()
            one = wo.at[c, r]
            pltpu.make_async_copy(one, one, loc_sem.at[4]).wait()
        if t < NZ - 1:
            copy = remote(view, view, ring_ssem.at[t, half], ring_rsem.at[t, half], chip_at(NZ - 1, 0), y)
            copy.start()
            wo_copies.append(copy)
        remote(view, view, pair_ssem, pair_rsem, mate, y).start()

    def heads():
        view = qb.at[:, :, own_tok]
        pltpu.make_async_copy(view, view, loc_sem.at[2]).wait()
        view = qb.at[:, :, mate_tok]
        pltpu.make_async_copy(view, view, half_rsem.at[2]).wait()
        for k in range(2):
            qt[k] = jnp.concatenate([qb[k, 0].T, qb[k, 1].T], axis=1)
            for h in range(2):
                peak[k, :, 512 * h:512 * h + 512] = jnp.full((1, 512), sink_ref[4 * c + 2 * k + h] * HEAD_SIZE ** 0.5, F32)
        mass[...] = jnp.ones_like(mass)
        acc[...] = jnp.zeros_like(acc)
        pltpu.make_async_copy(starts.at[c], starts.at[c], loc_sem.at[3]).wait()
        pltpu.make_async_copy(starts.at[1 - c], starts.at[1 - c], half_rsem.at[3]).wait()

    def attend(s, k):
        first = (chip - s) * 512
        scores = dot(kv[s, k, 0], qt[k])
        token = iota((1, 1024), 1) & 511
        both = jnp.concatenate([starts[0], starts[1]], axis=1)
        low = jnp.maximum(jnp.concatenate([both, both], axis=1) - first, token + (512 * s - 4095))
        key = iota((512, 1024), 0)
        seen = key >= low
        if s == 0:
            seen = seen & (key <= token)
        scores = jnp.where(seen, scores, MASKED)
        old = peak[k]
        new = jnp.maximum(old, jnp.max(scores, axis=0, keepdims=True))
        probs = jnp.exp((scores - new) * SCALE)
        alpha = jnp.exp((old - new) * SCALE)
        peak[k] = new
        mass[k] = mass[k] * alpha + jnp.sum(probs, axis=0, keepdims=True)
        acc[k] = acc[k] * alpha + dot_tn(kv[s, k, 1], probs.astype(BF))

    def tables():
        route0, route1 = routes_ref[0:1, :], routes_ref[1:2, :]
        dest = iota((NREQ, TOK), 0)
        hot0 = jnp.where(dest == route0, 1.0, 0.0)
        hot1 = jnp.where(dest == route1, 1.0, 0.0)
        before = jnp.where(iota((TOK, TOK), 0) < iota((TOK, TOK), 1), 1.0, 0.0).astype(BF)
        earlier = dot((hot0 + hot1).astype(BF), before)
        slot0 = route0.astype(F32) * 16.0 + jnp.sum(hot0 * earlier, axis=0, keepdims=True)
        slot1 = route1.astype(F32) * 16.0 + jnp.sum(hot1 * (earlier + hot0), axis=0, keepdims=True)
        line = iota((512, TOK), 0)
        main_id = ((line >> 3) * 16 + (line & 7)).astype(F32)
        rem_id = ((line >> 3) * 16 + 8 + (line & 1)).astype(F32)
        e_main[...] = jnp.where((main_id == slot0) | (main_id == slot1), 1.0, 0.0).astype(BF)
        e_rem[...] = jnp.where((rem_id == slot0) | (rem_id == slot1), 1.0, 0.0).astype(BF)
        hosts = jnp.where(iota((EXPERTS, NREQ), 0) == placement_ref[...], 1.0, 0.0).astype(BF)
        logits = logits_ref[...]
        pick0 = jnp.sum(logits * dot(hosts, hot0.astype(BF)), axis=0, keepdims=True)
        pick1 = jnp.sum(logits * dot(hosts, hot1.astype(BF)), axis=0, keepdims=True)
        top = jnp.maximum(pick0, pick1)
        exp0, exp1 = jnp.exp(pick0 - top), jnp.exp(pick1 - top)
        total = exp0 + exp1
        sub = iota((128, TOK), 0)
        packed = jnp.where(sub == 0, slot0, jnp.where(sub == 1, slot1, jnp.where(sub == 2, exp0 / total, exp1 / total)))
        turned = packed.T
        s0, s1, w0, w1 = turned[:, 0:1], turned[:, 1:2], turned[:, 2:3], turned[:, 3:4]
        col = iota((TOK, 512), 1)
        for ids, ref in (((col >> 3) * 16 + (col & 7), g_main), ((col >> 3) * 16 + 8 + (col & 1), g_rem)):
            ids = ids.astype(F32)
            gate = jnp.where(ids == s0, w0, 0.0) + jnp.where(ids == s1, w1, 0.0)
            high = gate.astype(BF)
            ref[0] = high
            ref[1] = (gate - high.astype(F32)).astype(BF)

    for name, *at in PLAN:
        if name == "heads":
            heads()
        elif name == "tables":
            tables()
        elif name == "R":
            ring(*at)
        elif name == "A":
            need(*at)
            attend(*at)
        elif name == "z4":
            send(0, 4, at[0], 1, 0)
        elif name == "z8":
            need(4, at[0])
            send(4, 8, at[0], 1, 0)
        elif name == "z6":
            need(2, at[0])
            send(2, 6, at[0], 1, 0)
        elif name == "f":
            along_x(1, 2, at[0], 1, (0, 2))
            along_x(3, 2, at[0], 3, (1, 3))
        else:
            d, k = at
            wrapped, second = int(name[1]), 4 * (name[2] == "b")
            columns = tuple(v for v in ALL if (v in WRAPS[d]) == bool(wrapped))
            along_x(4 * wrapped + second, d + second, k, d, columns)

    for k in range(2):
        out = acc[k] / mass[k]
        for h in range(2):
            block = out[:, 512 * h:512 * h + 512].astype(BF).T
            part_cols = slice(128 * (2 * k + h), 128 * (2 * k + h) + 128)
            att_out[0, :, part_cols] = block[0:TOK]
            att_out[1, :, part_cols] = block[TOK:2 * TOK]
    copy = remote(att_out.at[1 - c], att_in, att_ssem, att_rsem, mate, y)
    copy.start()
    mate_copies.append(copy)
    wo2 = wo.reshape(2, D, 512)
    pltpu.make_async_copy(wo.at[1 - c], wo.at[1 - c], pair_rsem).wait()
    pltpu.make_async_copy(att_in, att_in, att_rsem).wait()


    def project(which):
        f = pl.ds(pl.multiple_of(which * Q, Q), Q)
        return dot_nt(att_out[c], wo2[c, f, :]) + dot_nt(att_in[...], wo2[1 - c, f, :])

    proj_copies = []
    for i in (1, 0, 2):
        proj_send[i] = project(peers[i]).astype(BF)
        copy = remote(proj_send.at[i], proj_recv.at[2 - i], proj_ssem.at[i], proj_rsem.at[2 - i], r, peers[i])
        copy.start()
        proj_copies.append(copy)
    loads[0].wait()
    own = res[...].astype(F32) + project(y)
    for i in range(3):
        pltpu.make_async_copy(proj_recv.at[i], proj_recv.at[i], proj_rsem.at[i]).wait()
    hidden = own + proj_recv[0].astype(F32) + proj_recv[1].astype(F32) + proj_recv[2].astype(F32)
    hid[...] = hidden

    square = jnp.sum(hidden * hidden, axis=1, keepdims=True)
    stat_send[...] = jnp.broadcast_to(square, (TOK, 128)).T[0:8, :]
    stat_copies = []
    for i in range(3):
        copy = remote(stat_send, stat_recv.at[2 - i], stat_ssem.at[i], stat_rsem.at[2 - i], r, peers[i])
        copy.start()
        stat_copies.append(copy)
    loads[1].wait()
    for i in range(3):
        pltpu.make_async_copy(stat_recv.at[i], stat_recv.at[i], stat_rsem.at[i]).wait()
    squares = stat_send[...] + stat_recv[0] + stat_recv[1] + stat_recv[2]
    factor = lax.rsqrt(squares[0:1, :] * (1.0 / D) + EPS)
    factor = jnp.broadcast_to(factor, (128, TOK)).T[:, 0:1]
    normed = (hidden * factor * gain[...]).astype(BF)

    disp2 = disp.reshape(512, WIDE)
    disp2[:, 0:Q] = dot(e_main[...], normed).astype(BF)
    spread = dot(e_rem[...], normed)
    piece = (iota((512, 128), 0) & 7) >> 1

    def by_piece(parts):
        return jnp.where(piece == 0, parts[0], jnp.where(piece == 1, parts[1], jnp.where(piece == 2, parts[2], parts[3])))

    disp2[:, Q:WIDE] = by_piece([spread[:, 128 * k:128 * k + 128] for k in range(4)]).astype(BF)

    def exchange(source, target, send_sem, recv_sems, picks, ordered):
        for i in picks:
            g = lax.rem(z + Z_ORDER[i], NZ)
            base = i * 8 if ordered else g * 8

            def push(k, carry):
                m = lax.rem(r + k, 8)
                remote(source.at[base + m], target.at[r], send_sem, recv_sems.at[z], g * 8 + m, y).start()
                return carry

            lax.fori_loop(1 if i == 0 else 0, 8, push, 0)
            if i == 0:
                copy = pltpu.make_async_copy(source.at[base + lax.rem(r, 8)], target.at[r], own_sem)
                copy.start()
                copy.wait()

    def arrived(target, recv_sems, dz):
        g = lax.rem(z + dz, NZ)
        count = 7 if dz == 0 else 8
        view = target.at[pl.ds(g * 8, count)]
        pltpu.make_async_copy(view, view, recv_sems.at[g]).wait()

    mine = rows.at[y]
    exchange(disp, mine, a2a_ssem, a2a_rsem, range(8), False)

    ag_copies = []

    def forward(i):
        g = pl.ds(lax.rem(z + Z_ORDER[i], NZ) * 8, 8)
        here, there, side = (ym, yp, 0) if i % 2 == 0 else (yp, ym, 1)
        view = rows.at[here, g]
        pltpu.make_async_copy(view, view, ag_rsem.at[side, i]).wait()
        copy = remote(view, view, ag_ssem.at[2, i], ag_rsem.at[2, i], r, there)
        copy.start()
        ag_copies.append(copy)

    for i, dz in enumerate(Z_ORDER):
        arrived(mine, a2a_rsem, dz)
        g = pl.ds(lax.rem(z + dz, NZ) * 8, 8)
        view = rows.at[y, g]
        for side, there in ((0, yp), (1, ym)):
            copy = remote(view, view, ag_ssem.at[side, i], ag_rsem.at[side, i], r, there)
            copy.start()
            ag_copies.append(copy)
        if i > 0:
            forward(i - 1)

    def gathered(i):
        g = pl.ds(lax.rem(z + Z_ORDER[i], NZ) * 8, 8)
        here, side = (yp, 1) if i % 2 == 0 else (ym, 0)
        view = rows.at[here, g]
        pltpu.make_async_copy(view, view, ag_rsem.at[side, i]).wait()
        view = rows.at[y2, g]
        pltpu.make_async_copy(view, view, ag_rsem.at[2, i]).wait()

    rows2 = rows.reshape(4, 512, WIDE)
    part2 = part.reshape(4, 512, WIDE)
    fin2 = fin.reshape(512, WIDE)
    from_l2, from_r2 = from_l.reshape(512, WIDE), from_r.reshape(512, WIDE)
    hop_l2, hop_r2 = hop_l.reshape(2, 128, WIDE), hop_r.reshape(2, 128, WIDE)
    row_id, line_id = iota((64, 256), 0), iota((64, 256), 1)
    line_of, row_of = iota((256, 256), 0), iota((256, 256), 1)
    scatter = jnp.where(
        line_of == ((row_of & 63) >> 1) * 8 + 2 * (row_of >> 6) + (row_of & 1), 1.0, 0.0
    ).astype(BF)
    rs = []

    def hidden_units(p):
        starts_at = [pl.multiple_of(lax.rem(z + Z_ORDER[4 * p + j], NZ) * 64, 64) for j in range(4)]
        for q in range(4):
            for j in range(4):
                xbuf[64 * j:64 * j + 64, Q * q:Q * q + Q] = rows2[q, pl.ds(starts_at[j], 64), 0:Q]
            tails = jnp.concatenate([rows2[q, pl.ds(at, 64), Q:WIDE] for at in starts_at], axis=0)
            for k in range(4):
                select = jnp.where(line_id == (row_id >> 1) * 8 + 2 * k + (row_id & 1), 1.0, 0.0).astype(BF)
                xbuf[256:320, Q * q + 128 * k:Q * q + 128 * k + 128] = dot(select, tails).astype(BF)

        def inner(n, carry):
            cols = pl.ds(pl.multiple_of(n * 256, 256), 256)
            gate = dot(xbuf[...], wg[:, cols])
            up = dot(xbuf[...], wu[:, cols])
            act[:, cols] = (gate / (1.0 + jnp.exp(-gate)) * up).astype(BF)
            return carry

        lax.fori_loop(0, HID // 256, inner, 0)

    def reduce_send(p, n, src, dst, device):
        copy = remote(src, dst, rs_ssem.at[p, n], rs_rsem.at[p, n], r, device)
        copy.start()
        rs.append(copy)

    def outputs(p):
        low, high = pl.ds(32 * p, 16), pl.ds(32 * p + 16, 16)
        for j, which in enumerate((y2, yp, ym, y)):
            piece_out = dot_nt(act[...], wd[pl.ds(pl.multiple_of(which * Q, Q), Q), :])
            part2[j, 256 * p:256 * p + 256, 0:Q] = piece_out[0:256].astype(BF)
            tail = piece_out[256:320].astype(BF)
            stacked = jnp.concatenate([tail[:, 128 * k:128 * k + 128] for k in range(4)], axis=0)
            part2[j, 256 * p:256 * p + 256, Q:WIDE] = dot(scatter, stacked).astype(BF)
            if j == 0:
                reduce_send(p, 0, part.at[0, low], hop_l.at[p], yp)
                reduce_send(p, 1, part.at[0, high], hop_r.at[p], ym)
            if j == 1:
                reduce_send(p, 2, part.at[1, high], from_l.at[high], yp)
            if j == 2:
                reduce_send(p, 3, part.at[2, low], from_r.at[low], ym)

    def hop(p):
        low, high = pl.ds(32 * p, 16), pl.ds(32 * p + 16, 16)
        low2, high2 = slice(256 * p, 256 * p + 128), slice(256 * p + 128, 256 * p + 256)
        pltpu.make_async_copy(hop_l.at[p], hop_l.at[p], rs_rsem.at[p, 0]).wait()
        part2[1, low2, :] = (part2[1, low2, :].astype(F32) + hop_l2[p].astype(F32)).astype(BF)
        reduce_send(p, 4, part.at[1, low], from_l.at[low], yp)
        pltpu.make_async_copy(hop_r.at[p], hop_r.at[p], rs_rsem.at[p, 1]).wait()
        part2[2, high2, :] = (part2[2, high2, :].astype(F32) + hop_r2[p].astype(F32)).astype(BF)
        reduce_send(p, 5, part.at[2, high], from_r.at[high], ym)

    def give_back(p):
        low, high = pl.ds(32 * p, 16), pl.ds(32 * p + 16, 16)
        for ref, half, k in ((from_l, high, 2), (from_r, low, 3), (from_l, low, 4), (from_r, high, 5)):
            view = ref.at[half]
            pltpu.make_async_copy(view, view, rs_rsem.at[p, k]).wait()
        at = slice(256 * p, 256 * p + 256)
        total_out = part2[3, at, :].astype(F32) + from_l2[at, :].astype(F32) + from_r2[at, :].astype(F32)
        fin2[at, :] = total_out.astype(BF)
        exchange(fin, ret, ret_ssem, ret_rsem, range(4 * p, 4 * p + 4), True)

    for i in range(4):
        gathered(i)
    loads[2].wait()
    loads[3].wait()
    hidden_units(0)
    forward(7)
    loads[4].wait()
    outputs(0)
    for i in range(4, 8):
        gathered(i)
    hidden_units(1)
    hop(0)
    outputs(1)
    give_back(0)
    hop(1)
    give_back(1)
    for dz in Z_ORDER:
        arrived(ret, ret_rsem, dz)
    ret2 = ret.reshape(512, WIDE)
    back = ret2[:, 0:Q]
    lines = ret2[:, Q:WIDE]
    masked = jnp.concatenate([jnp.where(piece == k, lines.astype(F32), 0.0).astype(BF) for k in range(4)], axis=1)
    mixture = dot(g_main[0], back) + dot(g_main[1], back) + dot(g_rem[0], masked) + dot(g_rem[1], masked)
    out_ref[...] = (hid[...] + mixture).astype(BF)

    for copy in mate_copies + wo_copies + proj_copies + stat_copies + ag_copies + rs:
        copy.wait_send()
    few = wo.at[0, pl.ds(0, 7)]
    pltpu.make_async_copy(few, few, wo_ssem.at[0]).wait()
    pltpu.make_async_copy(wo.at[c], wo.at[c], pair_ssem).wait()
    for sem, ref in ((a2a_ssem, disp), (ret_ssem, fin)):
        view = ref.at[pl.ds(0, NREQ - 1)]
        pltpu.make_async_copy(view, view, sem).wait()
    for s in range(1, 9):
        for k in range(2):
            view = kv.at[s, k]
            pltpu.make_async_copy(view, view, kv_ssem.at[s, k]).wait()


def layer_call(*args):
    vmem = pl.BlockSpec(memory_space=pltpu.VMEM)
    smem = pl.BlockSpec(memory_space=pltpu.SMEM)
    hbm = pl.BlockSpec(memory_space=pl.ANY)
    dma = pltpu.SemaphoreType.DMA
    chunk = (NREQ, 8, WIDE)
    return pl.pallas_call(
        layer_kernel,
        out_shape=jax.ShapeDtypeStruct((TOK, Q), BF),
        in_specs=[hbm, hbm, hbm, hbm, smem, hbm, hbm, hbm, vmem, vmem, vmem, hbm, hbm, hbm],
        out_specs=vmem,
        scratch_shapes=[
            pltpu.VMEM((9, 2, 2, 512, HEAD_SIZE), BF), pltpu.VMEM((2, 2, 512, HEAD_SIZE), BF),
            pltpu.VMEM((2, HEAD_SIZE, 1024), BF), pltpu.VMEM((2, 1, TOK), jnp.int32),
            pltpu.VMEM((2, 1, 1024), F32), pltpu.VMEM((2, 1, 1024), F32), pltpu.VMEM((2, HEAD_SIZE, 1024), F32),
            pltpu.VMEM((2, TOK, 512), BF), pltpu.VMEM((TOK, 512), BF),
            pltpu.VMEM((2, NREQ, 32, 512), BF), pltpu.VMEM((TOK, Q), BF), pltpu.VMEM((1, Q), F32),
            pltpu.VMEM((D, HID), BF), pltpu.VMEM((D, HID), BF), pltpu.VMEM((D, HID), BF),
            pltpu.VMEM((3, TOK, Q), BF), pltpu.VMEM((3, TOK, Q), BF), pltpu.VMEM((TOK, Q), F32),
            pltpu.VMEM((8, TOK), F32), pltpu.VMEM((3, 8, TOK), F32),
            pltpu.VMEM((512, TOK), BF), pltpu.VMEM((512, TOK), BF),
            pltpu.VMEM((2, TOK, 512), BF), pltpu.VMEM((2, TOK, 512), BF),
            pltpu.VMEM(chunk, BF), pltpu.VMEM((4,) + chunk, BF), pltpu.VMEM((320, D), BF), pltpu.VMEM((320, HID), BF),
            pltpu.VMEM((4,) + chunk, BF), pltpu.VMEM((2, 16, 8, WIDE), BF), pltpu.VMEM((2, 16, 8, WIDE), BF),
            pltpu.VMEM(chunk, BF), pltpu.VMEM(chunk, BF), pltpu.VMEM(chunk, BF), pltpu.VMEM(chunk, BF),
            dma((9, 2)), dma((9, 2)), dma((9,)), dma((4,)), dma((5,)), dma((1,)), dma((1,)), dma((7, 2)), dma((7, 2)),
            dma, dma, dma, dma,
            dma((5,)), dma((3,)), dma((3,)), dma((3,)), dma((3,)),
            dma, dma((8,)), dma((3, 8)), dma((3, 8)), dma((2, 6)), dma((2, 6)), dma, dma((8,)), dma,
        ],
        compiler_params=pltpu.CompilerParams(
            collective_id=1, has_side_effects=True, vmem_limit_bytes=60 << 20
        ),
        name="layer",
    )(*args)


def per_device(
    residual, queries, rotated_key_rows, values, req_start, head_sink_logit, out_proj, mid_gain,
    router_logits, routes, placement, w_gate, w_up, w_down,
):
    return layer_call(
        queries, rotated_key_rows, values, req_start.reshape(1, TOK), head_sink_logit, out_proj.T, residual,
        mid_gain.reshape(1, D), router_logits.T, routes.T, placement.reshape(1, NREQ), w_gate[0], w_up[0], w_down[0],
    )


def solution(mesh):
    in_specs = (
        P("req", None),
        P("req", "ffn"),
        P("req", "ffn"),
        P("req", "ffn"),
        P("req"),
        P("ffn"),
        P("ffn", "req"),
        P(),
        P("req", None),
        P("req", None),
        P(),
        P("req", None, "ffn"),
        P("req", None, "ffn"),
        P("req", None, "ffn"),
    )
    out_specs = P("req", "ffn")
    return jax.shard_map(
        per_device, mesh=mesh, in_specs=in_specs, out_specs=out_specs, check_vma=False
    )
```

```python
import jax
import jax.numpy as jnp
from jax import lax
from jax.experimental import pallas as pl
from jax.experimental.pallas import tpu as pltpu
from jax.sharding import PartitionSpec as P

QUERY_HEADS = 32
KEY_VALUE_HEADS = 16
HEAD_SIZE = 128
EXPERTS = 8
EPS = 1e-06
MESH = pl.DeviceIdType.MESH
BF = jnp.bfloat16
F32 = jnp.float32

NREQ = 64
NFFN = 4
NZ = 8
TOK = 256
D = 2048
Q = D // NFFN
HID = 768
WIDE = Q + 128
PARTS = 4
SPAN = 8 // PARTS
LINES = 64 * SPAN
TAIL = 16 * SPAN
Z_ORDER = (0, 1, 7, 2, 6, 3, 5, 4)
PLAN = (
    ("w0a", 1, 0), ("R", 0, 0), ("w0a", 3, 0), ("w0a", 3, 1), ("z4", 0), ("R", 1, 0), ("heads",), ("R", 0, 1),
    ("z4", 1), ("w0a", 1, 1), ("w1a", 3, 0), ("w1a", 1, 0), ("w0b", 1, 0), ("R", 2, 0), ("R", 1, 1),
    ("w1a", 3, 1), ("f", 0), ("w1a", 1, 1), ("z8", 0), ("A", 1, 0), ("w0b", 3, 0), ("R", 2, 1), ("tables",),
    ("A", 4, 1), ("z8", 1), ("R", 3, 0), ("R", 3, 1), ("A", 0, 1), ("f", 1), ("w1b", 1, 0), ("A", 8, 0),
    ("A", 1, 1), ("R", 4, 0), ("R", 4, 1), ("A", 3, 0), ("w0b", 1, 1), ("z6", 0), ("A", 3, 1), ("w1b", 1, 1),
    ("w1b", 3, 1), ("A", 0, 0), ("R", 5, 0), ("A", 2, 0), ("w1b", 3, 0), ("w0b", 3, 1), ("A", 2, 1),
    ("R", 5, 1), ("z6", 1), ("A", 4, 0), ("A", 5, 0), ("R", 6, 0), ("A", 5, 1), ("A", 6, 0), ("R", 6, 1),
    ("A", 8, 1), ("A", 6, 1), ("A", 7, 1), ("A", 7, 0), ("R", 7, 0), ("R", 7, 1),
)
ALL = (0, 1, 2, 3)
WRAPS = {1: (3,), 3: (1, 2, 3)}


def dot(a, b):
    return jnp.dot(a, b, preferred_element_type=F32)


def dot_nt(a, b):
    return lax.dot_general(a, b, (((1,), (1,)), ((), ())), preferred_element_type=F32)


def dot_tn(a, b):
    return lax.dot_general(a, b, (((0,), (0,)), ((), ())), preferred_element_type=F32)


def iota(shape, dim):
    return lax.broadcasted_iota(jnp.int32, shape, dim)


def remote(src, dst, send_sem, recv_sem, req, ffn):
    return pltpu.make_async_remote_copy(
        src_ref=src, dst_ref=dst, send_sem=send_sem, recv_sem=recv_sem,
        device_id=(req, ffn), device_id_type=MESH,
    )


SCALE = HEAD_SIZE ** (-0.5)
MASKED = -1e30


def layer_kernel(
    q_hbm, k_hbm, v_hbm, start_hbm, sink_ref, wo_hbm, res_hbm, gain_hbm, logits_ref, routes_ref, placement_ref,
    wg_hbm, wu_hbm, wd_hbm,
    out_ref,
    kv, qb, qt, starts, peak, mass, acc, att_out, att_in,
    wo, res, gain, wg, wu, wd,
    proj_send, proj_recv, hid, stat_send, stat_recv,
    e_main, e_rem, g_main, g_rem,
    disp, rows, xbuf, act, part, hop_l, hop_r, from_l, from_r, fin, ret,
    kv_ssem, kv_rsem, half_ssem, half_rsem, loc_sem, wo_ssem, wo_rsem, ring_ssem, ring_rsem, pair_ssem, pair_rsem,
    att_ssem, att_rsem,
    in_sem, proj_ssem, proj_rsem, stat_ssem, stat_rsem,
    a2a_ssem, a2a_rsem, ag_ssem, ag_rsem, rs_ssem, rs_rsem, ret_ssem, ret_rsem, own_sem,
):
    r = lax.axis_index("req")
    y = lax.axis_index("ffn")
    z = r // 8
    x = lax.rem(r // 2, 4)
    c = lax.rem(r, 2)
    chip = r // 2
    mate = r + 1 - 2 * c
    yp, ym, y2 = lax.rem(y + 1, 4), lax.rem(y + 3, 4), lax.rem(y + 2, 4)
    peers = (yp, y2, ym)

    bar = pltpu.get_barrier_semaphore()

    near = [(lax.rem(r + 8, NREQ), y), (lax.rem(r + NREQ - 8, NREQ), y)]
    near += [(z * 8 + lax.rem(r + k, 8), y) for k in range(1, 8)]
    near += [(r, p) for p in peers]
    for device in near:
        pl.semaphore_signal(bar, inc=1, device_id=device, device_id_type=MESH)

    y_cols = pl.ds(pl.multiple_of(y * Q, Q), Q)
    loads = [
        pltpu.make_async_copy(res_hbm.at[:, y_cols], res, in_sem.at[0]),
        pltpu.make_async_copy(gain_hbm.at[:, y_cols], gain, in_sem.at[1]),
        pltpu.make_async_copy(wg_hbm, wg, in_sem.at[2]),
        pltpu.make_async_copy(wu_hbm, wu, in_sem.at[3]),
        pltpu.make_async_copy(wd_hbm, wd, in_sem.at[4]),
    ]
    for load in loads:
        load.start()

    def head(n):
        return pl.ds(pl.multiple_of(n * HEAD_SIZE, HEAD_SIZE), HEAD_SIZE)

    own_tok = pl.ds(pl.multiple_of(c * TOK, TOK), TOK)
    mate_tok = pl.ds(pl.multiple_of((1 - c) * TOK, TOK), TOK)
    for k in range(2):
        for i, ref in ((0, k_hbm), (1, v_hbm)):
            pltpu.make_async_copy(ref.at[:, head(2 * c + k)], kv.at[0, k, i, own_tok], loc_sem.at[k]).start()
    for k in range(2):
        for h in range(2):
            pltpu.make_async_copy(q_hbm.at[:, head(4 * c + 2 * k + h)], qb.at[k, h, own_tok], loc_sem.at[2]).start()
    pltpu.make_async_copy(start_hbm, starts.at[c], loc_sem.at[3]).start()
    pltpu.make_async_copy(wo_hbm.at[:, pl.ds(pl.multiple_of(c * 512, 512), 512)], wo.at[c, r], loc_sem.at[4]).start()

    pl.semaphore_wait(bar, len(near))

    mate_copies = []

    def to_mate(src, dst, n, sem):
        copy = remote(src, dst, half_ssem.at[n], sem, mate, y)
        copy.start()
        mate_copies.append(copy)

    for k in range(2):
        for i, ref in ((0, k_hbm), (1, v_hbm)):
            to_mate(ref.at[:, head(2 * (1 - c) + k)], kv.at[0, k, i, own_tok], 2 * k + i, half_rsem.at[k])
    for k in range(2):
        for h in range(2):
            to_mate(q_hbm.at[:, head(4 * (1 - c) + 2 * k + h)], qb.at[k, h, own_tok], 4 + 2 * k + h, half_rsem.at[2])
    to_mate(start_hbm, starts.at[c], 8, half_rsem.at[3])

    def chip_at(dz, dx):
        return lax.rem(z + dz, NZ) * 8 + lax.rem(x + dx, 4) * 2 + c

    def send(src, dst, k, dz, dx):
        remote(kv.at[src, k], kv.at[dst, k], kv_ssem.at[dst, k], kv_rsem.at[dst, k], chip_at(dz, dx), y).start()

    def took(slot, k):
        view = kv.at[slot, k]
        pltpu.make_async_copy(view, view, kv_rsem.at[slot, k]).wait()

    for k in range(2):
        view = kv.at[0, k, :, own_tok]
        pltpu.make_async_copy(view, view, loc_sem.at[k]).wait()
        view = kv.at[0, k, :, mate_tok]
        pltpu.make_async_copy(view, view, half_rsem.at[k]).wait()

    def only(columns, action):
        if len(columns) == 4:
            action()
        elif columns:
            hit = x == columns[0]
            for v in columns[1:]:
                hit = hit | (x == v)
            pl.when(hit)(action)

    waited = {(0, 0): set(ALL), (0, 1): set(ALL)}

    def need(slot, k, columns=ALL):
        done = waited.setdefault((slot, k), set())
        left = tuple(v for v in columns if v not in done)
        done.update(left)
        only(left, lambda: took(slot, k))

    def along_x(slot, dst, k, d, columns):
        need(slot, k, columns)
        only(columns, lambda: send(slot, dst, k, 0, d))

    wo_copies = []
    for h in range(2):
        half = pl.ds(h * 512, 512)
        for dx in range(4):
            target = z * 8 + lax.rem(x + dx, 4) * 2 + h

            def give(target=target, half=half, h=h):
                remote(wo_hbm.at[:, half], wo.at[h, r], wo_ssem.at[0], wo_rsem.at[0], target, y).start()

            if dx == 0:
                pl.when(c != h)(give)
            else:
                give()

    def ring(t, half):
        view = wo.at[c, pl.ds(lax.rem(z + t, NZ) * 8 + 4 * half, 4)]
        if t > 0:
            pltpu.make_async_copy(view, view, ring_rsem.at[t - 1, half]).wait()
        elif half == 0:
            few = wo.at[c, pl.ds(z * 8, 7)]
            pltpu.make_async_copy(few, few, wo_rsem.at[0]).wait()
            one = wo.at[c, r]
            pltpu.make_async_copy(one, one, loc_sem.at[4]).wait()
        if t < NZ - 1:
            copy = remote(view, view, ring_ssem.at[t, half], ring_rsem.at[t, half], chip_at(NZ - 1, 0), y)
            copy.start()
            wo_copies.append(copy)
        remote(view, view, pair_ssem, pair_rsem, mate, y).start()

    def heads():
        view = qb.at[:, :, own_tok]
        pltpu.make_async_copy(view, view, loc_sem.at[2]).wait()
        view = qb.at[:, :, mate_tok]
        pltpu.make_async_copy(view, view, half_rsem.at[2]).wait()
        for k in range(2):
            qt[k] = jnp.concatenate([qb[k, 0].T, qb[k, 1].T], axis=1)
            for h in range(2):
                peak[k, :, 512 * h:512 * h + 512] = jnp.full((1, 512), sink_ref[4 * c + 2 * k + h] * HEAD_SIZE ** 0.5, F32)
        mass[...] = jnp.ones_like(mass)
        acc[...] = jnp.zeros_like(acc)
        pltpu.make_async_copy(starts.at[c], starts.at[c], loc_sem.at[3]).wait()
        pltpu.make_async_copy(starts.at[1 - c], starts.at[1 - c], half_rsem.at[3]).wait()

    def attend(s, k):
        first = (chip - s) * 512
        scores = dot(kv[s, k, 0], qt[k])
        token = iota((1, 1024), 1) & 511
        both = jnp.concatenate([starts[0], starts[1]], axis=1)
        low = jnp.maximum(jnp.concatenate([both, both], axis=1) - first, token + (512 * s - 4095))
        key = iota((512, 1024), 0)
        seen = key >= low
        if s == 0:
            seen = seen & (key <= token)
        scores = jnp.where(seen, scores, MASKED)
        old = peak[k]
        new = jnp.maximum(old, jnp.max(scores, axis=0, keepdims=True))
        probs = jnp.exp((scores - new) * SCALE)
        alpha = jnp.exp((old - new) * SCALE)
        peak[k] = new
        mass[k] = mass[k] * alpha + jnp.sum(probs, axis=0, keepdims=True)
        acc[k] = acc[k] * alpha + dot_tn(kv[s, k, 1], probs.astype(BF))

    def tables():
        route0, route1 = routes_ref[0:1, :], routes_ref[1:2, :]
        dest = iota((NREQ, TOK), 0)
        hot0 = jnp.where(dest == route0, 1.0, 0.0)
        hot1 = jnp.where(dest == route1, 1.0, 0.0)
        before = jnp.where(iota((TOK, TOK), 0) < iota((TOK, TOK), 1), 1.0, 0.0).astype(BF)
        earlier = dot((hot0 + hot1).astype(BF), before)
        slot0 = route0.astype(F32) * 16.0 + jnp.sum(hot0 * earlier, axis=0, keepdims=True)
        slot1 = route1.astype(F32) * 16.0 + jnp.sum(hot1 * (earlier + hot0), axis=0, keepdims=True)
        line = iota((512, TOK), 0)
        main_id = ((line >> 3) * 16 + (line & 7)).astype(F32)
        rem_id = ((line >> 3) * 16 + 8 + (line & 1)).astype(F32)
        e_main[...] = jnp.where((main_id == slot0) | (main_id == slot1), 1.0, 0.0).astype(BF)
        e_rem[...] = jnp.where((rem_id == slot0) | (rem_id == slot1), 1.0, 0.0).astype(BF)
        hosts = jnp.where(iota((EXPERTS, NREQ), 0) == placement_ref[...], 1.0, 0.0).astype(BF)
        logits = logits_ref[...]
        pick0 = jnp.sum(logits * dot(hosts, hot0.astype(BF)), axis=0, keepdims=True)
        pick1 = jnp.sum(logits * dot(hosts, hot1.astype(BF)), axis=0, keepdims=True)
        top = jnp.maximum(pick0, pick1)
        exp0, exp1 = jnp.exp(pick0 - top), jnp.exp(pick1 - top)
        total = exp0 + exp1
        sub = iota((128, TOK), 0)
        packed = jnp.where(sub == 0, slot0, jnp.where(sub == 1, slot1, jnp.where(sub == 2, exp0 / total, exp1 / total)))
        turned = packed.T
        s0, s1, w0, w1 = turned[:, 0:1], turned[:, 1:2], turned[:, 2:3], turned[:, 3:4]
        col = iota((TOK, 512), 1)
        for ids, ref in (((col >> 3) * 16 + (col & 7), g_main), ((col >> 3) * 16 + 8 + (col & 1), g_rem)):
            ids = ids.astype(F32)
            gate = jnp.where(ids == s0, w0, 0.0) + jnp.where(ids == s1, w1, 0.0)
            high = gate.astype(BF)
            ref[0] = high
            ref[1] = (gate - high.astype(F32)).astype(BF)

    for name, *at in PLAN:
        if name == "heads":
            heads()
        elif name == "tables":
            tables()
        elif name == "R":
            ring(*at)
        elif name == "A":
            need(*at)
            attend(*at)
        elif name == "z4":
            send(0, 4, at[0], 1, 0)
        elif name == "z8":
            need(4, at[0])
            send(4, 8, at[0], 1, 0)
        elif name == "z6":
            need(2, at[0])
            send(2, 6, at[0], 1, 0)
        elif name == "f":
            along_x(1, 2, at[0], 1, (0, 2))
            along_x(3, 2, at[0], 3, (1, 3))
        else:
            d, k = at
            wrapped, second = int(name[1]), 4 * (name[2] == "b")
            columns = tuple(v for v in ALL if (v in WRAPS[d]) == bool(wrapped))
            along_x(4 * wrapped + second, d + second, k, d, columns)

    for k in range(2):
        out = acc[k] / mass[k]
        for h in range(2):
            block = out[:, 512 * h:512 * h + 512].astype(BF).T
            part_cols = slice(128 * (2 * k + h), 128 * (2 * k + h) + 128)
            att_out[0, :, part_cols] = block[0:TOK]
            att_out[1, :, part_cols] = block[TOK:2 * TOK]
    copy = remote(att_out.at[1 - c], att_in, att_ssem, att_rsem, mate, y)
    copy.start()
    mate_copies.append(copy)
    wo2 = wo.reshape(2, D, 512)
    pltpu.make_async_copy(wo.at[1 - c], wo.at[1 - c], pair_rsem).wait()
    pltpu.make_async_copy(att_in, att_in, att_rsem).wait()


    def project(which):
        f = pl.ds(pl.multiple_of(which * Q, Q), Q)
        return dot_nt(att_out[c], wo2[c, f, :]) + dot_nt(att_in[...], wo2[1 - c, f, :])

    proj_copies = []
    for i in (1, 0, 2):
        proj_send[i] = project(peers[i]).astype(BF)
        copy = remote(proj_send.at[i], proj_recv.at[2 - i], proj_ssem.at[i], proj_rsem.at[2 - i], r, peers[i])
        copy.start()
        proj_copies.append(copy)
    loads[0].wait()
    own = res[...].astype(F32) + project(y)
    for i in range(3):
        pltpu.make_async_copy(proj_recv.at[i], proj_recv.at[i], proj_rsem.at[i]).wait()
    hidden = own + proj_recv[0].astype(F32) + proj_recv[1].astype(F32) + proj_recv[2].astype(F32)
    hid[...] = hidden

    square = jnp.sum(hidden * hidden, axis=1, keepdims=True)
    stat_send[...] = jnp.broadcast_to(square, (TOK, 128)).T[0:8, :]
    stat_copies = []
    for i in range(3):
        copy = remote(stat_send, stat_recv.at[2 - i], stat_ssem.at[i], stat_rsem.at[2 - i], r, peers[i])
        copy.start()
        stat_copies.append(copy)
    loads[1].wait()
    for i in range(3):
        pltpu.make_async_copy(stat_recv.at[i], stat_recv.at[i], stat_rsem.at[i]).wait()
    squares = stat_send[...] + stat_recv[0] + stat_recv[1] + stat_recv[2]
    factor = lax.rsqrt(squares[0:1, :] * (1.0 / D) + EPS)
    factor = jnp.broadcast_to(factor, (128, TOK)).T[:, 0:1]
    normed = (hidden * factor * gain[...]).astype(BF)

    disp2 = disp.reshape(512, WIDE)
    disp2[:, 0:Q] = dot(e_main[...], normed).astype(BF)
    spread = dot(e_rem[...], normed)
    piece = (iota((512, 128), 0) & 7) >> 1

    def by_piece(parts):
        return jnp.where(piece == 0, parts[0], jnp.where(piece == 1, parts[1], jnp.where(piece == 2, parts[2], parts[3])))

    disp2[:, Q:WIDE] = by_piece([spread[:, 128 * k:128 * k + 128] for k in range(4)]).astype(BF)

    def exchange(source, target, send_sem, recv_sems, picks, ordered):
        for i in picks:
            g = lax.rem(z + Z_ORDER[i], NZ)
            base = i * 8 if ordered else g * 8

            def push(k, carry):
                m = lax.rem(r + k, 8)
                remote(source.at[base + m], target.at[r], send_sem, recv_sems.at[z], g * 8 + m, y).start()
                return carry

            lax.fori_loop(1 if i == 0 else 0, 8, push, 0)
            if i == 0:
                copy = pltpu.make_async_copy(source.at[base + lax.rem(r, 8)], target.at[r], own_sem)
                copy.start()
                copy.wait()

    def arrived(target, recv_sems, dz):
        g = lax.rem(z + dz, NZ)
        count = 7 if dz == 0 else 8
        view = target.at[pl.ds(g * 8, count)]
        pltpu.make_async_copy(view, view, recv_sems.at[g]).wait()

    mine = rows.at[y]
    exchange(disp, mine, a2a_ssem, a2a_rsem, range(8), False)

    ag_copies = []

    def forward(i):
        g = pl.ds(lax.rem(z + Z_ORDER[i], NZ) * 8, 8)
        here, there, side = (ym, yp, 0) if i % 2 == 0 else (yp, ym, 1)
        view = rows.at[here, g]
        pltpu.make_async_copy(view, view, ag_rsem.at[side, i]).wait()
        copy = remote(view, view, ag_ssem.at[2, i], ag_rsem.at[2, i], r, there)
        copy.start()
        ag_copies.append(copy)

    for i, dz in enumerate(Z_ORDER):
        arrived(mine, a2a_rsem, dz)
        g = pl.ds(lax.rem(z + dz, NZ) * 8, 8)
        view = rows.at[y, g]
        for side, there in ((0, yp), (1, ym)):
            copy = remote(view, view, ag_ssem.at[side, i], ag_rsem.at[side, i], r, there)
            copy.start()
            ag_copies.append(copy)
        if i > 0:
            forward(i - 1)

    def gathered(i):
        g = pl.ds(lax.rem(z + Z_ORDER[i], NZ) * 8, 8)
        here, side = (yp, 1) if i % 2 == 0 else (ym, 0)
        view = rows.at[here, g]
        pltpu.make_async_copy(view, view, ag_rsem.at[side, i]).wait()
        view = rows.at[y2, g]
        pltpu.make_async_copy(view, view, ag_rsem.at[2, i]).wait()

    rows2 = rows.reshape(4, 512, WIDE)
    part2 = part.reshape(4, 512, WIDE)
    fin2 = fin.reshape(512, WIDE)
    from_l2, from_r2 = from_l.reshape(512, WIDE), from_r.reshape(512, WIDE)
    hop_l2, hop_r2 = hop_l.reshape(PARTS, LINES // 2, WIDE), hop_r.reshape(PARTS, LINES // 2, WIDE)
    row_id, line_id = iota((TAIL, LINES), 0), iota((TAIL, LINES), 1)
    line_of, row_of = iota((LINES, LINES), 0), iota((LINES, LINES), 1)
    scatter = jnp.where(
        line_of == (row_of % TAIL >> 1) * 8 + 2 * (row_of // TAIL) + (row_of & 1), 1.0, 0.0
    ).astype(BF)
    rs = []

    def hidden_units(p):
        starts_at = [pl.multiple_of(lax.rem(z + Z_ORDER[SPAN * p + j], NZ) * 64, 64) for j in range(SPAN)]
        for q in range(4):
            for j in range(SPAN):
                xbuf[64 * j:64 * j + 64, Q * q:Q * q + Q] = rows2[q, pl.ds(starts_at[j], 64), 0:Q]
            tails = jnp.concatenate([rows2[q, pl.ds(at, 64), Q:WIDE] for at in starts_at], axis=0)
            for k in range(4):
                select = jnp.where(line_id == (row_id >> 1) * 8 + 2 * k + (row_id & 1), 1.0, 0.0).astype(BF)
                xbuf[LINES:LINES + TAIL, Q * q + 128 * k:Q * q + 128 * k + 128] = dot(select, tails).astype(BF)

        def inner(n, carry):
            cols = pl.ds(pl.multiple_of(n * 256, 256), 256)
            gate = dot(xbuf[...], wg[:, cols])
            up = dot(xbuf[...], wu[:, cols])
            act[:, cols] = (gate / (1.0 + jnp.exp(-gate)) * up).astype(BF)
            return carry

        lax.fori_loop(0, HID // 256, inner, 0)

    def reduce_send(p, n, src, dst, device):
        copy = remote(src, dst, rs_ssem.at[p, n], rs_rsem.at[p, n], r, device)
        copy.start()
        rs.append(copy)

    def outputs(p):
        low, high = pl.ds(8 * SPAN * p, 4 * SPAN), pl.ds(8 * SPAN * p + 4 * SPAN, 4 * SPAN)
        for j, which in enumerate((y2, yp, ym, y)):
            piece_out = dot_nt(act[...], wd[pl.ds(pl.multiple_of(which * Q, Q), Q), :])
            part2[j, LINES * p:LINES * p + LINES, 0:Q] = piece_out[0:LINES].astype(BF)
            tail = piece_out[LINES:LINES + TAIL].astype(BF)
            stacked = jnp.concatenate([tail[:, 128 * k:128 * k + 128] for k in range(4)], axis=0)
            part2[j, LINES * p:LINES * p + LINES, Q:WIDE] = dot(scatter, stacked).astype(BF)
            if j == 0:
                reduce_send(p, 0, part.at[0, low], hop_l.at[p], yp)
                reduce_send(p, 1, part.at[0, high], hop_r.at[p], ym)
            if j == 1:
                reduce_send(p, 2, part.at[1, high], from_l.at[high], yp)
            if j == 2:
                reduce_send(p, 3, part.at[2, low], from_r.at[low], ym)

    def hop(p):
        low, high = pl.ds(8 * SPAN * p, 4 * SPAN), pl.ds(8 * SPAN * p + 4 * SPAN, 4 * SPAN)
        middle = LINES * p + LINES // 2
        low2, high2 = slice(LINES * p, middle), slice(middle, LINES * p + LINES)
        pltpu.make_async_copy(hop_l.at[p], hop_l.at[p], rs_rsem.at[p, 0]).wait()
        part2[1, low2, :] = (part2[1, low2, :].astype(F32) + hop_l2[p].astype(F32)).astype(BF)
        reduce_send(p, 4, part.at[1, low], from_l.at[low], yp)
        pltpu.make_async_copy(hop_r.at[p], hop_r.at[p], rs_rsem.at[p, 1]).wait()
        part2[2, high2, :] = (part2[2, high2, :].astype(F32) + hop_r2[p].astype(F32)).astype(BF)
        reduce_send(p, 5, part.at[2, high], from_r.at[high], ym)

    def give_back(p):
        low, high = pl.ds(8 * SPAN * p, 4 * SPAN), pl.ds(8 * SPAN * p + 4 * SPAN, 4 * SPAN)
        for ref, half, k in ((from_l, high, 2), (from_r, low, 3), (from_l, low, 4), (from_r, high, 5)):
            view = ref.at[half]
            pltpu.make_async_copy(view, view, rs_rsem.at[p, k]).wait()
        at = slice(LINES * p, LINES * p + LINES)
        total_out = part2[3, at, :].astype(F32) + from_l2[at, :].astype(F32) + from_r2[at, :].astype(F32)
        fin2[at, :] = total_out.astype(BF)
        exchange(fin, ret, ret_ssem, ret_rsem, range(SPAN * p, SPAN * p + SPAN), True)

    for p in range(PARTS):
        for i in range(SPAN * p, SPAN * p + SPAN):
            gathered(i)
        if p == 0:
            loads[2].wait()
            loads[3].wait()
        hidden_units(p)
        if p == 0:
            forward(7)
            loads[4].wait()
        if p > 0:
            hop(p - 1)
        if p > 1:
            give_back(p - 2)
        outputs(p)
    give_back(PARTS - 2)
    hop(PARTS - 1)
    give_back(PARTS - 1)
    for dz in Z_ORDER:
        arrived(ret, ret_rsem, dz)
    ret2 = ret.reshape(512, WIDE)
    back = ret2[:, 0:Q]
    lines = ret2[:, Q:WIDE]
    masked = jnp.concatenate([jnp.where(piece == k, lines.astype(F32), 0.0).astype(BF) for k in range(4)], axis=1)
    mixture = dot(g_main[0], back) + dot(g_main[1], back) + dot(g_rem[0], masked) + dot(g_rem[1], masked)
    out_ref[...] = (hid[...] + mixture).astype(BF)

    for copy in mate_copies + wo_copies + proj_copies + stat_copies + ag_copies + rs:
        copy.wait_send()
    few = wo.at[0, pl.ds(0, 7)]
    pltpu.make_async_copy(few, few, wo_ssem.at[0]).wait()
    pltpu.make_async_copy(wo.at[c], wo.at[c], pair_ssem).wait()
    for sem, ref in ((a2a_ssem, disp), (ret_ssem, fin)):
        view = ref.at[pl.ds(0, NREQ - 1)]
        pltpu.make_async_copy(view, view, sem).wait()
    for s in range(1, 9):
        for k in range(2):
            view = kv.at[s, k]
            pltpu.make_async_copy(view, view, kv_ssem.at[s, k]).wait()


def layer_call(*args):
    vmem = pl.BlockSpec(memory_space=pltpu.VMEM)
    smem = pl.BlockSpec(memory_space=pltpu.SMEM)
    hbm = pl.BlockSpec(memory_space=pl.ANY)
    dma = pltpu.SemaphoreType.DMA
    chunk = (NREQ, 8, WIDE)
    return pl.pallas_call(
        layer_kernel,
        out_shape=jax.ShapeDtypeStruct((TOK, Q), BF),
        in_specs=[hbm, hbm, hbm, hbm, smem, hbm, hbm, hbm, vmem, vmem, vmem, hbm, hbm, hbm],
        out_specs=vmem,
        scratch_shapes=[
            pltpu.VMEM((9, 2, 2, 512, HEAD_SIZE), BF), pltpu.VMEM((2, 2, 512, HEAD_SIZE), BF),
            pltpu.VMEM((2, HEAD_SIZE, 1024), BF), pltpu.VMEM((2, 1, TOK), jnp.int32),
            pltpu.VMEM((2, 1, 1024), F32), pltpu.VMEM((2, 1, 1024), F32), pltpu.VMEM((2, HEAD_SIZE, 1024), F32),
            pltpu.VMEM((2, TOK, 512), BF), pltpu.VMEM((TOK, 512), BF),
            pltpu.VMEM((2, NREQ, 32, 512), BF), pltpu.VMEM((TOK, Q), BF), pltpu.VMEM((1, Q), F32),
            pltpu.VMEM((D, HID), BF), pltpu.VMEM((D, HID), BF), pltpu.VMEM((D, HID), BF),
            pltpu.VMEM((3, TOK, Q), BF), pltpu.VMEM((3, TOK, Q), BF), pltpu.VMEM((TOK, Q), F32),
            pltpu.VMEM((8, TOK), F32), pltpu.VMEM((3, 8, TOK), F32),
            pltpu.VMEM((512, TOK), BF), pltpu.VMEM((512, TOK), BF),
            pltpu.VMEM((2, TOK, 512), BF), pltpu.VMEM((2, TOK, 512), BF),
            pltpu.VMEM(chunk, BF), pltpu.VMEM((4,) + chunk, BF), pltpu.VMEM((LINES + TAIL, D), BF), pltpu.VMEM((LINES + TAIL, HID), BF),
            pltpu.VMEM((4,) + chunk, BF), pltpu.VMEM((PARTS, 4 * SPAN, 8, WIDE), BF), pltpu.VMEM((PARTS, 4 * SPAN, 8, WIDE), BF),
            pltpu.VMEM(chunk, BF), pltpu.VMEM(chunk, BF), pltpu.VMEM(chunk, BF), pltpu.VMEM(chunk, BF),
            dma((9, 2)), dma((9, 2)), dma((9,)), dma((4,)), dma((5,)), dma((1,)), dma((1,)), dma((7, 2)), dma((7, 2)),
            dma, dma, dma, dma,
            dma((5,)), dma((3,)), dma((3,)), dma((3,)), dma((3,)),
            dma, dma((8,)), dma((3, 8)), dma((3, 8)), dma((PARTS, 6)), dma((PARTS, 6)), dma, dma((8,)), dma,
        ],
        compiler_params=pltpu.CompilerParams(
            collective_id=1, has_side_effects=True, vmem_limit_bytes=60 << 20
        ),
        name="layer",
    )(*args)


def per_device(
    residual, queries, rotated_key_rows, values, req_start, head_sink_logit, out_proj, mid_gain,
    router_logits, routes, placement, w_gate, w_up, w_down,
):
    return layer_call(
        queries, rotated_key_rows, values, req_start.reshape(1, TOK), head_sink_logit, out_proj.T, residual,
        mid_gain.reshape(1, D), router_logits.T, routes.T, placement.reshape(1, NREQ), w_gate[0], w_up[0], w_down[0],
    )


def solution(mesh):
    in_specs = (
        P("req", None),
        P("req", "ffn"),
        P("req", "ffn"),
        P("req", "ffn"),
        P("req"),
        P("ffn"),
        P("ffn", "req"),
        P(),
        P("req", None),
        P("req", None),
        P(),
        P("req", None, "ffn"),
        P("req", None, "ffn"),
        P("req", None, "ffn"),
    )
    out_specs = P("req", "ffn")
    return jax.shard_map(
        per_device, mesh=mesh, in_specs=in_specs, out_specs=out_specs, check_vma=False
    )
```

```python
import jax
import jax.numpy as jnp
from jax import lax
from jax.experimental import pallas as pl
from jax.experimental.pallas import tpu as pltpu
from jax.sharding import PartitionSpec as P

QUERY_HEADS = 32
KEY_VALUE_HEADS = 16
HEAD_SIZE = 128
EXPERTS = 8
EPS = 1e-06
MESH = pl.DeviceIdType.MESH
BF = jnp.bfloat16
F32 = jnp.float32

NREQ = 64
NFFN = 4
NZ = 8
TOK = 256
D = 2048
Q = D // NFFN
HID = 768
WIDE = Q + 128
PARTS = 4
SPAN = 8 // PARTS
LINES = 64 * SPAN
TAIL = 16 * SPAN
Z_ORDER = (0, 1, 7, 2, 6, 3, 5, 4)
PLAN = (
    ("z4", 0), ("w0a", 1, 0), ("w0a", 3, 0), ("R", 0, 0), ("R", 0, 1), ("R", 1, 0), ("z4", 1), ("w1a", 1, 0),
    ("w1a", 3, 0), ("w0a", 3, 1), ("w0a", 1, 1), ("R", 1, 1), ("w1a", 3, 1), ("z8", 1), ("w0b", 1, 1),
    ("R", 2, 1), ("w1a", 1, 1), ("heads",), ("R", 2, 0), ("A", 4, 1), ("f", 0), ("z8", 0), ("R", 3, 1),
    ("A", 0, 1), ("R", 3, 0), ("tables",), ("A", 1, 0), ("w1b", 1, 1), ("w0b", 3, 0), ("R", 4, 1), ("f", 1),
    ("A", 4, 0), ("A", 8, 0), ("R", 4, 0), ("A", 3, 1), ("w0b", 1, 0), ("z6", 0), ("w0b", 3, 1), ("w1b", 3, 0),
    ("A", 2, 0), ("R", 5, 1), ("A", 0, 0), ("w1b", 1, 0), ("A", 5, 1), ("A", 8, 1), ("w1b", 3, 1), ("R", 5, 0),
    ("z6", 1), ("A", 1, 1), ("A", 3, 0), ("R", 6, 1), ("A", 6, 0), ("A", 2, 1), ("R", 6, 0), ("A", 5, 0),
    ("A", 7, 0), ("A", 6, 1), ("A", 7, 1), ("R", 7, 0), ("R", 7, 1),
)
ALL = (0, 1, 2, 3)
WRAPS = {1: (3,), 3: (1, 2, 3)}


def dot(a, b):
    return jnp.dot(a, b, preferred_element_type=F32)


def dot_nt(a, b):
    return lax.dot_general(a, b, (((1,), (1,)), ((), ())), preferred_element_type=F32)


def dot_tn(a, b):
    return lax.dot_general(a, b, (((0,), (0,)), ((), ())), preferred_element_type=F32)


def iota(shape, dim):
    return lax.broadcasted_iota(jnp.int32, shape, dim)


def remote(src, dst, send_sem, recv_sem, req, ffn):
    return pltpu.make_async_remote_copy(
        src_ref=src, dst_ref=dst, send_sem=send_sem, recv_sem=recv_sem,
        device_id=(req, ffn), device_id_type=MESH,
    )


SCALE = HEAD_SIZE ** (-0.5)
MASKED = -1e30


def layer_kernel(
    q_hbm, k_hbm, v_hbm, start_hbm, sink_ref, wo_hbm, res_hbm, gain_hbm, logits_ref, routes_ref, placement_ref,
    wg_hbm, wu_hbm, wd_hbm,
    out_ref,
    kv, qb, qt, starts, peak, mass, acc, att_out, att_in,
    wo, res, gain, wg, wu, wd,
    proj_send, proj_recv, hid, stat_send, stat_recv,
    e_main, e_rem, g_main, g_rem,
    disp, rows, xbuf, act, part, hop_l, hop_r, from_l, from_r, fin, ret,
    kv_ssem, kv_rsem, half_ssem, half_rsem, loc_sem, wo_ssem, wo_rsem, ring_ssem, ring_rsem, pair_ssem, pair_rsem,
    att_ssem, att_rsem,
    in_sem, proj_ssem, proj_rsem, stat_ssem, stat_rsem,
    a2a_ssem, a2a_rsem, ag_ssem, ag_rsem, rs_ssem, rs_rsem, ret_ssem, ret_rsem, own_sem,
):
    r = lax.axis_index("req")
    y = lax.axis_index("ffn")
    z = r // 8
    x = lax.rem(r // 2, 4)
    c = lax.rem(r, 2)
    chip = r // 2
    mate = r + 1 - 2 * c
    yp, ym, y2 = lax.rem(y + 1, 4), lax.rem(y + 3, 4), lax.rem(y + 2, 4)
    peers = (yp, y2, ym)

    bar = pltpu.get_barrier_semaphore()

    near = [(lax.rem(r + 8, NREQ), y), (lax.rem(r + NREQ - 8, NREQ), y)]
    near += [(z * 8 + lax.rem(r + k, 8), y) for k in range(1, 8)]
    near += [(r, p) for p in peers]
    for device in near:
        pl.semaphore_signal(bar, inc=1, device_id=device, device_id_type=MESH)

    y_cols = pl.ds(pl.multiple_of(y * Q, Q), Q)
    loads = [
        pltpu.make_async_copy(res_hbm.at[:, y_cols], res, in_sem.at[0]),
        pltpu.make_async_copy(gain_hbm.at[:, y_cols], gain, in_sem.at[1]),
        pltpu.make_async_copy(wg_hbm, wg, in_sem.at[2]),
        pltpu.make_async_copy(wu_hbm, wu, in_sem.at[3]),
        pltpu.make_async_copy(wd_hbm, wd, in_sem.at[4]),
    ]
    for load in loads:
        load.start()

    def head(n):
        return pl.ds(pl.multiple_of(n * HEAD_SIZE, HEAD_SIZE), HEAD_SIZE)

    own_tok = pl.ds(pl.multiple_of(c * TOK, TOK), TOK)
    mate_tok = pl.ds(pl.multiple_of((1 - c) * TOK, TOK), TOK)
    for k in range(2):
        for i, ref in ((0, k_hbm), (1, v_hbm)):
            pltpu.make_async_copy(ref.at[:, head(2 * c + k)], kv.at[0, k, i, own_tok], loc_sem.at[k]).start()
    for k in range(2):
        for h in range(2):
            pltpu.make_async_copy(q_hbm.at[:, head(4 * c + 2 * k + h)], qb.at[k, h, own_tok], loc_sem.at[2]).start()
    pltpu.make_async_copy(start_hbm, starts.at[c], loc_sem.at[3]).start()
    pltpu.make_async_copy(wo_hbm.at[:, pl.ds(pl.multiple_of(c * 512, 512), 512)], wo.at[c, r], loc_sem.at[4]).start()

    pl.semaphore_wait(bar, len(near))

    mate_copies = []

    def to_mate(src, dst, n, sem):
        copy = remote(src, dst, half_ssem.at[n], sem, mate, y)
        copy.start()
        mate_copies.append(copy)

    for k in range(2):
        for i, ref in ((0, k_hbm), (1, v_hbm)):
            to_mate(ref.at[:, head(2 * (1 - c) + k)], kv.at[0, k, i, own_tok], 2 * k + i, half_rsem.at[k])
    for k in range(2):
        for h in range(2):
            to_mate(q_hbm.at[:, head(4 * (1 - c) + 2 * k + h)], qb.at[k, h, own_tok], 4 + 2 * k + h, half_rsem.at[2])
    to_mate(start_hbm, starts.at[c], 8, half_rsem.at[3])

    def chip_at(dz, dx):
        return lax.rem(z + dz, NZ) * 8 + lax.rem(x + dx, 4) * 2 + c

    def send(src, dst, k, dz, dx):
        remote(kv.at[src, k], kv.at[dst, k], kv_ssem.at[dst, k], kv_rsem.at[dst, k], chip_at(dz, dx), y).start()

    def took(slot, k):
        view = kv.at[slot, k]
        pltpu.make_async_copy(view, view, kv_rsem.at[slot, k]).wait()

    for k in range(2):
        view = kv.at[0, k, :, own_tok]
        pltpu.make_async_copy(view, view, loc_sem.at[k]).wait()
        view = kv.at[0, k, :, mate_tok]
        pltpu.make_async_copy(view, view, half_rsem.at[k]).wait()

    def only(columns, action):
        if len(columns) == 4:
            action()
        elif columns:
            hit = x == columns[0]
            for v in columns[1:]:
                hit = hit | (x == v)
            pl.when(hit)(action)

    waited = {(0, 0): set(ALL), (0, 1): set(ALL)}

    def need(slot, k, columns=ALL):
        done = waited.setdefault((slot, k), set())
        left = tuple(v for v in columns if v not in done)
        done.update(left)
        only(left, lambda: took(slot, k))

    def along_x(slot, dst, k, d, columns):
        need(slot, k, columns)
        only(columns, lambda: send(slot, dst, k, 0, d))

    wo_copies = []
    for h in range(2):
        half = pl.ds(h * 512, 512)
        for dx in range(4):
            target = z * 8 + lax.rem(x + dx, 4) * 2 + h

            def give(target=target, half=half, h=h):
                remote(wo_hbm.at[:, half], wo.at[h, r], wo_ssem.at[0], wo_rsem.at[0], target, y).start()

            if dx == 0:
                pl.when(c != h)(give)
            else:
                give()

    def ring(t, half):
        view = wo.at[c, pl.ds(lax.rem(z + t, NZ) * 8 + 4 * half, 4)]
        if t > 0:
            pltpu.make_async_copy(view, view, ring_rsem.at[t - 1, half]).wait()
        elif half == 0:
            few = wo.at[c, pl.ds(z * 8, 7)]
            pltpu.make_async_copy(few, few, wo_rsem.at[0]).wait()
            one = wo.at[c, r]
            pltpu.make_async_copy(one, one, loc_sem.at[4]).wait()
        if t < NZ - 1:
            copy = remote(view, view, ring_ssem.at[t, half], ring_rsem.at[t, half], chip_at(NZ - 1, 0), y)
            copy.start()
            wo_copies.append(copy)
        remote(view, view, pair_ssem, pair_rsem, mate, y).start()

    def heads():
        view = qb.at[:, :, own_tok]
        pltpu.make_async_copy(view, view, loc_sem.at[2]).wait()
        view = qb.at[:, :, mate_tok]
        pltpu.make_async_copy(view, view, half_rsem.at[2]).wait()
        for k in range(2):
            qt[k] = jnp.concatenate([qb[k, 0].T, qb[k, 1].T], axis=1)
            for h in range(2):
                peak[k, :, 512 * h:512 * h + 512] = jnp.full((1, 512), sink_ref[4 * c + 2 * k + h] * HEAD_SIZE ** 0.5, F32)
        mass[...] = jnp.ones_like(mass)
        acc[...] = jnp.zeros_like(acc)
        pltpu.make_async_copy(starts.at[c], starts.at[c], loc_sem.at[3]).wait()
        pltpu.make_async_copy(starts.at[1 - c], starts.at[1 - c], half_rsem.at[3]).wait()

    def attend(s, k):
        first = (chip - s) * 512
        scores = dot(kv[s, k, 0], qt[k])
        token = iota((1, 1024), 1) & 511
        both = jnp.concatenate([starts[0], starts[1]], axis=1)
        low = jnp.maximum(jnp.concatenate([both, both], axis=1) - first, token + (512 * s - 4095))
        key = iota((512, 1024), 0)
        seen = key >= low
        if s == 0:
            seen = seen & (key <= token)
        scores = jnp.where(seen, scores, MASKED)
        old = peak[k]
        new = jnp.maximum(old, jnp.max(scores, axis=0, keepdims=True))
        probs = jnp.exp((scores - new) * SCALE)
        alpha = jnp.exp((old - new) * SCALE)
        peak[k] = new
        mass[k] = mass[k] * alpha + jnp.sum(probs, axis=0, keepdims=True)
        acc[k] = acc[k] * alpha + dot_tn(kv[s, k, 1], probs.astype(BF))

    def tables():
        route0, route1 = routes_ref[0:1, :], routes_ref[1:2, :]
        dest = iota((NREQ, TOK), 0)
        hot0 = jnp.where(dest == route0, 1.0, 0.0)
        hot1 = jnp.where(dest == route1, 1.0, 0.0)
        before = jnp.where(iota((TOK, TOK), 0) < iota((TOK, TOK), 1), 1.0, 0.0).astype(BF)
        earlier = dot((hot0 + hot1).astype(BF), before)
        slot0 = route0.astype(F32) * 16.0 + jnp.sum(hot0 * earlier, axis=0, keepdims=True)
        slot1 = route1.astype(F32) * 16.0 + jnp.sum(hot1 * (earlier + hot0), axis=0, keepdims=True)
        line = iota((512, TOK), 0)
        main_id = ((line >> 3) * 16 + (line & 7)).astype(F32)
        rem_id = ((line >> 3) * 16 + 8 + (line & 1)).astype(F32)
        e_main[...] = jnp.where((main_id == slot0) | (main_id == slot1), 1.0, 0.0).astype(BF)
        e_rem[...] = jnp.where((rem_id == slot0) | (rem_id == slot1), 1.0, 0.0).astype(BF)
        hosts = jnp.where(iota((EXPERTS, NREQ), 0) == placement_ref[...], 1.0, 0.0).astype(BF)
        logits = logits_ref[...]
        pick0 = jnp.sum(logits * dot(hosts, hot0.astype(BF)), axis=0, keepdims=True)
        pick1 = jnp.sum(logits * dot(hosts, hot1.astype(BF)), axis=0, keepdims=True)
        top = jnp.maximum(pick0, pick1)
        exp0, exp1 = jnp.exp(pick0 - top), jnp.exp(pick1 - top)
        total = exp0 + exp1
        sub = iota((128, TOK), 0)
        packed = jnp.where(sub == 0, slot0, jnp.where(sub == 1, slot1, jnp.where(sub == 2, exp0 / total, exp1 / total)))
        turned = packed.T
        s0, s1, w0, w1 = turned[:, 0:1], turned[:, 1:2], turned[:, 2:3], turned[:, 3:4]
        col = iota((TOK, 512), 1)
        for ids, ref in (((col >> 3) * 16 + (col & 7), g_main), ((col >> 3) * 16 + 8 + (col & 1), g_rem)):
            ids = ids.astype(F32)
            gate = jnp.where(ids == s0, w0, 0.0) + jnp.where(ids == s1, w1, 0.0)
            high = gate.astype(BF)
            ref[0] = high
            ref[1] = (gate - high.astype(F32)).astype(BF)

    for name, *at in PLAN:
        if name == "heads":
            heads()
        elif name == "tables":
            tables()
        elif name == "R":
            ring(*at)
        elif name == "A":
            need(*at)
            attend(*at)
        elif name == "z4":
            send(0, 4, at[0], 1, 0)
        elif name == "z8":
            need(4, at[0])
            send(4, 8, at[0], 1, 0)
        elif name == "z6":
            need(2, at[0])
            send(2, 6, at[0], 1, 0)
        elif name == "f":
            along_x(1, 2, at[0], 1, (0, 2))
            along_x(3, 2, at[0], 3, (1, 3))
        else:
            d, k = at
            wrapped, second = int(name[1]), 4 * (name[2] == "b")
            columns = tuple(v for v in ALL if (v in WRAPS[d]) == bool(wrapped))
            along_x(4 * wrapped + second, d + second, k, d, columns)

    for k in range(2):
        out = acc[k] / mass[k]
        for h in range(2):
            block = out[:, 512 * h:512 * h + 512].astype(BF).T
            part_cols = slice(128 * (2 * k + h), 128 * (2 * k + h) + 128)
            att_out[0, :, part_cols] = block[0:TOK]
            att_out[1, :, part_cols] = block[TOK:2 * TOK]
    copy = remote(att_out.at[1 - c], att_in, att_ssem, att_rsem, mate, y)
    copy.start()
    mate_copies.append(copy)
    wo2 = wo.reshape(2, D, 512)
    pltpu.make_async_copy(wo.at[1 - c], wo.at[1 - c], pair_rsem).wait()
    pltpu.make_async_copy(att_in, att_in, att_rsem).wait()


    def project(which):
        f = pl.ds(pl.multiple_of(which * Q, Q), Q)
        return dot_nt(att_out[c], wo2[c, f, :]) + dot_nt(att_in[...], wo2[1 - c, f, :])

    proj_copies = []
    for i in (1, 0, 2):
        proj_send[i] = project(peers[i]).astype(BF)
        copy = remote(proj_send.at[i], proj_recv.at[2 - i], proj_ssem.at[i], proj_rsem.at[2 - i], r, peers[i])
        copy.start()
        proj_copies.append(copy)
    loads[0].wait()
    own = res[...].astype(F32) + project(y)
    for i in range(3):
        pltpu.make_async_copy(proj_recv.at[i], proj_recv.at[i], proj_rsem.at[i]).wait()
    hidden = own + proj_recv[0].astype(F32) + proj_recv[1].astype(F32) + proj_recv[2].astype(F32)
    hid[...] = hidden

    square = jnp.sum(hidden * hidden, axis=1, keepdims=True)
    stat_send[...] = jnp.broadcast_to(square, (TOK, 128)).T[0:8, :]
    stat_copies = []
    for i in range(3):
        copy = remote(stat_send, stat_recv.at[2 - i], stat_ssem.at[i], stat_rsem.at[2 - i], r, peers[i])
        copy.start()
        stat_copies.append(copy)
    loads[1].wait()
    for i in range(3):
        pltpu.make_async_copy(stat_recv.at[i], stat_recv.at[i], stat_rsem.at[i]).wait()
    squares = stat_send[...] + stat_recv[0] + stat_recv[1] + stat_recv[2]
    factor = lax.rsqrt(squares[0:1, :] * (1.0 / D) + EPS)
    factor = jnp.broadcast_to(factor, (128, TOK)).T[:, 0:1]
    normed = (hidden * factor * gain[...]).astype(BF)

    disp2 = disp.reshape(512, WIDE)
    disp2[:, 0:Q] = dot(e_main[...], normed).astype(BF)
    spread = dot(e_rem[...], normed)
    piece = (iota((512, 128), 0) & 7) >> 1

    def by_piece(parts):
        return jnp.where(piece == 0, parts[0], jnp.where(piece == 1, parts[1], jnp.where(piece == 2, parts[2], parts[3])))

    disp2[:, Q:WIDE] = by_piece([spread[:, 128 * k:128 * k + 128] for k in range(4)]).astype(BF)

    def exchange(source, target, send_sem, recv_sems, picks, ordered):
        for i in picks:
            g = lax.rem(z + Z_ORDER[i], NZ)
            base = i * 8 if ordered else g * 8

            def push(k, carry):
                m = lax.rem(r + k, 8)
                remote(source.at[base + m], target.at[r], send_sem, recv_sems.at[z], g * 8 + m, y).start()
                return carry

            lax.fori_loop(1 if i == 0 else 0, 8, push, 0)
            if i == 0:
                copy = pltpu.make_async_copy(source.at[base + lax.rem(r, 8)], target.at[r], own_sem)
                copy.start()
                copy.wait()

    def arrived(target, recv_sems, dz):
        g = lax.rem(z + dz, NZ)
        count = 7 if dz == 0 else 8
        view = target.at[pl.ds(g * 8, count)]
        pltpu.make_async_copy(view, view, recv_sems.at[g]).wait()

    mine = rows.at[y]
    exchange(disp, mine, a2a_ssem, a2a_rsem, range(8), False)

    ag_copies = []

    def forward(i):
        g = pl.ds(lax.rem(z + Z_ORDER[i], NZ) * 8, 8)
        here, there, side = (ym, yp, 0) if i % 2 == 0 else (yp, ym, 1)
        view = rows.at[here, g]
        pltpu.make_async_copy(view, view, ag_rsem.at[side, i]).wait()
        copy = remote(view, view, ag_ssem.at[2, i], ag_rsem.at[2, i], r, there)
        copy.start()
        ag_copies.append(copy)

    for i, dz in enumerate(Z_ORDER):
        arrived(mine, a2a_rsem, dz)
        g = pl.ds(lax.rem(z + dz, NZ) * 8, 8)
        view = rows.at[y, g]
        for side, there in ((0, yp), (1, ym)):
            copy = remote(view, view, ag_ssem.at[side, i], ag_rsem.at[side, i], r, there)
            copy.start()
            ag_copies.append(copy)
        if i > 0:
            forward(i - 1)

    def gathered(i):
        g = pl.ds(lax.rem(z + Z_ORDER[i], NZ) * 8, 8)
        here, side = (yp, 1) if i % 2 == 0 else (ym, 0)
        view = rows.at[here, g]
        pltpu.make_async_copy(view, view, ag_rsem.at[side, i]).wait()
        view = rows.at[y2, g]
        pltpu.make_async_copy(view, view, ag_rsem.at[2, i]).wait()

    rows2 = rows.reshape(4, 512, WIDE)
    part2 = part.reshape(4, 512, WIDE)
    fin2 = fin.reshape(512, WIDE)
    from_l2, from_r2 = from_l.reshape(512, WIDE), from_r.reshape(512, WIDE)
    hop_l2, hop_r2 = hop_l.reshape(PARTS, LINES // 2, WIDE), hop_r.reshape(PARTS, LINES // 2, WIDE)
    row_id, line_id = iota((TAIL, LINES), 0), iota((TAIL, LINES), 1)
    line_of, row_of = iota((LINES, LINES), 0), iota((LINES, LINES), 1)
    scatter = jnp.where(
        line_of == (row_of % TAIL >> 1) * 8 + 2 * (row_of // TAIL) + (row_of & 1), 1.0, 0.0
    ).astype(BF)
    rs = []

    def hidden_units(p):
        starts_at = [pl.multiple_of(lax.rem(z + Z_ORDER[SPAN * p + j], NZ) * 64, 64) for j in range(SPAN)]
        for q in range(4):
            for j in range(SPAN):
                xbuf[64 * j:64 * j + 64, Q * q:Q * q + Q] = rows2[q, pl.ds(starts_at[j], 64), 0:Q]
            tails = jnp.concatenate([rows2[q, pl.ds(at, 64), Q:WIDE] for at in starts_at], axis=0)
            for k in range(4):
                select = jnp.where(line_id == (row_id >> 1) * 8 + 2 * k + (row_id & 1), 1.0, 0.0).astype(BF)
                xbuf[LINES:LINES + TAIL, Q * q + 128 * k:Q * q + 128 * k + 128] = dot(select, tails).astype(BF)

        def inner(n, carry):
            cols = pl.ds(pl.multiple_of(n * 256, 256), 256)
            gate = dot(xbuf[...], wg[:, cols])
            up = dot(xbuf[...], wu[:, cols])
            act[:, cols] = (gate / (1.0 + jnp.exp(-gate)) * up).astype(BF)
            return carry

        lax.fori_loop(0, HID // 256, inner, 0)

    def reduce_send(p, n, src, dst, device):
        copy = remote(src, dst, rs_ssem.at[p, n], rs_rsem.at[p, n], r, device)
        copy.start()
        rs.append(copy)

    def outputs(p):
        low, high = pl.ds(8 * SPAN * p, 4 * SPAN), pl.ds(8 * SPAN * p + 4 * SPAN, 4 * SPAN)
        for j, which in enumerate((y2, yp, ym, y)):
            piece_out = dot_nt(act[...], wd[pl.ds(pl.multiple_of(which * Q, Q), Q), :])
            part2[j, LINES * p:LINES * p + LINES, 0:Q] = piece_out[0:LINES].astype(BF)
            tail = piece_out[LINES:LINES + TAIL].astype(BF)
            stacked = jnp.concatenate([tail[:, 128 * k:128 * k + 128] for k in range(4)], axis=0)
            part2[j, LINES * p:LINES * p + LINES, Q:WIDE] = dot(scatter, stacked).astype(BF)
            if j == 0:
                reduce_send(p, 0, part.at[0, low], hop_l.at[p], yp)
                reduce_send(p, 1, part.at[0, high], hop_r.at[p], ym)
            if j == 1:
                reduce_send(p, 2, part.at[1, high], from_l.at[high], yp)
            if j == 2:
                reduce_send(p, 3, part.at[2, low], from_r.at[low], ym)

    def hop(p):
        low, high = pl.ds(8 * SPAN * p, 4 * SPAN), pl.ds(8 * SPAN * p + 4 * SPAN, 4 * SPAN)
        middle = LINES * p + LINES // 2
        low2, high2 = slice(LINES * p, middle), slice(middle, LINES * p + LINES)
        pltpu.make_async_copy(hop_l.at[p], hop_l.at[p], rs_rsem.at[p, 0]).wait()
        part2[1, low2, :] = (part2[1, low2, :].astype(F32) + hop_l2[p].astype(F32)).astype(BF)
        reduce_send(p, 4, part.at[1, low], from_l.at[low], yp)
        pltpu.make_async_copy(hop_r.at[p], hop_r.at[p], rs_rsem.at[p, 1]).wait()
        part2[2, high2, :] = (part2[2, high2, :].astype(F32) + hop_r2[p].astype(F32)).astype(BF)
        reduce_send(p, 5, part.at[2, high], from_r.at[high], ym)

    def give_back(p):
        low, high = pl.ds(8 * SPAN * p, 4 * SPAN), pl.ds(8 * SPAN * p + 4 * SPAN, 4 * SPAN)
        for ref, half, k in ((from_l, high, 2), (from_r, low, 3), (from_l, low, 4), (from_r, high, 5)):
            view = ref.at[half]
            pltpu.make_async_copy(view, view, rs_rsem.at[p, k]).wait()
        at = slice(LINES * p, LINES * p + LINES)
        total_out = part2[3, at, :].astype(F32) + from_l2[at, :].astype(F32) + from_r2[at, :].astype(F32)
        fin2[at, :] = total_out.astype(BF)
        exchange(fin, ret, ret_ssem, ret_rsem, range(SPAN * p, SPAN * p + SPAN), True)

    for p in range(PARTS):
        for i in range(SPAN * p, SPAN * p + SPAN):
            gathered(i)
        if p == 0:
            loads[2].wait()
            loads[3].wait()
        hidden_units(p)
        if p == 0:
            forward(7)
            loads[4].wait()
        if p > 0:
            hop(p - 1)
        if p > 1:
            give_back(p - 2)
        outputs(p)
    give_back(PARTS - 2)
    hop(PARTS - 1)
    give_back(PARTS - 1)
    for dz in Z_ORDER:
        arrived(ret, ret_rsem, dz)
    ret2 = ret.reshape(512, WIDE)
    back = ret2[:, 0:Q]
    lines = ret2[:, Q:WIDE]
    masked = jnp.concatenate([jnp.where(piece == k, lines.astype(F32), 0.0).astype(BF) for k in range(4)], axis=1)
    mixture = dot(g_main[0], back) + dot(g_main[1], back) + dot(g_rem[0], masked) + dot(g_rem[1], masked)
    out_ref[...] = (hid[...] + mixture).astype(BF)

    for copy in mate_copies + wo_copies + proj_copies + stat_copies + ag_copies + rs:
        copy.wait_send()
    few = wo.at[0, pl.ds(0, 7)]
    pltpu.make_async_copy(few, few, wo_ssem.at[0]).wait()
    pltpu.make_async_copy(wo.at[c], wo.at[c], pair_ssem).wait()
    for sem, ref in ((a2a_ssem, disp), (ret_ssem, fin)):
        view = ref.at[pl.ds(0, NREQ - 1)]
        pltpu.make_async_copy(view, view, sem).wait()
    for s in range(1, 9):
        for k in range(2):
            view = kv.at[s, k]
            pltpu.make_async_copy(view, view, kv_ssem.at[s, k]).wait()


def layer_call(*args):
    vmem = pl.BlockSpec(memory_space=pltpu.VMEM)
    smem = pl.BlockSpec(memory_space=pltpu.SMEM)
    hbm = pl.BlockSpec(memory_space=pl.ANY)
    dma = pltpu.SemaphoreType.DMA
    chunk = (NREQ, 8, WIDE)
    return pl.pallas_call(
        layer_kernel,
        out_shape=jax.ShapeDtypeStruct((TOK, Q), BF),
        in_specs=[hbm, hbm, hbm, hbm, smem, hbm, hbm, hbm, vmem, vmem, vmem, hbm, hbm, hbm],
        out_specs=vmem,
        scratch_shapes=[
            pltpu.VMEM((9, 2, 2, 512, HEAD_SIZE), BF), pltpu.VMEM((2, 2, 512, HEAD_SIZE), BF),
            pltpu.VMEM((2, HEAD_SIZE, 1024), BF), pltpu.VMEM((2, 1, TOK), jnp.int32),
            pltpu.VMEM((2, 1, 1024), F32), pltpu.VMEM((2, 1, 1024), F32), pltpu.VMEM((2, HEAD_SIZE, 1024), F32),
            pltpu.VMEM((2, TOK, 512), BF), pltpu.VMEM((TOK, 512), BF),
            pltpu.VMEM((2, NREQ, 32, 512), BF), pltpu.VMEM((TOK, Q), BF), pltpu.VMEM((1, Q), F32),
            pltpu.VMEM((D, HID), BF), pltpu.VMEM((D, HID), BF), pltpu.VMEM((D, HID), BF),
            pltpu.VMEM((3, TOK, Q), BF), pltpu.VMEM((3, TOK, Q), BF), pltpu.VMEM((TOK, Q), F32),
            pltpu.VMEM((8, TOK), F32), pltpu.VMEM((3, 8, TOK), F32),
            pltpu.VMEM((512, TOK), BF), pltpu.VMEM((512, TOK), BF),
            pltpu.VMEM((2, TOK, 512), BF), pltpu.VMEM((2, TOK, 512), BF),
            pltpu.VMEM(chunk, BF), pltpu.VMEM((4,) + chunk, BF), pltpu.VMEM((LINES + TAIL, D), BF), pltpu.VMEM((LINES + TAIL, HID), BF),
            pltpu.VMEM((4,) + chunk, BF), pltpu.VMEM((PARTS, 4 * SPAN, 8, WIDE), BF), pltpu.VMEM((PARTS, 4 * SPAN, 8, WIDE), BF),
            pltpu.VMEM(chunk, BF), pltpu.VMEM(chunk, BF), pltpu.VMEM(chunk, BF), pltpu.VMEM(chunk, BF),
            dma((9, 2)), dma((9, 2)), dma((9,)), dma((4,)), dma((5,)), dma((1,)), dma((1,)), dma((7, 2)), dma((7, 2)),
            dma, dma, dma, dma,
            dma((5,)), dma((3,)), dma((3,)), dma((3,)), dma((3,)),
            dma, dma((8,)), dma((3, 8)), dma((3, 8)), dma((PARTS, 6)), dma((PARTS, 6)), dma, dma((8,)), dma,
        ],
        compiler_params=pltpu.CompilerParams(
            collective_id=1, has_side_effects=True, vmem_limit_bytes=60 << 20
        ),
        name="layer",
    )(*args)


def per_device(
    residual, queries, rotated_key_rows, values, req_start, head_sink_logit, out_proj, mid_gain,
    router_logits, routes, placement, w_gate, w_up, w_down,
):
    return layer_call(
        queries, rotated_key_rows, values, req_start.reshape(1, TOK), head_sink_logit, out_proj.T, residual,
        mid_gain.reshape(1, D), router_logits.T, routes.T, placement.reshape(1, NREQ), w_gate[0], w_up[0], w_down[0],
    )


def solution(mesh):
    in_specs = (
        P("req", None),
        P("req", "ffn"),
        P("req", "ffn"),
        P("req", "ffn"),
        P("req"),
        P("ffn"),
        P("ffn", "req"),
        P(),
        P("req", None),
        P("req", None),
        P(),
        P("req", None, "ffn"),
        P("req", None, "ffn"),
        P("req", None, "ffn"),
    )
    out_specs = P("req", "ffn")
    return jax.shard_map(
        per_device, mesh=mesh, in_specs=in_specs, out_specs=out_specs, check_vma=False
    )
```
